32 devices in a mesh: wshard: 8 (over z, y), seq: 4 (over x, core).
Axes of the slice: x: 2, y: 2, z: 4, core: 2. Of those that a mesh axis runs over, the one named last changes fastest.
Arguments:
- tokens: bfloat16 [24576, 768], P(('wshard', 'seq')), may hold values from -6 to 6
- cotangent: bfloat16 [24576, 768], P(('wshard', 'seq')), may hold values from -6 to 6
- starts: int32 [8, 8], P('wshard'), may hold values from 0 to 2688, as said below
- w_query: bfloat16 [768, 768], P('wshard'), may hold values from -0.21875 to 0.21875
- w_key: bfloat16 [768, 768], P('wshard'), may hold values from -0.21875 to 0.21875
- w_value: bfloat16 [768, 768], P('wshard'), may hold values from -0.21875 to 0.21875
- w_output: bfloat16 [768, 768], P('wshard'), may hold values from -1.25 to 1.25
- w_inner: bfloat16 [768, 3072], P('wshard'), may hold values from -0.21875 to 0.21875
- w_outer: bfloat16 [3072, 768], P('wshard'), may hold values from -0.109375 to 0.109375
- b_query: bfloat16 [768], P('wshard'), may hold values from -3 to 3
- b_value: bfloat16 [768], P('wshard'), may hold values from -3 to 3
- b_output: bfloat16 [768], P('wshard'), may hold values from -3 to 3
- b_inner: bfloat16 [3072], P('wshard'), may hold values from -3 to 3
- b_outer: bfloat16 [768], P('wshard'), may hold values from -3 to 3
- gain_first: bfloat16 [768], P('wshard'), may hold values from 0.5 to 2
- bias_first: bfloat16 [768], P('wshard'), may hold values from -3 to 3
- gain_second: bfloat16 [768], P('wshard'), may hold values from 0.5 to 2
- bias_second: bfloat16 [768], P('wshard'), may hold values from -3 to 3
Outputs:
- layer_out: bfloat16 [24576, 768], P(('wshard', 'seq'))
- grad_tokens: float32 [24576, 768], P(('wshard', 'seq'))
- grad_w_query: float32 [768, 768], P('wshard')
- grad_w_key: float32 [768, 768], P('wshard')
- grad_w_value: float32 [768, 768], P('wshard')
- grad_w_output: float32 [768, 768], P('wshard')
- grad_w_inner: float32 [768, 3072], P('wshard')
- grad_w_outer: float32 [3072, 768], P('wshard')
- grad_b_query: float32 [768], P('wshard')
- grad_b_value: float32 [768], P('wshard')
- grad_b_output: float32 [768], P('wshard')
- grad_b_inner: float32 [3072], P('wshard')
- grad_b_outer: float32 [768], P('wshard')
- grad_gain_first: float32 [768], P('wshard')
- grad_bias_first: float32 [768], P('wshard')
- grad_gain_second: float32 [768], P('wshard')
- grad_bias_second: float32 [768], P('wshard')
The draws below stay inside these ranges and needn't reach their ends.
Inputs may be any that keep to these rules, and one draw needn't show every extreme that they name: `starts`: row w lists where the 8 documents of stream w begin: the first is 0 and they strictly increase; the last document of every stream holds exactly 384 positions; documents run across the devices of a stream.
All inputs are finite; a program needn't handle non-finite values.
Results may differ from the reference program's by a relative error of at most 0.017.
Values may be sent and summed in bfloat16 or wider, within the bound.
A program may use at most 192 MiB of HBM per device.

```python
import math
import jax
import jax.numpy as jnp
from jax import lax

D = 768
H = 12
HD = 64
FF = 3072
TOK_DEV = 768
NDOC = 8
STREAM = 3072
STREAMS = 8
TOKENS = 24576


def draw_starts(key, part):
    key_weights = jax.random.fold_in(key, 11)
    key_heavy = jax.random.fold_in(key, 23)
    front_docs = NDOC - 1
    tail_rows = TOK_DEV // 2
    doc_weights = jax.random.randint(key_weights, (STREAMS, front_docs), 1, 17)
    heavy_doc = jax.random.randint(key_heavy, (STREAMS, 1), 0, front_docs)
    column = jnp.arange(front_docs, dtype=jnp.int32)[None, :]
    doc_weights = jnp.where(column == heavy_doc, 48, doc_weights)
    front_rows = STREAM - tail_rows
    spare_rows = front_rows - front_docs
    weight_sum = jnp.sum(doc_weights, axis=1, keepdims=True)
    doc_lengths = 1 + doc_weights * spare_rows // weight_sum
    excess_rows = front_rows - jnp.sum(doc_lengths, axis=1, keepdims=True)
    doc_lengths = doc_lengths + jnp.where(column == front_docs - 1, excess_rows, 0)
    front_starts = jnp.cumsum(doc_lengths, axis=1) - doc_lengths
    last_start = jnp.full((STREAMS, 1), front_rows, jnp.int32)
    return jnp.concatenate([front_starts.astype(jnp.int32), last_start], axis=1).astype(jnp.int32)


def level_of(rng, extent, shards, low, largest):
    gain, own = 1.0, jax.random.fold_in(rng, 6)
    for position, shards_of in shards:
        heights = jnp.exp(jax.random.uniform(jax.random.fold_in(own, position), (shards_of,), jnp.float32, low / len(shards), largest / len(shards)))
        gain = gain * jnp.repeat(heights, extent[position] // shards_of).reshape([-1 if axis == position else 1 for axis in range(len(extent))])
    return gain


def normal_values(own_key, shape, width, most, pieces=(), kind=jnp.bfloat16):
    level = level_of(own_key, shape, pieces, -0.22, 0.18) if pieces else 1.0
    entries = jax.random.normal(own_key, shape, jnp.float32) * width * level
    return jnp.minimum(jnp.maximum(entries, -most), most).astype(kind)


def setup_inputs(seed: int = 0) -> dict:
    key_list = jax.random.split(jax.random.key(seed), 19)
    tokens = normal_values(key_list[0], (TOKENS, D), 1.0, 6.0, ((0, 32),))
    cotangent = normal_values(key_list[1], (TOKENS, D), 1.0, 6.0, ((0, 32),))
    starts = draw_starts(jax.random.fold_in(key_list[18], 71), 0)
    w_query = normal_values(key_list[3], (D, D), D ** -0.5, 0.21875, ((0, 8),))
    w_key = normal_values(key_list[4], (D, D), D ** -0.5, 0.21875, ((0, 8),))
    w_value = normal_values(key_list[5], (D, D), D ** -0.5, 0.21875, ((0, 8),))
    w_output = normal_values(key_list[6], (D, D), (D // 32) ** -0.5, 1.25, ((0, 8),))
    w_inner = normal_values(key_list[7], (D, FF), D ** -0.5, 0.21875, ((0, 8),))
    w_outer = normal_values(key_list[8], (FF, D), FF ** -0.5, 0.109375, ((0, 8),))
    b_query = normal_values(key_list[9], (D,), 0.5, 3.0, ((0, 8),))
    b_value = normal_values(key_list[10], (D,), 0.5, 3.0, ((0, 8),))
    b_output = normal_values(key_list[11], (D,), 0.5, 3.0, ((0, 8),))
    b_inner = normal_values(key_list[12], (FF,), 0.5, 3.0, ((0, 8),))
    b_outer = normal_values(key_list[13], (D,), 0.5, 3.0, ((0, 8),))
    gain_first = jnp.clip(jnp.exp(math.log(2.0) - 1.3862944 * jax.random.uniform(key_list[14], (D,), jnp.float32) ** level_of(key_list[14], (D,), ((0, 8),), -0.2, 0.2)), 0.5, 2.0).astype(jnp.bfloat16)
    bias_first = normal_values(key_list[15], (D,), 0.5, 3.0, ((0, 8),))
    gain_second = jnp.clip(jnp.exp(math.log(2.0) - 1.3862944 * jax.random.uniform(key_list[16], (D,), jnp.float32) ** level_of(key_list[16], (D,), ((0, 8),), -0.2, 0.2)), 0.5, 2.0).astype(jnp.bfloat16)
    bias_second = normal_values(key_list[17], (D,), 0.5, 3.0, ((0, 8),))
    return {"tokens": tokens, "cotangent": cotangent, "starts": starts, "w_query": w_query, "w_key": w_key, "w_value": w_value, "w_output": w_output, "w_inner": w_inner, "w_outer": w_outer, "b_query": b_query, "b_value": b_value, "b_output": b_output, "b_inner": b_inner, "b_outer": b_outer, "gain_first": gain_first, "bias_first": bias_first, "gain_second": gain_second, "bias_second": bias_second}


@jax.custom_vjp
def low(v):
    return lax.optimization_barrier(v.astype(jnp.bfloat16)).astype(jnp.float32)

@jax.custom_vjp
def low_back(v):
    return v

def low_keep(v):
    return (low(v), None)

def low_pass(kept, grad):
    return (grad,)

def back_keep(v):
    return (v, None)

def back_low(kept, grad):
    return (low(grad),)
low.defvjp(low_keep, low_pass)
low_back.defvjp(back_keep, back_low)
HIGHEST = lax.Precision.HIGHEST
NORM_EPS = 1e-05

def layer_norm(inputs, norm_gain, norm_bias):
    row_mean = lax.optimization_barrier(jnp.mean(inputs, axis=-1, keepdims=True))
    centred = inputs - row_mean
    row_var = lax.optimization_barrier(jnp.mean(centred * centred, axis=-1, keepdims=True))
    return centred * lax.rsqrt(row_var + NORM_EPS) * norm_gain + norm_bias

def matmul(left_in, right_in):
    return jnp.dot(left_in, right_in, precision=HIGHEST, preferred_element_type=jnp.float32)

def stream_forward(weights_all, layer_in, segment):
    query_mat, key_mat, value_mat, output_mat, inner_mat, outer_mat, query_bias, value_bias, output_bias, inner_bias, outer_bias, gain_one, shift_one, gain_two, shift_two = weights_all
    length = layer_in.shape[0]
    queries = low_back(low(matmul(layer_in, query_mat) + query_bias)).reshape(length, H, HD)
    keys_all = low_back(low(matmul(layer_in, key_mat))).reshape(length, H, HD)
    vals_all = low_back(low(matmul(layer_in, value_mat) + value_bias)).reshape(length, H, HD)
    score_scale = HD ** (-0.5)
    block_rows = min(512, length)
    block_count = length // block_rows
    query_blocks = queries.reshape(block_count, block_rows, H, HD)
    segment_blocks = segment.reshape(block_count, block_rows)

    def attend(block_inputs):
        query_block, segment_block = block_inputs
        scores = jnp.einsum('qhd,khd->hqk', query_block, keys_all, precision=HIGHEST) * score_scale
        scores = low_back(scores)
        allowed = segment_block[:, None] == segment[None, :]
        scores = jnp.where(allowed[None], scores, -1e+30)
        attn_probs = jax.nn.softmax(scores, axis=-1)
        return jnp.einsum('hqk,khd->qhd', low(attn_probs), vals_all, precision=HIGHEST)
    mixed_heads = lax.map(jax.checkpoint(attend), (query_blocks, segment_blocks))
    mixed_heads = low_back(low(mixed_heads.reshape(length, H * HD)))
    attn_out = low_back(matmul(mixed_heads, output_mat) + output_bias)
    first_norm = layer_norm(layer_in + attn_out, gain_one, shift_one)
    inner_act = low_back(matmul(low(first_norm), inner_mat) + inner_bias)
    outer_act = low_back(matmul(low(jax.nn.gelu(inner_act, approximate=False)), outer_mat) + outer_bias)
    return layer_norm(first_norm + outer_act, gain_two, shift_two)

def reference(tokens, cotangent, starts, w_query, w_key, w_value, w_output, w_inner, w_outer, b_query, b_value, b_output, b_inner, b_outer, gain_first, bias_first, gain_second, bias_second):
    params = tuple((member.astype(jnp.float32) for member in (w_query, w_key, w_value, w_output, w_inner, w_outer, b_query, b_value, b_output, b_inner, b_outer, gain_first, bias_first, gain_second, bias_second)))
    stream_x = tokens.astype(jnp.float32).reshape(STREAMS, STREAM, D)
    stream_cot = cotangent.astype(jnp.float32).reshape(STREAMS, STREAM, D)
    positions = jnp.arange(STREAM, dtype=jnp.int32)

    def one_stream(totals, inputs):
        stream_in, stream_grad, doc_starts = inputs
        segment = lax.optimization_barrier(jnp.sum((doc_starts[None, :] <= positions[:, None]).astype(jnp.int32), axis=1))

        def forward(weights_all, layer_in):
            return stream_forward(weights_all, layer_in, segment)
        layer_result, pullback = jax.vjp(forward, params, stream_in)
        grad_parts, grad_input = pullback(stream_grad)
        totals = tuple((total_acc + grad_part for total_acc, grad_part in zip(totals, grad_parts)))
        return (totals, (layer_result.astype(jnp.bfloat16), grad_input))
    zeros_all = tuple((jnp.zeros(member.shape, jnp.float32) for member in params))
    totals, (layer_all, grad_all) = lax.scan(one_stream, zeros_all, (stream_x, stream_cot, starts))
    return (layer_all.reshape(TOKENS, D), grad_all.reshape(TOKENS, D), totals[0], totals[1], totals[2], totals[3], totals[4], totals[5], totals[6], totals[7], totals[8], totals[9], totals[10], totals[11], totals[12], totals[13], totals[14])
```

```python
import functools

import jax
import jax.numpy as jnp
from jax import lax
from jax.experimental import pallas as pl
from jax.experimental.pallas import tpu as pltpu
from jax.sharding import PartitionSpec as P

NORM_EPS = 1e-05

HD = 64
bf = jnp.bfloat16
f32 = jnp.float32

def doc_bounds(starts_ref, pos, total):
    lo = jnp.zeros_like(pos); hi = jnp.full_like(pos, total)
    for d in range(starts_ref.shape[1]):
        s = starts_ref[0, d]
        lo = jnp.where(s <= pos, jnp.maximum(lo, s), lo)
        hi = jnp.where(s > pos, jnp.minimum(hi, s), hi)
    return lo, hi

def dot(a, b):
    return lax.dot_general(a, b, (((1,), (0,)), ((), ())), preferred_element_type=f32)

def fwd_kernel(heads, bq, bk, starts, qT, k3, vT, oT, mixT, lse, acc, ml):
    total = k3.shape[1]
    i = pl.program_id(0)
    q0 = i * bq
    first, _ = doc_bounds(starts, jnp.int32(q0), total)
    _, last = doc_bounds(starts, jnp.int32(q0 + bq - 1), total)
    pos = q0 + lax.broadcasted_iota(jnp.int32, (1, bq), 1)
    lo, hi = doc_bounds(starts, pos, total)
    kb0 = first // bk
    kb1 = (last + bk - 1) // bk
    acc[...] = jnp.zeros_like(acc)
    ml[0] = jnp.full((heads, bq), -1e30, f32)
    ml[1] = jnp.zeros((heads, bq), f32)
    kio = lax.broadcasted_iota(jnp.int32, (bk, bq), 0)
    def body(j, _):
        ks = pl.multiple_of(j * bk, bk)
        mask = (kio >= lo - ks) & (kio < hi - ks)
        for h in range(heads):
            s = dot(k3[h, pl.ds(ks, bk), :], qT[HD * h:HD * (h + 1), :])
            s = jnp.where(mask, s, -1e30)
            m_old = ml[0, h:h + 1]
            m = jnp.maximum(m_old, jnp.max(s, axis=0, keepdims=True))
            p = jnp.exp(s - m)
            al = jnp.exp(m_old - m)
            ml[0, h:h + 1] = m
            ml[1, h:h + 1] = ml[1, h:h + 1] * al + jnp.sum(p, axis=0, keepdims=True)
            sl = slice(HD * h, HD * (h + 1))
            acc[sl, :] = acc[sl, :] * al + dot(vT[sl, pl.ds(ks, bk)], p.astype(bf))
        return 0
    lax.fori_loop(kb0, kb1, body, 0)
    for h in range(heads):
        sl = slice(HD * h, HD * (h + 1))
        l = ml[1, h:h + 1]
        o = acc[sl, :] / l
        oT[sl, :] = o
        mixT[sl, :] = o.astype(bf)
        lse[h:h + 1, :] = ml[0, h:h + 1] + jnp.log(l)

def attn_fwd(starts, qT, k3, vT, bq=256, bk=256):
    heads, total, _ = k3.shape
    full2 = lambda i: (0, 0)
    return pl.pallas_call(
        functools.partial(fwd_kernel, heads, bq, bk),
        grid=(total // bq,),
        in_specs=[pl.BlockSpec(memory_space=pltpu.SMEM),
                  pl.BlockSpec((heads * HD, bq), lambda i: (0, i)),
                  pl.BlockSpec(k3.shape, lambda i: (0, 0, 0)),
                  pl.BlockSpec(vT.shape, full2)],
        out_specs=[pl.BlockSpec((heads * HD, bq), lambda i: (0, i)),
                   pl.BlockSpec((heads * HD, bq), lambda i: (0, i)),
                   pl.BlockSpec((heads, bq), lambda i: (0, i))],
        out_shape=[jax.ShapeDtypeStruct((heads * HD, total), f32),
                   jax.ShapeDtypeStruct((heads * HD, total), bf),
                   jax.ShapeDtypeStruct((heads, total), f32)],
        scratch_shapes=[pltpu.VMEM((heads * HD, bq), f32), pltpu.VMEM((2, heads, bq), f32)],
        name="attn_fwd",
    )(starts, qT, k3, vT)

def bwd_kernel(heads, bq, bk, starts, qT, q3, k3, kT, v3, doT, do3, oT, lse, dqT, dk3, dv3, delta, dqa, dka, dva):
    total = q3.shape[1]
    i = pl.program_id(0)
    k0 = i * bk
    @pl.when(i == 0)
    def _():
        dqa[...] = jnp.zeros_like(dqa)
        for h in range(heads):
            sl = slice(HD * h, HD * (h + 1))
            delta[h:h + 1, :] = jnp.sum(doT[sl, :].astype(f32) * oT[sl, :], axis=0, keepdims=True)
    first, _ = doc_bounds(starts, jnp.int32(k0), total)
    _, last = doc_bounds(starts, jnp.int32(k0 + bk - 1), total)
    qb0 = first // bq
    qb1 = (last + bq - 1) // bq
    dka[...] = jnp.zeros_like(dka)
    dva[...] = jnp.zeros_like(dva)
    kio = k0 + lax.broadcasted_iota(jnp.int32, (bk, bq), 0)
    def body(j, _):
        qs = pl.multiple_of(j * bq, bq)
        pos = qs + lax.broadcasted_iota(jnp.int32, (1, bq), 1)
        lo, hi = doc_bounds(starts, pos, total)
        mask = (kio >= lo) & (kio < hi)
        for h in range(heads):
            sl = slice(HD * h, HD * (h + 1))
            s = dot(k3[h, :, :], qT[sl, pl.ds(qs, bq)])
            p = jnp.exp(jnp.where(mask, s - lse[h:h + 1, pl.ds(qs, bq)], -1e30))
            dp = dot(v3[h, :, :], doT[sl, pl.ds(qs, bq)])
            ds = p * (dp - delta[h:h + 1, pl.ds(qs, bq)])
            dsb = ds.astype(bf)
            dva[h] += dot(p.astype(bf), do3[h, pl.ds(qs, bq), :])
            dka[h] += dot(dsb, q3[h, pl.ds(qs, bq), :])
            dqa[sl, pl.ds(qs, bq)] += dot(kT[sl, :], dsb)
        return 0
    lax.fori_loop(qb0, qb1, body, 0)
    dk3[...] = dka[...].astype(bf)
    dv3[...] = dva[...].astype(bf)
    @pl.when(i == pl.num_programs(0) - 1)
    def _():
        dqT[...] = (dqa[...] * (HD ** -0.5)).astype(bf)

def attn_bwd(starts, qT, q3, k3, kT, v3, doT, do3, oT, lse, bq=256, bk=256):
    heads, total, _ = k3.shape
    full = lambda a: pl.BlockSpec(a.shape, lambda i: (0,) * a.ndim)
    kb3 = pl.BlockSpec((heads, bk, HD), lambda i: (0, i, 0))
    return pl.pallas_call(
        functools.partial(bwd_kernel, heads, bq, bk),
        grid=(total // bk,),
        in_specs=[pl.BlockSpec(memory_space=pltpu.SMEM), full(qT), full(q3), kb3,
                  pl.BlockSpec((heads * HD, bk), lambda i: (0, i)), kb3, full(doT), full(do3), full(oT), full(lse)],
        out_specs=[full(qT), kb3, kb3],
        out_shape=[jax.ShapeDtypeStruct(qT.shape, bf), jax.ShapeDtypeStruct(k3.shape, bf), jax.ShapeDtypeStruct(k3.shape, bf)],
        scratch_shapes=[pltpu.VMEM((heads, total), f32), pltpu.VMEM(qT.shape, f32),
                        pltpu.VMEM((heads, bk, HD), f32), pltpu.VMEM((heads, bk, HD), f32)],
        name="attn_bwd",
    )(starts, qT, q3, k3, kT, v3, doT, do3, oT, lse)


def layer_norm(inputs, norm_gain, norm_bias):
    row_mean = jnp.mean(inputs, axis=-1, keepdims=True)
    centred = inputs - row_mean
    row_var = jnp.mean(centred * centred, axis=-1, keepdims=True)
    return centred * lax.rsqrt(row_var + NORM_EPS) * norm_gain + norm_bias


def gelu_exact(inputs):
    return jax.nn.gelu(inputs, approximate=False)


def contract(left_in, right_in, left_dim, right_dim):
    return lax.dot_general(
        left_in,
        right_in,
        (((left_dim,), (right_dim,)), ((), ())),
        preferred_element_type=jnp.float32,
    )


def shards(
    tokens, cotangent, starts,
    w_query, w_key, w_value, w_output, w_inner, w_outer,
    b_query, b_value, b_output, b_inner, b_outer,
    gain_first, bias_first, gain_second, bias_second,
):
    model = tokens.shape[1]
    seq_n = lax.axis_size("seq")
    seq_i = lax.axis_index("seq")
    shard_i = lax.axis_index("wshard")
    width = model // seq_n
    heads = width // HD

    def own(columns):
        return lax.dynamic_slice_in_dim(columns, seq_i * width, width, columns.ndim - 1)

    def gather(shard):
        return lax.all_gather(shard, "wshard", axis=0, tiled=True)

    smalls = (b_query, b_value, b_output, b_inner, b_outer, gain_first, bias_first, gain_second, bias_second)
    sizes = [member.shape[0] for member in smalls]
    packed = lax.all_gather(jnp.concatenate(smalls), "wshard", axis=0, tiled=False).astype(f32)
    full, at = [], 0
    for size in sizes:
        full.append(packed[:, at:at + size].reshape(-1))
        at += size
    bias_query, bias_value, bias_output, bias_inner, bias_outer, gain_one, shift_one, gain_two, shift_two = full

    stream = lax.all_gather(tokens, "seq", axis=0, tiled=True)
    w_own = gather(jnp.concatenate([own(w_query), own(w_key), own(w_value)], axis=1))
    output_full, inner_full, outer_full = gather(w_output), gather(w_inner), gather(w_outer)
    scale = HD ** -0.5
    qT = ((contract(w_own[:, :width], stream, 0, 1) + own(bias_query)[:, None]).astype(bf) * bf(scale))
    kT = contract(w_own[:, width:2 * width], stream, 0, 1).astype(bf)
    vT = (contract(w_own[:, 2 * width:], stream, 0, 1) + own(bias_value)[:, None]).astype(bf)

    def by_token(arr):
        return arr.reshape(heads, HD, -1).transpose(0, 2, 1)

    def by_feature(arr):
        return arr.transpose(0, 2, 1).reshape(width, -1)

    q3, k3, v3 = by_token(qT), by_token(kT), by_token(vT)
    oT, mixT, lse = attn_fwd(starts, qT, k3, vT, 512, 512)
    mixed = lax.all_to_all(mixT, "seq", split_axis=1, concat_axis=0, tiled=True)

    residual_in = tokens.astype(f32) + contract(mixed, output_full, 0, 0) + bias_output
    first_norm, first_back = jax.vjp(layer_norm, residual_in, gain_one, shift_one)
    first_low = first_norm.astype(bf)
    inner_act = jnp.dot(first_low, inner_full, preferred_element_type=f32) + bias_inner
    gelu_out, gelu_back = jax.vjp(gelu_exact, inner_act)
    gelu_low = gelu_out.astype(bf)
    second_in = first_norm + jnp.dot(gelu_low, outer_full, preferred_element_type=f32) + bias_outer
    layer_result, second_back = jax.vjp(layer_norm, second_in, gain_two, shift_two)
    d_second, grad_gain_two, grad_bias_two = second_back(cotangent.astype(f32))
    d_outer = d_second.astype(bf)
    grad_bias_outer = jnp.sum(d_outer.astype(f32), axis=0)
    grad_outer = contract(gelu_low, d_outer, 0, 0)
    (d_inner,) = gelu_back(contract(d_outer, outer_full, 1, 1))
    d_inner_low = d_inner.astype(bf)
    grad_bias_inner = jnp.sum(d_inner_low.astype(f32), axis=0)
    grad_inner = contract(first_low, d_inner_low, 0, 0)
    d_first = contract(d_inner_low, inner_full, 1, 1) + d_second
    d_resid, grad_gain_one, grad_bias_one = first_back(d_first)
    d_attn = d_resid.astype(bf)
    grad_bias_output = jnp.sum(d_attn.astype(f32), axis=0)
    grad_output = contract(mixed, d_attn, 1, 0)
    d_mixed = contract(output_full, d_attn, 1, 1).astype(bf)
    doT = lax.all_to_all(d_mixed, "seq", split_axis=0, concat_axis=1, tiled=True)

    dqT, dk3, dv3 = attn_bwd(starts, qT, q3, k3, kT, v3, doT, by_token(doT), oT, lse, 256, 512)
    dT = jnp.concatenate([dqT, by_feature(dk3), by_feature(dv3)], axis=0)
    grad_own = contract(stream, dT, 0, 1).astype(bf)
    d_part = contract(dT, w_own, 0, 1).astype(bf)
    d_tokens = lax.psum_scatter(d_part, "seq", scatter_dimension=0, tiled=True).astype(f32) + d_resid

    def spread(own_sum):
        return lax.dynamic_update_slice(jnp.zeros((model,), f32), own_sum, (seq_i * width,))

    grad_small = (
        spread(jnp.sum(dqT.astype(f32), axis=1)),
        spread(jnp.sum(dv3.astype(f32), axis=1).reshape(-1)),
        grad_bias_output, grad_bias_inner, grad_bias_outer,
        grad_gain_one, grad_bias_one, grad_gain_two, grad_bias_two,
    )
    shards_n = lax.axis_size("wshard")
    small_sum = lax.psum(
        jnp.concatenate([member.reshape(shards_n, -1) for member in grad_small], axis=1), ("wshard", "seq")
    )
    small_own = lax.dynamic_index_in_dim(small_sum, shard_i, 0, keepdims=False)
    outs, at = [], 0
    for size in sizes:
        outs.append(small_own[at:at + size])
        at += size

    def scatter(grad):
        low = lax.psum_scatter(grad.astype(bf), "wshard", scatter_dimension=0, tiled=True)
        return lax.psum(low, "seq").astype(f32)

    own_shard = lax.psum_scatter(grad_own, "wshard", scatter_dimension=0, tiled=True)
    parts = lax.all_gather(own_shard, "seq", axis=0, tiled=False).astype(f32)
    qkv_grads = [
        parts[:, :, i * width:(i + 1) * width].transpose(1, 0, 2).reshape(-1, model) for i in range(3)
    ]
    return (
        layer_result.astype(bf), d_tokens, *qkv_grads,
        scatter(grad_output), scatter(grad_inner), scatter(grad_outer), *outs,
    )


def solution(mesh):
    placed = (
        P(("wshard", "seq"), None),
        P(("wshard", "seq"), None),
        P("wshard", None),
        P("wshard", None),
        P("wshard", None),
        P("wshard", None),
        P("wshard", None),
        P("wshard", None),
        P("wshard", None),
        P("wshard"),
        P("wshard"),
        P("wshard"),
        P("wshard"),
        P("wshard"),
        P("wshard"),
        P("wshard"),
        P("wshard"),
        P("wshard"),
    )
    return jax.shard_map(
        shards,
        mesh=mesh,
        in_specs=placed,
        out_specs=(
            P(("wshard", "seq"), None),
            P(("wshard", "seq"), None),
            P("wshard", None),
            P("wshard", None),
            P("wshard", None),
            P("wshard", None),
            P("wshard", None),
            P("wshard", None),
            P("wshard"),
            P("wshard"),
            P("wshard"),
            P("wshard"),
            P("wshard"),
            P("wshard"),
            P("wshard"),
            P("wshard"),
            P("wshard"),
        ),
        check_vma=False,
    )
```

```python
import functools

import jax
import jax.numpy as jnp
from jax import lax
from jax.experimental import pallas as pl
from jax.experimental.pallas import tpu as pltpu
from jax.sharding import PartitionSpec as P

NORM_EPS = 1e-05
HD = 64
bf = jnp.bfloat16
f32 = jnp.float32


def doc_bounds(starts_ref, pos, total):
    lo = jnp.zeros_like(pos); hi = jnp.full_like(pos, total)
    for d in range(starts_ref.shape[1]):
        s = starts_ref[0, d]
        lo = jnp.where(s <= pos, jnp.maximum(lo, s), lo)
        hi = jnp.where(s > pos, jnp.minimum(hi, s), hi)
    return lo, hi

def dot(a, b):
    return lax.dot_general(a, b, (((1,), (0,)), ((), ())), preferred_element_type=f32)

def fwd_kernel(heads, bq, bk, starts, qT, k3, vT, oT, mixT, lse, acc, ml):
    total = k3.shape[1]
    i = pl.program_id(0)
    q0 = i * bq
    first, _ = doc_bounds(starts, jnp.int32(q0), total)
    _, last = doc_bounds(starts, jnp.int32(q0 + bq - 1), total)
    pos = q0 + lax.broadcasted_iota(jnp.int32, (1, bq), 1)
    lo, hi = doc_bounds(starts, pos, total)
    kb0 = first // bk
    kb1 = (last + bk - 1) // bk
    acc[...] = jnp.zeros_like(acc)
    ml[0] = jnp.full((heads, bq), -1e30, f32)
    ml[1] = jnp.zeros((heads, bq), f32)
    kio = lax.broadcasted_iota(jnp.int32, (bk, bq), 0)
    def body(j, _):
        ks = pl.multiple_of(j * bk, bk)
        mask = (kio >= lo - ks) & (kio < hi - ks)
        for h in range(heads):
            s = dot(k3[h, pl.ds(ks, bk), :], qT[HD * h:HD * (h + 1), :])
            s = jnp.where(mask, s, -1e30)
            m_old = ml[0, h:h + 1]
            m = jnp.maximum(m_old, jnp.max(s, axis=0, keepdims=True))
            p = jnp.exp(s - m)
            al = jnp.exp(m_old - m)
            ml[0, h:h + 1] = m
            ml[1, h:h + 1] = ml[1, h:h + 1] * al + jnp.sum(p, axis=0, keepdims=True)
            sl = slice(HD * h, HD * (h + 1))
            acc[sl, :] = acc[sl, :] * al + dot(vT[sl, pl.ds(ks, bk)], p.astype(bf))
        return 0
    lax.fori_loop(kb0, kb1, body, 0)
    for h in range(heads):
        sl = slice(HD * h, HD * (h + 1))
        l = ml[1, h:h + 1]
        o = acc[sl, :] / l
        oT[sl, :] = o
        mixT[sl, :] = o.astype(bf)
        lse[h:h + 1, :] = ml[0, h:h + 1] + jnp.log(l)

def attn_fwd(starts, qT, k3, vT, bq=256, bk=256):
    heads, total, _ = k3.shape
    full2 = lambda i: (0, 0)
    return pl.pallas_call(
        functools.partial(fwd_kernel, heads, bq, bk),
        grid=(total // bq,),
        in_specs=[pl.BlockSpec(memory_space=pltpu.SMEM),
                  pl.BlockSpec((heads * HD, bq), lambda i: (0, i)),
                  pl.BlockSpec(k3.shape, lambda i: (0, 0, 0)),
                  pl.BlockSpec(vT.shape, full2)],
        out_specs=[pl.BlockSpec((heads * HD, bq), lambda i: (0, i)),
                   pl.BlockSpec((heads * HD, bq), lambda i: (0, i)),
                   pl.BlockSpec((heads, bq), lambda i: (0, i))],
        out_shape=[jax.ShapeDtypeStruct((heads * HD, total), f32),
                   jax.ShapeDtypeStruct((heads * HD, total), bf),
                   jax.ShapeDtypeStruct((heads, total), f32)],
        scratch_shapes=[pltpu.VMEM((heads * HD, bq), f32), pltpu.VMEM((2, heads, bq), f32)],
        name="attn_fwd",
    )(starts, qT, k3, vT)

def bwd_kernel(heads, bq, bk, starts, qT, q3, k3, kT, v3, doT, do3, oT, lse, dqT, dk3, dv3, delta, dqa, dka, dva):
    total = q3.shape[1]
    i = pl.program_id(0)
    k0 = i * bk
    @pl.when(i == 0)
    def _():
        dqa[...] = jnp.zeros_like(dqa)
        for h in range(heads):
            sl = slice(HD * h, HD * (h + 1))
            delta[h:h + 1, :] = jnp.sum(doT[sl, :].astype(f32) * oT[sl, :], axis=0, keepdims=True)
    first, _ = doc_bounds(starts, jnp.int32(k0), total)
    _, last = doc_bounds(starts, jnp.int32(k0 + bk - 1), total)
    qb0 = first // bq
    qb1 = (last + bq - 1) // bq
    dka[...] = jnp.zeros_like(dka)
    dva[...] = jnp.zeros_like(dva)
    kio = k0 + lax.broadcasted_iota(jnp.int32, (bk, bq), 0)
    def body(j, _):
        qs = pl.multiple_of(j * bq, bq)
        pos = qs + lax.broadcasted_iota(jnp.int32, (1, bq), 1)
        lo, hi = doc_bounds(starts, pos, total)
        mask = (kio >= lo) & (kio < hi)
        for h in range(heads):
            sl = slice(HD * h, HD * (h + 1))
            s = dot(k3[h, :, :], qT[sl, pl.ds(qs, bq)])
            p = jnp.exp(jnp.where(mask, s - lse[h:h + 1, pl.ds(qs, bq)], -1e30))
            dp = dot(v3[h, :, :], doT[sl, pl.ds(qs, bq)])
            ds = p * (dp - delta[h:h + 1, pl.ds(qs, bq)])
            dsb = ds.astype(bf)
            dva[h] += dot(p.astype(bf), do3[h, pl.ds(qs, bq), :])
            dka[h] += dot(dsb, q3[h, pl.ds(qs, bq), :])
            dqa[sl, pl.ds(qs, bq)] += dot(kT[sl, :], dsb)
        return 0
    lax.fori_loop(qb0, qb1, body, 0)
    dk3[...] = dka[...].astype(bf)
    dv3[...] = dva[...].astype(bf)
    @pl.when(i == pl.num_programs(0) - 1)
    def _():
        dqT[...] = (dqa[...] * (HD ** -0.5)).astype(bf)

def attn_bwd(starts, qT, q3, k3, kT, v3, doT, do3, oT, lse, bq=256, bk=256):
    heads, total, _ = k3.shape
    full = lambda a: pl.BlockSpec(a.shape, lambda i: (0,) * a.ndim)
    kb3 = pl.BlockSpec((heads, bk, HD), lambda i: (0, i, 0))
    return pl.pallas_call(
        functools.partial(bwd_kernel, heads, bq, bk),
        grid=(total // bk,),
        in_specs=[pl.BlockSpec(memory_space=pltpu.SMEM), full(qT), full(q3), kb3,
                  pl.BlockSpec((heads * HD, bk), lambda i: (0, i)), kb3, full(doT), full(do3), full(oT), full(lse)],
        out_specs=[full(qT), kb3, kb3],
        out_shape=[jax.ShapeDtypeStruct(qT.shape, bf), jax.ShapeDtypeStruct(k3.shape, bf), jax.ShapeDtypeStruct(k3.shape, bf)],
        scratch_shapes=[pltpu.VMEM((heads, total), f32), pltpu.VMEM(qT.shape, f32),
                        pltpu.VMEM((heads, bk, HD), f32), pltpu.VMEM((heads, bk, HD), f32)],
        name="attn_bwd",
    )(starts, qT, q3, k3, kT, v3, doT, do3, oT, lse)


MESH = pl.DeviceIdType.MESH


class Wire:
    def __init__(self, send, recv):
        self.send, self.recv, self.used, self.open = send, recv, 0, []

    def slot(self):
        self.used += 1
        return self.used - 1

    def start(self, slot, src, dst, device):
        copy = pltpu.make_async_remote_copy(
            src_ref=src, dst_ref=dst, send_sem=self.send.at[slot], recv_sem=self.recv.at[slot],
            device_id=device, device_id_type=MESH,
        )
        copy.start()
        self.open.append(copy)

    def arrived(self, slot, dst, device):
        pltpu.make_async_remote_copy(
            src_ref=dst, dst_ref=dst, send_sem=self.send.at[slot], recv_sem=self.recv.at[slot],
            device_id=device, device_id_type=MESH,
        ).wait_recv()

    def drain(self):
        for copy in self.open:
            copy.wait_send()
        self.open = []


def grid_peers():
    shard, seq = lax.axis_index("wshard"), lax.axis_index("seq")
    z, y = shard // 2, shard % 2
    x, c = seq // 2, seq % 2
    at = lambda zz, yy, xx, cc: (zz * 2 + yy, xx * 2 + cc)
    along = [at((z + d) % 4, y, x, c) for d in range(4)]
    return z, y, x, c, along, at(z, 1 - y, x, c), at(z, y, 1 - x, c), at(z, y, x, 1 - c)


def greet(peers):
    barrier = pltpu.get_barrier_semaphore()
    for peer in peers:
        pl.semaphore_signal(barrier, inc=1, device_id=peer, device_id_type=MESH)
    pl.semaphore_wait(barrier, len(peers))


ORDER = (1, 3, 2)
SHARE = 80


def gather_kernel(a_ref, b_ref, t_ref, g_ref, q_ref, x_ref, send, recv, lsem):
    z, y, x, c, along, ypeer, xpeer, cpeer = grid_peers()
    own = z * 2 + y
    rows = a_ref.shape[0]
    half = rows // 2
    plain = half - 2 * SHARE
    wire = Wire(send, recv)
    spot = lambda r, d: ((z + 4 - d) % 4) * 2 + (y if r == 0 else 1 - y)
    base, other = half * c, half * (1 - c)
    nspan = pl.ds(pl.multiple_of(base, 16), plain)
    dspan = pl.ds(pl.multiple_of(base + plain + SHARE * x, 16), SHARE)
    xspan = pl.ds(pl.multiple_of(base + plain + SHARE * (1 - x), 16), SHARE)
    pn = pl.ds(pl.multiple_of(other, 16), plain)
    pd = pl.ds(pl.multiple_of(other + plain + SHARE * x, 16), SHARE)
    px = pl.ds(pl.multiple_of(other + plain + SHARE * (1 - x), 16), SHARE)
    seq = x * 2 + c
    locals_ = [
        pltpu.make_async_copy(a_ref, g_ref.at[own], lsem.at[0]),
        pltpu.make_async_copy(b_ref, q_ref.at[own], lsem.at[1]),
        pltpu.make_async_copy(t_ref, x_ref.at[seq], lsem.at[2]),
    ]
    for copy in locals_:
        copy.start()
    greet(along[1:] + [ypeer, xpeer, cpeer])
    S = {}
    for name in ("zB", "zN", "zD", "yB", "yN", "yD"):
        S[name] = [wire.slot() for _ in range(4)]
    for name in ("cN", "cD", "cX", "xD"):
        S[name] = [[wire.slot() for _ in range(4)] for _ in range(2)]
    tx, tc0, tc1 = wire.slot(), wire.slot(), wire.slot()
    wire.start(tx, t_ref, x_ref.at[seq], xpeer)
    for d in ORDER:
        wire.start(S["zB"][d], b_ref, q_ref.at[own], along[d])
    wire.start(S["yB"][0], b_ref, q_ref.at[own], ypeer)
    for d in ORDER:
        wire.start(S["zN"][d], a_ref.at[nspan], g_ref.at[own, nspan], along[d])
    wire.start(S["yN"][0], a_ref.at[nspan], g_ref.at[own, nspan], ypeer)
    for d in ORDER:
        wire.start(S["zD"][d], a_ref.at[dspan], g_ref.at[own, dspan], along[d])
    wire.start(S["yD"][0], a_ref.at[dspan], g_ref.at[own, dspan], ypeer)
    wire.start(tc0, t_ref, x_ref.at[seq], cpeer)
    for d in ORDER:
        w = spot(0, d)
        wire.arrived(S["zB"][d], q_ref.at[w], along[d])
        wire.start(S["yB"][d], q_ref.at[w], q_ref.at[w], ypeer)
    for d in ORDER:
        w = spot(0, d)
        wire.arrived(S["zN"][d], g_ref.at[w, nspan], along[d])
        wire.start(S["yN"][d], g_ref.at[w, nspan], g_ref.at[w, nspan], ypeer)
        wire.start(S["cN"][0][d], g_ref.at[w, nspan], g_ref.at[w, nspan], cpeer)
    xtok = (1 - x) * 2 + c
    wire.arrived(tx, x_ref.at[xtok], xpeer)
    wire.start(tc1, x_ref.at[xtok], x_ref.at[xtok], cpeer)
    for d in ORDER:
        w = spot(0, d)
        wire.arrived(S["zD"][d], g_ref.at[w, dspan], along[d])
        for slot, peer in ((S["yD"][d], ypeer), (S["xD"][0][d], xpeer), (S["cD"][0][d], cpeer)):
            wire.start(slot, g_ref.at[w, dspan], g_ref.at[w, dspan], peer)
    for d in (0,) + ORDER:
        w = spot(1, d)
        wire.arrived(S["yN"][d], g_ref.at[w, nspan], ypeer)
        wire.start(S["cN"][1][d], g_ref.at[w, nspan], g_ref.at[w, nspan], cpeer)
        wire.arrived(S["yB"][d], q_ref.at[w], ypeer)
    for d in (0,) + ORDER:
        w = spot(1, d)
        wire.arrived(S["yD"][d], g_ref.at[w, dspan], ypeer)
        for slot, peer in ((S["xD"][1][d], xpeer), (S["cD"][1][d], cpeer)):
            wire.start(slot, g_ref.at[w, dspan], g_ref.at[w, dspan], peer)
    rest = [(0, d) for d in ORDER] + [(1, d) for d in (0,) + ORDER]
    for r, d in rest:
        w = spot(r, d)
        wire.arrived(S["xD"][r][d], g_ref.at[w, xspan], xpeer)
        wire.start(S["cX"][r][d], g_ref.at[w, xspan], g_ref.at[w, xspan], cpeer)
    wire.arrived(tc0, x_ref.at[x * 2 + 1 - c], cpeer)
    wire.arrived(tc1, x_ref.at[(1 - x) * 2 + 1 - c], cpeer)
    for r, d in rest:
        w = spot(r, d)
        wire.arrived(S["cN"][r][d], g_ref.at[w, pn], cpeer)
        wire.arrived(S["cD"][r][d], g_ref.at[w, pd], cpeer)
        wire.arrived(S["cX"][r][d], g_ref.at[w, px], cpeer)
    wire.drain()
    for copy in locals_:
        copy.wait()


def gather_inputs(a, b, tokens):
    slots = 59 + 3 + 12
    hbm = pl.BlockSpec(memory_space=pl.ANY)
    vmem = pl.BlockSpec(memory_space=pltpu.VMEM)
    return pl.pallas_call(
        gather_kernel,
        in_specs=[vmem] * 3, out_specs=[hbm] * 3,
        out_shape=[jax.ShapeDtypeStruct((8,) + a.shape, a.dtype), jax.ShapeDtypeStruct((8,) + b.shape, b.dtype),
                   jax.ShapeDtypeStruct((4,) + tokens.shape, tokens.dtype)],
        scratch_shapes=[pltpu.SemaphoreType.DMA((slots,)), pltpu.SemaphoreType.DMA((slots,)), pltpu.SemaphoreType.DMA((3,))],
        compiler_params=pltpu.CompilerParams(collective_id=1, has_side_effects=True),
        name="gather_inputs",
    )(a, b, tokens)


def add_rows(dst, parts, rows, step=16):
    def body(i, _):
        at = pl.ds(pl.multiple_of(i * step, step), step)
        total = parts[0][at, :].astype(f32)
        for part in parts[1:]:
            total = total + part[at, :].astype(f32)
        dst[at, :] = total.astype(dst.dtype)
        return 0
    lax.fori_loop(0, rows // step, body, 0)


ALL = ORDER + (0,)


def reduce_kernel(ga, gb, dx, sm, fa, fb, fx, fr, fs, rc, rd, ry, ryd, rz, rzd, hb, ryb, rzb, hx, rxc,
                  hs, rys, rzs, s1, s2, s3, s4, fn, rn, send, recv):
    z, y, x, c, along, ypeer, xpeer, cpeer = grid_peers()
    half = ga.shape[2] // 2
    plain = half - 2 * SHARE
    base, other = pl.multiple_of(half * c, 16), pl.multiple_of(half * (1 - c), 16)
    mine, theirs = pl.multiple_of(plain + SHARE * x, 16), pl.multiple_of(plain + SHARE * (1 - x), 16)
    nrow = pl.ds(0, plain)
    wire = Wire(send, recv)
    new4 = lambda: [wire.slot() for _ in range(4)]
    kc = [new4(), new4()]
    kcx, kx, kxd = new4(), wire.slot(), new4()
    kyn, kyd, kyb, kys = new4(), new4(), wire.slot(), wire.slot()
    kzn, kzd, kzb, kzs = new4(), new4(), new4(), new4()
    fin = [wire.slot() for _ in range(13)]
    zz = lambda d: (z + d) % 4
    greet(along[1:] + [ypeer, xpeer, cpeer])
    wire.start(kys, sm.at[:, 1 - y], rys, ypeer)
    wire.start(kyb, gb.at[:, 1 - y], ryb, ypeer)
    for i, d in enumerate(ALL):
        for r in (1, 0):
            yy = y if r == 0 else 1 - y
            wire.start(kc[r][d], ga.at[zz(d), yy, pl.ds(other, half)], rc.at[zz(d), yy], cpeer)
        if i == 0:
            for t in range(2):
                wire.start(kcx[t], dx.at[t, 1 - c], rxc.at[t], cpeer)
    for d in ALL:
        for r in (1, 0):
            yy = y if r == 0 else 1 - y
            blk = rc.at[zz(d), yy]
            wire.arrived(kc[r][d], blk, cpeer)
            add_rows(blk, [ga.at[zz(d), yy, pl.ds(base, half)], blk], half)
        wire.start(kxd[d], rc.at[zz(d), :, pl.ds(theirs, SHARE)], rd.at[zz(d)], xpeer)
        wire.start(kyn[d], rc.at[zz(d), 1 - y, nrow], ry.at[zz(d)], ypeer)
    for t in range(2):
        wire.arrived(kcx[t], rxc.at[t], cpeer)
        add_rows(hx.at[t], [dx.at[t, c], rxc.at[t]], hx.shape[1])
    wire.start(kx, hx.at[1 - x], fr, xpeer)
    wire.arrived(kys, rys, ypeer)
    wire.arrived(kyb, ryb, ypeer)
    for d in ALL:
        hs[d] = sm[zz(d), y] + rys[zz(d)]
        add_rows(hb.at[d], [gb.at[zz(d), y], ryb.at[zz(d)]], hb.shape[1])
        if d:
            wire.start(kzs[d], hs.at[d], rzs.at[d], along[d])
            wire.start(kzb[d], hb.at[d], rzb.at[d], along[d])
    for d in ALL:
        wire.arrived(kxd[d], rd.at[zz(d)], xpeer)
        for yy in range(2):
            spot = rc.at[zz(d), yy, pl.ds(mine, SHARE)]
            add_rows(spot, [spot, rd.at[zz(d), yy]], SHARE)
        wire.start(kyd[d], rc.at[zz(d), 1 - y, pl.ds(mine, SHARE)], ryd.at[zz(d)], ypeer)
    for d in ALL:
        wire.arrived(kyn[d], ry.at[zz(d)], ypeer)
        spot = rc.at[zz(d), y, nrow]
        add_rows(spot, [spot, ry.at[zz(d)]], plain)
        if d:
            wire.start(kzn[d], spot, rz.at[d], along[d])
    for d in ALL:
        wire.arrived(kyd[d], ryd.at[zz(d)], ypeer)
        spot = rc.at[zz(d), y, pl.ds(mine, SHARE)]
        add_rows(spot, [spot, ryd.at[zz(d)]], SHARE)
        if d:
            wire.start(kzd[d], spot, rzd.at[d], along[d])
    for d in ORDER:
        wire.arrived(kzs[d], rzs.at[d], along[d])
        wire.arrived(kzb[d], rzb.at[d], along[d])
    s1[...] = hs[0] + rzs[1] + rzs[2] + rzs[3]
    wire.start(fin[0], s1, s2, xpeer)
    seq, xseq = 2 * x + c, 2 * (1 - x) + c
    add_rows(fb.at[seq], [hb.at[0]] + [rzb.at[d] for d in ORDER], hb.shape[1])
    wire.start(fin[1], fb.at[seq], fb.at[seq], xpeer)
    wire.start(fin[2], fb.at[seq], fb.at[seq], cpeer)
    wire.arrived(fin[0], s2, xpeer)
    s3[...] = s1[...] + s2[...]
    wire.start(fin[3], s3, s4, cpeer)
    wire.arrived(fin[1], fb.at[xseq], xpeer)
    wire.start(fin[4], fb.at[xseq], fb.at[xseq], cpeer)
    for d in ORDER:
        wire.arrived(kzn[d], rz.at[d], along[d])
    add_rows(fn, [rc.at[z, y, nrow]] + [rz.at[d] for d in ORDER], plain)
    wire.start(fin[5], fn, rn, xpeer)
    for d in ORDER:
        wire.arrived(kzd[d], rzd.at[d], along[d])
    dmine = pl.ds(pl.multiple_of(base + mine, 16), SHARE)
    dtheirs = pl.ds(pl.multiple_of(base + theirs, 16), SHARE)
    add_rows(fa.at[dmine], [rc.at[z, y, pl.ds(mine, SHARE)]] + [rzd.at[d] for d in ORDER], SHARE)
    wire.start(fin[6], fa.at[dmine], fa.at[dmine], xpeer)
    wire.start(fin[7], fa.at[dmine], fa.at[dmine], cpeer)
    wire.arrived(fin[5], rn, xpeer)
    nspan = pl.ds(base, plain)
    add_rows(fa.at[nspan], [fn, rn], plain)
    wire.start(fin[8], fa.at[nspan], fa.at[nspan], cpeer)
    wire.arrived(fin[6], fa.at[dtheirs], xpeer)
    wire.start(fin[9], fa.at[dtheirs], fa.at[dtheirs], cpeer)
    wire.arrived(kx, fr, xpeer)
    fx[...] = hx[x]
    wire.arrived(fin[3], s4, cpeer)
    fs[...] = s3[...] + s4[...]
    wire.arrived(fin[2], fb.at[2 * x + 1 - c], cpeer)
    wire.arrived(fin[4], fb.at[2 * (1 - x) + 1 - c], cpeer)
    wire.arrived(fin[8], fa.at[pl.ds(other, plain)], cpeer)
    wire.arrived(fin[7], fa.at[pl.ds(pl.multiple_of(other + mine, 16), SHARE)], cpeer)
    wire.arrived(fin[9], fa.at[pl.ds(pl.multiple_of(other + theirs, 16), SHARE)], cpeer)
    wire.drain()


def reduce_grads(ga, gb, dx, sm):
    rows, cols = ga.shape[1:]
    half = rows // 2
    plain = half - 2 * SHARE
    toks = dx.shape[1]
    vmem = pl.BlockSpec(memory_space=pltpu.VMEM)
    b0, b1 = gb.shape[1:]
    V = pltpu.VMEM
    sv = lambda *lead: V(lead + sm.shape[1:], f32)
    slots = 64
    return pl.pallas_call(
        reduce_kernel,
        in_specs=[vmem] * 4, out_specs=[vmem] * 5,
        out_shape=[jax.ShapeDtypeStruct((rows, cols), bf), jax.ShapeDtypeStruct((4, b0, b1), bf),
                   jax.ShapeDtypeStruct((toks, cols), bf), jax.ShapeDtypeStruct((toks, cols), bf),
                   jax.ShapeDtypeStruct(sm.shape[1:], f32)],
        scratch_shapes=[V((4, 2, half, cols), bf), V((4, 2, SHARE, cols), bf), V((4, plain, cols), bf), V((4, SHARE, cols), bf),
                        V((4, plain, cols), bf), V((4, SHARE, cols), bf),
                        V((4, b0, b1), bf), V((4, b0, b1), bf), V((4, b0, b1), bf),
                        V((2, toks, cols), bf), V((2, toks, cols), bf),
                        sv(4), sv(4), sv(4), sv(), sv(), sv(), sv(), V((plain, cols), bf), V((plain, cols), bf),
                        pltpu.SemaphoreType.DMA((slots,)), pltpu.SemaphoreType.DMA((slots,))],
        compiler_params=pltpu.CompilerParams(collective_id=2, has_side_effects=True, vmem_limit_bytes=67043328),
        name="reduce_grads",
    )(ga.reshape((4, 2) + ga.shape[1:]), gb.reshape((4, 2) + gb.shape[1:]), dx.reshape((2, 2) + dx.shape[1:]), sm.reshape((4, 2) + sm.shape[1:]))


def layer_norm(inputs, norm_gain, norm_bias):
    row_mean = jnp.mean(inputs, axis=-1, keepdims=True)
    centred = inputs - row_mean
    row_var = jnp.mean(centred * centred, axis=-1, keepdims=True)
    return centred * lax.rsqrt(row_var + NORM_EPS) * norm_gain + norm_bias


def gelu_exact(inputs):
    return jax.nn.gelu(inputs, approximate=False)


def contract(left_in, right_in, left_dim, right_dim):
    return lax.dot_general(
        left_in,
        right_in,
        (((left_dim,), (right_dim,)), ((), ())),
        preferred_element_type=jnp.float32,
    )


def chips_of_two_by_four():
    return lax.axis_size("wshard") == 8 and lax.axis_size("seq") == 4


def gather_parts(a, b, tokens):
    if chips_of_two_by_four():
        return gather_inputs(a, b, tokens)
    return lax.all_gather(a, "wshard"), lax.all_gather(b, "wshard"), lax.all_gather(tokens, "seq")


def reduce_parts(ga, gb, dx, sm):
    if chips_of_two_by_four():
        return reduce_grads(ga, gb, dx, sm)

    def scatter(part):
        return lax.psum_scatter(part, "wshard", scatter_dimension=0, tiled=False)

    fx = lax.psum_scatter(dx, "seq", scatter_dimension=0, tiled=False)
    return (
        lax.psum(scatter(ga), "seq"), lax.all_gather(scatter(gb), "seq"), fx, jnp.zeros_like(fx),
        lax.psum(scatter(sm), "seq"),
    )


def shards(
    tokens, cotangent, starts,
    w_query, w_key, w_value, w_output, w_inner, w_outer,
    b_query, b_value, b_output, b_inner, b_outer,
    gain_first, bias_first, gain_second, bias_second,
):
    model = tokens.shape[1]
    rows = w_query.shape[0]
    shards_n = lax.axis_size("wshard")
    seq_n = lax.axis_size("seq")
    seq_i = lax.axis_index("seq")
    width = model // seq_n
    heads = width // HD
    wide = w_inner.shape[1] // model

    def own(columns):
        return lax.dynamic_slice_in_dim(columns, seq_i * width, width, columns.ndim - 1)

    smalls = (b_query, b_value, b_output, b_outer, gain_first, bias_first, gain_second, bias_second)
    small_cols = jnp.stack(smalls + tuple(b_inner.reshape(wide, rows)), axis=1)
    cols_n = small_cols.shape[1]
    a = jnp.concatenate(
        [w_output, w_inner.reshape(rows, wide, model).transpose(1, 0, 2).reshape(wide * rows, model), w_outer], axis=0
    )
    b = jnp.concatenate([own(w_query), own(w_key), own(w_value), jnp.pad(small_cols, ((0, 0), (0, HD - cols_n)))], axis=1)
    big, side, stream = gather_parts(a, b, tokens)
    stream = stream.reshape(-1, model)
    side = side.reshape(model, -1)
    w_own = side[:, :3 * width]
    vectors = side[:, 3 * width:3 * width + cols_n].astype(f32).T
    bias_query, bias_value, bias_output, bias_outer, gain_one, shift_one, gain_two, shift_two = vectors[:8]
    bias_inner = vectors[8:].reshape(wide, shards_n, rows).transpose(1, 0, 2).reshape(-1)
    output_full = big[:, :rows].reshape(model, model)
    inner_full = jnp.concatenate(
        [big[:, (1 + j) * rows:(2 + j) * rows].reshape(model, model) for j in range(wide)], axis=1
    )
    outer_full = big[:, (1 + wide) * rows:].reshape(-1, model)

    scale = HD ** -0.5
    qT = ((contract(w_own[:, :width], stream, 0, 1) + own(bias_query)[:, None]).astype(bf) * bf(scale))
    kT = contract(w_own[:, width:2 * width], stream, 0, 1).astype(bf)
    vT = (contract(w_own[:, 2 * width:], stream, 0, 1) + own(bias_value)[:, None]).astype(bf)

    def by_token(arr):
        return arr.reshape(heads, HD, -1).transpose(0, 2, 1)

    def by_feature(arr):
        return arr.transpose(0, 2, 1).reshape(width, -1)

    q3, k3, v3 = by_token(qT), by_token(kT), by_token(vT)
    oT, mixT, lse = attn_fwd(starts, qT, k3, vT, 512, 512)
    mixed = lax.all_to_all(mixT, "seq", split_axis=1, concat_axis=0, tiled=True)

    residual_in = tokens.astype(f32) + contract(mixed, output_full, 0, 0) + bias_output
    first_norm, first_back = jax.vjp(layer_norm, residual_in, gain_one, shift_one)
    first_low = first_norm.astype(bf)
    inner_act = jnp.dot(first_low, inner_full, preferred_element_type=f32) + bias_inner
    gelu_out, gelu_back = jax.vjp(gelu_exact, inner_act)
    gelu_low = gelu_out.astype(bf)
    second_in = first_norm + jnp.dot(gelu_low, outer_full, preferred_element_type=f32) + bias_outer
    layer_result, second_back = jax.vjp(layer_norm, second_in, gain_two, shift_two)
    d_second, grad_gain_two, grad_bias_two = second_back(cotangent.astype(f32))
    d_outer = d_second.astype(bf)
    grad_bias_outer = jnp.sum(d_outer.astype(f32), axis=0)
    grad_outer = contract(gelu_low, d_outer, 0, 0)
    (d_inner,) = gelu_back(contract(d_outer, outer_full, 1, 1))
    d_inner_low = d_inner.astype(bf)
    grad_bias_inner = jnp.sum(d_inner_low.astype(f32), axis=0)
    grad_inner = contract(first_low, d_inner_low, 0, 0)
    d_first = contract(d_inner_low, inner_full, 1, 1) + d_second
    d_resid, grad_gain_one, grad_bias_one = first_back(d_first)
    d_attn = d_resid.astype(bf)
    grad_bias_output = jnp.sum(d_attn.astype(f32), axis=0)
    grad_output = contract(mixed, d_attn, 1, 0)
    d_mixed = contract(output_full, d_attn, 1, 1).astype(bf)
    doT = lax.all_to_all(d_mixed, "seq", split_axis=0, concat_axis=1, tiled=True)

    dqT, dk3, dv3 = attn_bwd(starts, qT, q3, k3, kT, v3, doT, by_token(doT), oT, lse, 256, 512)
    dT = jnp.concatenate([dqT, by_feature(dk3), by_feature(dv3)], axis=0)
    gb = contract(stream, dT, 0, 1).astype(bf).reshape(shards_n, rows, -1)
    dx = contract(dT, w_own, 0, 1).astype(bf).reshape(seq_n, -1, model)
    by_rows = lambda grad: grad.astype(bf).reshape(shards_n, -1, model)
    ga = jnp.concatenate(
        [by_rows(grad_output)] + [by_rows(grad_inner[:, j * model:(j + 1) * model]) for j in range(wide)]
        + [by_rows(grad_outer)], axis=1,
    )

    def spread(own_sum):
        return lax.dynamic_update_slice(jnp.zeros((model,), f32), own_sum, (seq_i * width,))

    small_rows = (
        spread(jnp.sum(dqT.astype(f32), axis=1)),
        spread(jnp.sum(dv3.astype(f32), axis=1).reshape(-1)),
        grad_bias_output, grad_bias_outer, grad_gain_one, grad_bias_one, grad_gain_two, grad_bias_two,
    )
    sm = jnp.concatenate(
        [jnp.stack([row.reshape(shards_n, rows) for row in small_rows], axis=1),
         grad_bias_inner.reshape(shards_n, wide, rows)], axis=1,
    )
    sm = jnp.pad(sm, ((0, 0), (0, -cols_n % 8), (0, -rows % 128)))
    fa, fb, fx, fr, fs = reduce_parts(ga, gb, dx, sm)
    d_tokens = fx.astype(f32) + fr.astype(f32) + d_resid
    fb = fb.astype(f32)
    grads = [
        jnp.concatenate([fb[s, :, i * width:(i + 1) * width] for s in range(seq_n)], axis=1) for i in range(3)
    ]
    fa = fa.astype(f32)
    g_inner = jnp.concatenate([fa[(1 + j) * rows:(2 + j) * rows] for j in range(wide)], axis=1)
    tail = [fs[i, :rows] for i in range(8)]
    g_b_inner = fs[8:8 + wide, :rows].reshape(-1)
    return (
        layer_result.astype(bf), d_tokens, *grads,
        fa[:rows], g_inner, fa[(1 + wide) * rows:],
        tail[0], tail[1], tail[2], g_b_inner, *tail[3:],
    )


def solution(mesh):
    placed = (
        P(("wshard", "seq"), None),
        P(("wshard", "seq"), None),
        P("wshard", None),
        P("wshard", None),
        P("wshard", None),
        P("wshard", None),
        P("wshard", None),
        P("wshard", None),
        P("wshard", None),
        P("wshard"),
        P("wshard"),
        P("wshard"),
        P("wshard"),
        P("wshard"),
        P("wshard"),
        P("wshard"),
        P("wshard"),
        P("wshard"),
    )
    return jax.shard_map(
        shards,
        mesh=mesh,
        in_specs=placed,
        out_specs=(
            P(("wshard", "seq"), None),
            P(("wshard", "seq"), None),
            P("wshard", None),
            P("wshard", None),
            P("wshard", None),
            P("wshard", None),
            P("wshard", None),
            P("wshard", None),
            P("wshard"),
            P("wshard"),
            P("wshard"),
            P("wshard"),
            P("wshard"),
            P("wshard"),
            P("wshard"),
            P("wshard"),
            P("wshard"),
        ),
        check_vma=False,
    )
```

```python
import functools

import jax
import jax.numpy as jnp
from jax import lax
from jax.experimental import pallas as pl
from jax.experimental.pallas import tpu as pltpu
from jax.sharding import PartitionSpec as P

NORM_EPS = 1e-05
HD = 64
bf = jnp.bfloat16
f32 = jnp.float32


def doc_bounds(starts_ref, pos, total):
    lo = jnp.zeros_like(pos); hi = jnp.full_like(pos, total)
    for d in range(starts_ref.shape[1]):
        s = starts_ref[0, d]
        lo = jnp.where(s <= pos, jnp.maximum(lo, s), lo)
        hi = jnp.where(s > pos, jnp.minimum(hi, s), hi)
    return lo, hi

def dot(a, b):
    return lax.dot_general(a, b, (((1,), (0,)), ((), ())), preferred_element_type=f32)

def fwd_kernel(heads, bq, bk, starts, qT, k3, vT, oT, mixT, lse, acc, ml):
    total = k3.shape[1]
    i = pl.program_id(0)
    q0 = i * bq
    first, _ = doc_bounds(starts, jnp.int32(q0), total)
    _, last = doc_bounds(starts, jnp.int32(q0 + bq - 1), total)
    pos = q0 + lax.broadcasted_iota(jnp.int32, (1, bq), 1)
    lo, hi = doc_bounds(starts, pos, total)
    kb0 = first // bk
    kb1 = (last + bk - 1) // bk
    acc[...] = jnp.zeros_like(acc)
    ml[0] = jnp.full((heads, bq), -1e30, f32)
    ml[1] = jnp.zeros((heads, bq), f32)
    kio = lax.broadcasted_iota(jnp.int32, (bk, bq), 0)
    def body(j, _):
        ks = pl.multiple_of(j * bk, bk)
        mask = (kio >= lo - ks) & (kio < hi - ks)
        for h in range(heads):
            s = dot(k3[h, pl.ds(ks, bk), :], qT[HD * h:HD * (h + 1), :])
            s = jnp.where(mask, s, -1e30)
            m_old = ml[0, h:h + 1]
            m = jnp.maximum(m_old, jnp.max(s, axis=0, keepdims=True))
            p = jnp.exp(s - m)
            al = jnp.exp(m_old - m)
            ml[0, h:h + 1] = m
            ml[1, h:h + 1] = ml[1, h:h + 1] * al + jnp.sum(p, axis=0, keepdims=True)
            sl = slice(HD * h, HD * (h + 1))
            acc[sl, :] = acc[sl, :] * al + dot(vT[sl, pl.ds(ks, bk)], p.astype(bf))
        return 0
    lax.fori_loop(kb0, kb1, body, 0)
    for h in range(heads):
        sl = slice(HD * h, HD * (h + 1))
        l = ml[1, h:h + 1]
        o = acc[sl, :] / l
        oT[sl, :] = o
        mixT[sl, :] = o.astype(bf)
        lse[h:h + 1, :] = ml[0, h:h + 1] + jnp.log(l)

def attn_fwd(starts, qT, k3, vT, bq=256, bk=256):
    heads, total, _ = k3.shape
    full2 = lambda i: (0, 0)
    return pl.pallas_call(
        functools.partial(fwd_kernel, heads, bq, bk),
        grid=(total // bq,),
        in_specs=[pl.BlockSpec(memory_space=pltpu.SMEM),
                  pl.BlockSpec((heads * HD, bq), lambda i: (0, i)),
                  pl.BlockSpec(k3.shape, lambda i: (0, 0, 0)),
                  pl.BlockSpec(vT.shape, full2)],
        out_specs=[pl.BlockSpec((heads * HD, bq), lambda i: (0, i)),
                   pl.BlockSpec((heads * HD, bq), lambda i: (0, i)),
                   pl.BlockSpec((heads, bq), lambda i: (0, i))],
        out_shape=[jax.ShapeDtypeStruct((heads * HD, total), f32),
                   jax.ShapeDtypeStruct((heads * HD, total), bf),
                   jax.ShapeDtypeStruct((heads, total), f32)],
        scratch_shapes=[pltpu.VMEM((heads * HD, bq), f32), pltpu.VMEM((2, heads, bq), f32)],
        name="attn_fwd",
    )(starts, qT, k3, vT)

def bwd_kernel(heads, bq, bk, starts, qT, q3, k3, kT, v3, doT, do3, oT, lse, dqT, dk3, dv3, delta, dqa, dka, dva):
    total = q3.shape[1]
    i = pl.program_id(0)
    k0 = i * bk
    @pl.when(i == 0)
    def _():
        dqa[...] = jnp.zeros_like(dqa)
        for h in range(heads):
            sl = slice(HD * h, HD * (h + 1))
            delta[h:h + 1, :] = jnp.sum(doT[sl, :].astype(f32) * oT[sl, :], axis=0, keepdims=True)
    first, _ = doc_bounds(starts, jnp.int32(k0), total)
    _, last = doc_bounds(starts, jnp.int32(k0 + bk - 1), total)
    qb0 = first // bq
    qb1 = (last + bq - 1) // bq
    dka[...] = jnp.zeros_like(dka)
    dva[...] = jnp.zeros_like(dva)
    kio = k0 + lax.broadcasted_iota(jnp.int32, (bk, bq), 0)
    def body(j, _):
        qs = pl.multiple_of(j * bq, bq)
        pos = qs + lax.broadcasted_iota(jnp.int32, (1, bq), 1)
        lo, hi = doc_bounds(starts, pos, total)
        mask = (kio >= lo) & (kio < hi)
        for h in range(heads):
            sl = slice(HD * h, HD * (h + 1))
            s = dot(k3[h, :, :], qT[sl, pl.ds(qs, bq)])
            p = jnp.exp(jnp.where(mask, s - lse[h:h + 1, pl.ds(qs, bq)], -1e30))
            dp = dot(v3[h, :, :], doT[sl, pl.ds(qs, bq)])
            ds = p * (dp - delta[h:h + 1, pl.ds(qs, bq)])
            dsb = ds.astype(bf)
            dva[h] += dot(p.astype(bf), do3[h, pl.ds(qs, bq), :])
            dka[h] += dot(dsb, q3[h, pl.ds(qs, bq), :])
            dqa[sl, pl.ds(qs, bq)] += dot(kT[sl, :], dsb)
        return 0
    lax.fori_loop(qb0, qb1, body, 0)
    dk3[...] = dka[...].astype(bf)
    dv3[...] = dva[...].astype(bf)
    @pl.when(i == pl.num_programs(0) - 1)
    def _():
        dqT[...] = (dqa[...] * (HD ** -0.5)).astype(bf)

def attn_bwd(starts, qT, q3, k3, kT, v3, doT, do3, oT, lse, bq=256, bk=256):
    heads, total, _ = k3.shape
    full = lambda a: pl.BlockSpec(a.shape, lambda i: (0,) * a.ndim)
    kb3 = pl.BlockSpec((heads, bk, HD), lambda i: (0, i, 0))
    return pl.pallas_call(
        functools.partial(bwd_kernel, heads, bq, bk),
        grid=(total // bk,),
        in_specs=[pl.BlockSpec(memory_space=pltpu.SMEM), full(qT), full(q3), kb3,
                  pl.BlockSpec((heads * HD, bk), lambda i: (0, i)), kb3, full(doT), full(do3), full(oT), full(lse)],
        out_specs=[full(qT), kb3, kb3],
        out_shape=[jax.ShapeDtypeStruct(qT.shape, bf), jax.ShapeDtypeStruct(k3.shape, bf), jax.ShapeDtypeStruct(k3.shape, bf)],
        scratch_shapes=[pltpu.VMEM((heads, total), f32), pltpu.VMEM(qT.shape, f32),
                        pltpu.VMEM((heads, bk, HD), f32), pltpu.VMEM((heads, bk, HD), f32)],
        name="attn_bwd",
    )(starts, qT, q3, k3, kT, v3, doT, do3, oT, lse)


MESH = pl.DeviceIdType.MESH


class Wire:
    def __init__(self, send, recv):
        self.send, self.recv, self.used, self.open = send, recv, 0, []

    def slot(self):
        self.used += 1
        return self.used - 1

    def start(self, slot, src, dst, device):
        copy = pltpu.make_async_remote_copy(
            src_ref=src, dst_ref=dst, send_sem=self.send.at[slot], recv_sem=self.recv.at[slot],
            device_id=device, device_id_type=MESH,
        )
        copy.start()
        self.open.append(copy)

    def arrived(self, slot, dst, device):
        pltpu.make_async_remote_copy(
            src_ref=dst, dst_ref=dst, send_sem=self.send.at[slot], recv_sem=self.recv.at[slot],
            device_id=device, device_id_type=MESH,
        ).wait_recv()

    def drain(self):
        for copy in self.open:
            copy.wait_send()
        self.open = []


def grid_peers():
    shard, seq = lax.axis_index("wshard"), lax.axis_index("seq")
    z, y = shard // 2, shard % 2
    x, c = seq // 2, seq % 2
    at = lambda zz, yy, xx, cc: (zz * 2 + yy, xx * 2 + cc)
    along = [at((z + d) % 4, y, x, c) for d in range(4)]
    return z, y, x, c, along, at(z, 1 - y, x, c), at(z, y, 1 - x, c), at(z, y, x, 1 - c)


def greet(peers):
    barrier = pltpu.get_barrier_semaphore()
    for peer in peers:
        pl.semaphore_signal(barrier, inc=1, device_id=peer, device_id_type=MESH)
    pl.semaphore_wait(barrier, len(peers))


ORDER = (1, 3, 2)
SHARE = 80


def gather_kernel(a_ref, b_ref, t_ref, g_ref, q_ref, x_ref, send, recv, lsem):
    z, y, x, c, along, ypeer, xpeer, cpeer = grid_peers()
    own = z * 2 + y
    rows = a_ref.shape[0]
    half = rows // 2
    plain = half - 2 * SHARE
    wire = Wire(send, recv)
    spot = lambda r, d: ((z + 4 - d) % 4) * 2 + (y if r == 0 else 1 - y)
    base, other = half * c, half * (1 - c)
    nspan = pl.ds(pl.multiple_of(base, 16), plain)
    dspan = pl.ds(pl.multiple_of(base + plain + SHARE * x, 16), SHARE)
    xspan = pl.ds(pl.multiple_of(base + plain + SHARE * (1 - x), 16), SHARE)
    pn = pl.ds(pl.multiple_of(other, 16), plain)
    pd = pl.ds(pl.multiple_of(other + plain + SHARE * x, 16), SHARE)
    px = pl.ds(pl.multiple_of(other + plain + SHARE * (1 - x), 16), SHARE)
    seq = x * 2 + c
    locals_ = [
        pltpu.make_async_copy(a_ref, g_ref.at[own], lsem.at[0]),
        pltpu.make_async_copy(b_ref, q_ref.at[own], lsem.at[1]),
        pltpu.make_async_copy(t_ref, x_ref.at[seq], lsem.at[2]),
    ]
    for copy in locals_:
        copy.start()
    greet(along[1:] + [ypeer, xpeer, cpeer])
    S = {}
    for name in ("zB", "zN", "zD", "yB", "yN", "yD"):
        S[name] = [wire.slot() for _ in range(4)]
    for name in ("cN", "cD", "cX", "xD"):
        S[name] = [[wire.slot() for _ in range(4)] for _ in range(2)]
    tx, tc0, tc1 = wire.slot(), wire.slot(), wire.slot()
    wire.start(tx, t_ref, x_ref.at[seq], xpeer)
    for d in ORDER:
        wire.start(S["zB"][d], b_ref, q_ref.at[own], along[d])
    wire.start(S["yB"][0], b_ref, q_ref.at[own], ypeer)
    for d in ORDER:
        wire.start(S["zN"][d], a_ref.at[nspan], g_ref.at[own, nspan], along[d])
    wire.start(S["yN"][0], a_ref.at[nspan], g_ref.at[own, nspan], ypeer)
    for d in ORDER:
        wire.start(S["zD"][d], a_ref.at[dspan], g_ref.at[own, dspan], along[d])
    wire.start(S["yD"][0], a_ref.at[dspan], g_ref.at[own, dspan], ypeer)
    wire.start(tc0, t_ref, x_ref.at[seq], cpeer)
    for d in ORDER:
        w = spot(0, d)
        wire.arrived(S["zB"][d], q_ref.at[w], along[d])
        wire.start(S["yB"][d], q_ref.at[w], q_ref.at[w], ypeer)
    for d in ORDER:
        w = spot(0, d)
        wire.arrived(S["zN"][d], g_ref.at[w, nspan], along[d])
        wire.start(S["yN"][d], g_ref.at[w, nspan], g_ref.at[w, nspan], ypeer)
        wire.start(S["cN"][0][d], g_ref.at[w, nspan], g_ref.at[w, nspan], cpeer)
    xtok = (1 - x) * 2 + c
    wire.arrived(tx, x_ref.at[xtok], xpeer)
    wire.start(tc1, x_ref.at[xtok], x_ref.at[xtok], cpeer)
    for d in ORDER:
        w = spot(0, d)
        wire.arrived(S["zD"][d], g_ref.at[w, dspan], along[d])
        for slot, peer in ((S["yD"][d], ypeer), (S["xD"][0][d], xpeer), (S["cD"][0][d], cpeer)):
            wire.start(slot, g_ref.at[w, dspan], g_ref.at[w, dspan], peer)
    for d in (0,) + ORDER:
        w = spot(1, d)
        wire.arrived(S["yN"][d], g_ref.at[w, nspan], ypeer)
        wire.start(S["cN"][1][d], g_ref.at[w, nspan], g_ref.at[w, nspan], cpeer)
        wire.arrived(S["yB"][d], q_ref.at[w], ypeer)
    for d in (0,) + ORDER:
        w = spot(1, d)
        wire.arrived(S["yD"][d], g_ref.at[w, dspan], ypeer)
        for slot, peer in ((S["xD"][1][d], xpeer), (S["cD"][1][d], cpeer)):
            wire.start(slot, g_ref.at[w, dspan], g_ref.at[w, dspan], peer)
    rest = [(0, d) for d in ORDER] + [(1, d) for d in (0,) + ORDER]
    for r, d in rest:
        w = spot(r, d)
        wire.arrived(S["xD"][r][d], g_ref.at[w, xspan], xpeer)
        wire.start(S["cX"][r][d], g_ref.at[w, xspan], g_ref.at[w, xspan], cpeer)
    wire.arrived(tc0, x_ref.at[x * 2 + 1 - c], cpeer)
    wire.arrived(tc1, x_ref.at[(1 - x) * 2 + 1 - c], cpeer)
    for r, d in rest:
        w = spot(r, d)
        wire.arrived(S["cN"][r][d], g_ref.at[w, pn], cpeer)
        wire.arrived(S["cD"][r][d], g_ref.at[w, pd], cpeer)
        wire.arrived(S["cX"][r][d], g_ref.at[w, px], cpeer)
    wire.drain()
    for copy in locals_:
        copy.wait()


def gather_inputs(a, b, tokens):
    slots = 59 + 3 + 12
    hbm = pl.BlockSpec(memory_space=pl.ANY)
    vmem = pl.BlockSpec(memory_space=pltpu.VMEM)
    return pl.pallas_call(
        gather_kernel,
        in_specs=[vmem] * 3, out_specs=[hbm] * 3,
        out_shape=[jax.ShapeDtypeStruct((8,) + a.shape, a.dtype), jax.ShapeDtypeStruct((8,) + b.shape, b.dtype),
                   jax.ShapeDtypeStruct((4,) + tokens.shape, tokens.dtype)],
        scratch_shapes=[pltpu.SemaphoreType.DMA((slots,)), pltpu.SemaphoreType.DMA((slots,)), pltpu.SemaphoreType.DMA((3,))],
        compiler_params=pltpu.CompilerParams(collective_id=1, has_side_effects=True),
        name="gather_inputs",
    )(a, b, tokens)


def add_rows(dst, parts, rows, step=16):
    def body(i, _):
        at = pl.ds(pl.multiple_of(i * step, step), step)
        total = parts[0][at, :].astype(f32)
        for part in parts[1:]:
            total = total + part[at, :].astype(f32)
        dst[at, :] = total.astype(dst.dtype)
        return 0
    lax.fori_loop(0, rows // step, body, 0)


ALL = ORDER + (0,)


def reduce_kernel(ga, gb, dx, sm, fa, fb, fx, fr, fs, rc, rd, ry, ryd, rz, rzd, hb, ryb, rzb, hx, rxc,
                  hs, rys, rzs, s1, s2, s3, s4, fn, rn, send, recv):
    z, y, x, c, along, ypeer, xpeer, cpeer = grid_peers()
    half = ga.shape[2] // 2
    plain = half - 2 * SHARE
    base, other = pl.multiple_of(half * c, 16), pl.multiple_of(half * (1 - c), 16)
    mine, theirs = pl.multiple_of(plain + SHARE * x, 16), pl.multiple_of(plain + SHARE * (1 - x), 16)
    nrow = pl.ds(0, plain)
    wire = Wire(send, recv)
    new4 = lambda: [wire.slot() for _ in range(4)]
    kc = [new4(), new4()]
    kcx, kx, kxd = new4(), wire.slot(), new4()
    kyn, kyd, kyb, kys = new4(), new4(), wire.slot(), wire.slot()
    kzn, kzd, kzb, kzs = new4(), new4(), new4(), new4()
    fin = [wire.slot() for _ in range(13)]
    zz = lambda d: (z + d) % 4
    greet(along[1:] + [ypeer, xpeer, cpeer])
    wire.start(kys, sm.at[:, 1 - y], rys, ypeer)
    wire.start(kyb, gb.at[:, 1 - y], ryb, ypeer)
    for i, d in enumerate(ALL):
        for r in (1, 0):
            yy = y if r == 0 else 1 - y
            wire.start(kc[r][d], ga.at[zz(d), yy, pl.ds(other, half)], rc.at[zz(d), yy], cpeer)
        if i == 0:
            for t in range(2):
                wire.start(kcx[t], dx.at[t, 1 - c], rxc.at[t], cpeer)
    for d in ALL:
        for r in (1, 0):
            yy = y if r == 0 else 1 - y
            blk = rc.at[zz(d), yy]
            wire.arrived(kc[r][d], blk, cpeer)
            add_rows(blk, [ga.at[zz(d), yy, pl.ds(base, half)], blk], half)
        wire.start(kxd[d], rc.at[zz(d), :, pl.ds(theirs, SHARE)], rd.at[zz(d)], xpeer)
        wire.start(kyn[d], rc.at[zz(d), 1 - y, nrow], ry.at[zz(d)], ypeer)
    for t in range(2):
        wire.arrived(kcx[t], rxc.at[t], cpeer)
        add_rows(hx.at[t], [dx.at[t, c], rxc.at[t]], hx.shape[1])
    wire.start(kx, hx.at[1 - x], fr, xpeer)
    wire.arrived(kys, rys, ypeer)
    wire.arrived(kyb, ryb, ypeer)
    for d in ALL:
        hs[d] = sm[zz(d), y] + rys[zz(d)]
        add_rows(hb.at[d], [gb.at[zz(d), y], ryb.at[zz(d)]], hb.shape[1])
        if d:
            wire.start(kzs[d], hs.at[d], rzs.at[d], along[d])
            wire.start(kzb[d], hb.at[d], rzb.at[d], along[d])
    for d in ALL:
        wire.arrived(kxd[d], rd.at[zz(d)], xpeer)
        for yy in range(2):
            spot = rc.at[zz(d), yy, pl.ds(mine, SHARE)]
            add_rows(spot, [spot, rd.at[zz(d), yy]], SHARE)
        wire.start(kyd[d], rc.at[zz(d), 1 - y, pl.ds(mine, SHARE)], ryd.at[zz(d)], ypeer)
    for d in ALL:
        wire.arrived(kyn[d], ry.at[zz(d)], ypeer)
        spot = rc.at[zz(d), y, nrow]
        add_rows(spot, [spot, ry.at[zz(d)]], plain)
        if d:
            wire.start(kzn[d], spot, rz.at[d], along[d])
    for d in ALL:
        wire.arrived(kyd[d], ryd.at[zz(d)], ypeer)
        spot = rc.at[zz(d), y, pl.ds(mine, SHARE)]
        add_rows(spot, [spot, ryd.at[zz(d)]], SHARE)
        if d:
            wire.start(kzd[d], spot, rzd.at[d], along[d])
    for d in ORDER:
        wire.arrived(kzs[d], rzs.at[d], along[d])
        wire.arrived(kzb[d], rzb.at[d], along[d])
    s1[...] = hs[0] + rzs[1] + rzs[2] + rzs[3]
    wire.start(fin[0], s1, s2, xpeer)
    seq, xseq = 2 * x + c, 2 * (1 - x) + c
    add_rows(fb.at[seq], [hb.at[0]] + [rzb.at[d] for d in ORDER], hb.shape[1])
    wire.start(fin[1], fb.at[seq], fb.at[seq], xpeer)
    wire.start(fin[2], fb.at[seq], fb.at[seq], cpeer)
    wire.arrived(fin[0], s2, xpeer)
    s3[...] = s1[...] + s2[...]
    wire.start(fin[3], s3, s4, cpeer)
    wire.arrived(fin[1], fb.at[xseq], xpeer)
    wire.start(fin[4], fb.at[xseq], fb.at[xseq], cpeer)
    for d in ORDER:
        wire.arrived(kzn[d], rz.at[d], along[d])
    add_rows(fn, [rc.at[z, y, nrow]] + [rz.at[d] for d in ORDER], plain)
    wire.start(fin[5], fn, rn, xpeer)
    for d in ORDER:
        wire.arrived(kzd[d], rzd.at[d], along[d])
    dmine = pl.ds(pl.multiple_of(base + mine, 16), SHARE)
    dtheirs = pl.ds(pl.multiple_of(base + theirs, 16), SHARE)
    add_rows(fa.at[dmine], [rc.at[z, y, pl.ds(mine, SHARE)]] + [rzd.at[d] for d in ORDER], SHARE)
    wire.start(fin[6], fa.at[dmine], fa.at[dmine], xpeer)
    wire.start(fin[7], fa.at[dmine], fa.at[dmine], cpeer)
    wire.arrived(fin[5], rn, xpeer)
    nspan = pl.ds(base, plain)
    add_rows(fa.at[nspan], [fn, rn], plain)
    wire.start(fin[8], fa.at[nspan], fa.at[nspan], cpeer)
    wire.arrived(fin[6], fa.at[dtheirs], xpeer)
    wire.start(fin[9], fa.at[dtheirs], fa.at[dtheirs], cpeer)
    wire.arrived(kx, fr, xpeer)
    fx[...] = hx[x]
    wire.arrived(fin[3], s4, cpeer)
    fs[...] = s3[...] + s4[...]
    wire.arrived(fin[2], fb.at[2 * x + 1 - c], cpeer)
    wire.arrived(fin[4], fb.at[2 * (1 - x) + 1 - c], cpeer)
    wire.arrived(fin[8], fa.at[pl.ds(other, plain)], cpeer)
    wire.arrived(fin[7], fa.at[pl.ds(pl.multiple_of(other + mine, 16), SHARE)], cpeer)
    wire.arrived(fin[9], fa.at[pl.ds(pl.multiple_of(other + theirs, 16), SHARE)], cpeer)
    wire.drain()


def reduce_grads(ga, gb, dx, sm):
    rows, cols = ga.shape[1:]
    half = rows // 2
    plain = half - 2 * SHARE
    toks = dx.shape[1]
    vmem = pl.BlockSpec(memory_space=pltpu.VMEM)
    b0, b1 = gb.shape[1:]
    V = pltpu.VMEM
    sv = lambda *lead: V(lead + sm.shape[1:], f32)
    slots = 64
    return pl.pallas_call(
        reduce_kernel,
        in_specs=[vmem] * 4, out_specs=[vmem] * 5,
        out_shape=[jax.ShapeDtypeStruct((rows, cols), bf), jax.ShapeDtypeStruct((4, b0, b1), bf),
                   jax.ShapeDtypeStruct((toks, cols), bf), jax.ShapeDtypeStruct((toks, cols), bf),
                   jax.ShapeDtypeStruct(sm.shape[1:], f32)],
        scratch_shapes=[V((4, 2, half, cols), bf), V((4, 2, SHARE, cols), bf), V((4, plain, cols), bf), V((4, SHARE, cols), bf),
                        V((4, plain, cols), bf), V((4, SHARE, cols), bf),
                        V((4, b0, b1), bf), V((4, b0, b1), bf), V((4, b0, b1), bf),
                        V((2, toks, cols), bf), V((2, toks, cols), bf),
                        sv(4), sv(4), sv(4), sv(), sv(), sv(), sv(), V((plain, cols), bf), V((plain, cols), bf),
                        pltpu.SemaphoreType.DMA((slots,)), pltpu.SemaphoreType.DMA((slots,))],
        compiler_params=pltpu.CompilerParams(collective_id=2, has_side_effects=True, vmem_limit_bytes=67043328),
        name="reduce_grads",
    )(ga.reshape((4, 2) + ga.shape[1:]), gb.reshape((4, 2) + gb.shape[1:]), dx.reshape((2, 2) + dx.shape[1:]), sm.reshape((4, 2) + sm.shape[1:]))


def mm(a, b, left, right):
    return lax.dot_general(a, b, (((left,), (right,)), ((), ())), preferred_element_type=f32)


def chunks(total, step, body):
    def run(i, _):
        body(pl.ds(pl.multiple_of(i * step, step), step))
        return 0
    lax.fori_loop(0, total // step, run, 0)


def ffn_kernel(n, r, step, mixed, tokens, cot, vec, big, out, dres, ga, dO, small,
               w_out, w_in, w_outer, stage, fb, gp, xh1, n1b, dh2, dm, du, acc, r1, lsem, gsem):
    toks, model = tokens.shape
    wide = w_in.shape[0]
    per = n // wide
    def outer_at(ref, j):
        if per:
            return ref.at[pl.ds(j * per, per), pl.ds((1 + wide) * r, wide * r)]
        return ref.at[:, pl.ds((1 + wide + j) * r, r)]
    loads = [pltpu.make_async_copy(big.at[:, pl.ds(0, r)], w_out, lsem.at[0])]
    for j in range(wide):
        loads.append(pltpu.make_async_copy(big.at[:, pl.ds((1 + j) * r, r)], w_in.at[j], lsem.at[1 + j]))
    for j in range(wide):
        loads.append(pltpu.make_async_copy(outer_at(big, j), w_outer.at[j], lsem.at[1 + wide + j]))
    for load in loads:
        load.start()
    stores = []

    def put(value_rows, place):
        k = len(stores)
        slot = k % stage.shape[0]
        if k >= stage.shape[0]:
            stores[k - stage.shape[0]].wait()
        def body(at):
            stage[slot, at, :] = value_rows(at).astype(bf)
        chunks(model, step, body)
        shape = place.shape
        store = pltpu.make_async_copy(stage.at[slot].reshape(shape), place, gsem.at[slot])
        store.start()
        stores.append(store)

    flat = lambda ref: ref.reshape(model, model)
    row = lambda i: vec[i:i + 1, :]
    b_output, b_outer, g1, s1, g2, s2 = [row(i) for i in (2, 3, 4, 5, 6, 7)]
    small[...] = jnp.zeros_like(small)
    loads[0].wait()
    wo = flat(w_out)

    def first(at):
        attn = mm(mixed[:, at], wo[...], 0, 0)
        z = tokens[at, :].astype(f32) + (attn + b_output)
        cen = z - jnp.mean(z, axis=-1, keepdims=True)
        inv = lax.rsqrt(jnp.mean(cen * cen, axis=-1, keepdims=True) + NORM_EPS)
        xh = cen * inv
        norm = xh * g1 + s1
        xh1[at, :] = xh
        n1b[at, :] = norm.astype(bf)
        r1[at, :] = jnp.broadcast_to(inv, (inv.shape[0], 128))
        acc[at, :] = norm + b_outer
    chunks(toks, step, first)
    for j in range(wide):
        loads[1 + j].wait()
        wi = flat(w_in.at[j])
        bias = row(8 + j)
        def inner(at, j=j, wi=wi, bias=bias):
            u = mm(n1b[at, :], wi[...], 1, 0) + bias
            cdf = 0.5 * (1.0 + lax.erf(u * (0.5 ** 0.5)))
            pdf = jnp.exp(-0.5 * u * u) * 0.3989422804014327
            fb[j, at, :] = (u * cdf).astype(bf)
            gp[j, at, :] = cdf + u * pdf
        chunks(toks, step, inner)
        loads[1 + wide + j].wait()
        wout = flat(w_outer.at[j])
        def outer(at, j=j, wout=wout):
            acc[at, :] += mm(fb[j, at, :], wout[...], 1, 0)
        chunks(toks, step, outer)

    def second(at):
        z = acc[at, :]
        cen = z - jnp.mean(z, axis=-1, keepdims=True)
        inv = lax.rsqrt(jnp.mean(cen * cen, axis=-1, keepdims=True) + NORM_EPS)
        xh = cen * inv
        out[at, :] = (xh * g2 + s2).astype(bf)
        g = cot[at, :].astype(f32)
        gx = g * xh
        gh = g * g2
        d = inv * (gh - jnp.mean(gh, axis=-1, keepdims=True) - xh * jnp.mean(gh * xh, axis=-1, keepdims=True))
        dh2[at, :] = d
        low = d.astype(bf)
        dm[at, :] = low
        small[6:7, :] += jnp.sum(gx, axis=0, keepdims=True)
        small[7:8, :] += jnp.sum(g, axis=0, keepdims=True)
        small[3:4, :] += jnp.sum(low.astype(f32), axis=0, keepdims=True)
    chunks(toks, step, second)
    for j in range(wide):
        wout = flat(w_outer.at[j])
        put(lambda at, j=j: mm(fb[j, :, at], dm[...], 0, 0), outer_at(ga, j))
        def dinner(at, j=j, wout=wout):
            low = (gp[j, at, :] * mm(dm[at, :], wout[...], 1, 1)).astype(bf)
            du[at, :] = low
            small[8 + j:9 + j, :] += jnp.sum(low.astype(f32), axis=0, keepdims=True)
        chunks(toks, step, dinner)
        wi = flat(w_in.at[j])
        def dfirst(at, wi=wi):
            dh2[at, :] += mm(du[at, :], wi[...], 1, 1)
        chunks(toks, step, dfirst)
        put(lambda at: mm(n1b[:, at], du[...], 0, 0), ga.at[:, pl.ds((1 + j) * r, r)])

    def last(at):
        d = dh2[at, :]
        xh = xh1[at, :]
        gh = d * g1
        inv = r1[at, 0:1]
        z = inv * (gh - jnp.mean(gh, axis=-1, keepdims=True) - xh * jnp.mean(gh * xh, axis=-1, keepdims=True))
        dres[at, :] = z
        low = z.astype(bf)
        dm[at, :] = low
        small[4:5, :] += jnp.sum(d * xh, axis=0, keepdims=True)
        small[5:6, :] += jnp.sum(d, axis=0, keepdims=True)
        small[2:3, :] += jnp.sum(low.astype(f32), axis=0, keepdims=True)
    chunks(toks, step, last)

    def back(at):
        dO[at, :] = mm(wo[at, :], dm[...], 1, 1).astype(bf)
    chunks(model, step, back)
    put(lambda at: mm(mixed[at, :], dm[...], 1, 0), ga.at[:, pl.ds(0, r)])
    for store in stores[-stage.shape[0]:]:
        store.wait()


def ffn_block(mixed, tokens, cot, vec, big, step=384):
    n, rows9, model = big.shape
    r = model // n
    wide = (rows9 // r - 1) // 2
    toks = tokens.shape[0]
    vmem = pl.BlockSpec(memory_space=pltpu.VMEM)
    hbm = pl.BlockSpec(memory_space=pl.ANY)
    per = n // wide
    ohold = (per, wide * r, model) if per else (n, r, model)
    V = pltpu.VMEM
    sq = lambda dt, *lead: V(lead + (toks, model), dt)
    return pl.pallas_call(
        functools.partial(ffn_kernel, n, r, step),
        in_specs=[vmem] * 4 + [hbm],
        out_specs=[vmem, vmem, hbm, vmem, vmem],
        out_shape=[jax.ShapeDtypeStruct((toks, model), bf), jax.ShapeDtypeStruct((toks, model), f32),
                   jax.ShapeDtypeStruct(big.shape, bf), jax.ShapeDtypeStruct((model, toks), bf),
                   jax.ShapeDtypeStruct((16, model), f32)],
        scratch_shapes=[V((n, r, model), bf), V((wide, n, r, model), bf), V((wide,) + ohold, bf), V((4, model, model), bf),
                        sq(bf, wide), sq(f32, wide), sq(f32), sq(bf), sq(f32), sq(bf), sq(bf), sq(f32),
                        V((toks, 128), f32), pltpu.SemaphoreType.DMA((1 + 2 * wide,)), pltpu.SemaphoreType.DMA((4,))],
        compiler_params=pltpu.CompilerParams(vmem_limit_bytes=67043328),
        cost_estimate=pl.CostEstimate(flops=2 * toks * model * model * (3 + 6 * wide), bytes_accessed=4 * big.size, transcendentals=2 * toks * model * wide),
        name="ffn_block",
    )(mixed, tokens, cot, vec, big)


def layer_norm(inputs, norm_gain, norm_bias):
    row_mean = jnp.mean(inputs, axis=-1, keepdims=True)
    centred = inputs - row_mean
    row_var = jnp.mean(centred * centred, axis=-1, keepdims=True)
    return centred * lax.rsqrt(row_var + NORM_EPS) * norm_gain + norm_bias


def gelu_exact(inputs):
    return jax.nn.gelu(inputs, approximate=False)


def contract(left_in, right_in, left_dim, right_dim):
    return lax.dot_general(
        left_in,
        right_in,
        (((left_dim,), (right_dim,)), ((), ())),
        preferred_element_type=jnp.float32,
    )


def chips_of_two_by_four():
    return lax.axis_size("wshard") == 8 and lax.axis_size("seq") == 4


def gather_parts(a, b, tokens):
    if chips_of_two_by_four():
        return gather_inputs(a, b, tokens)
    return lax.all_gather(a, "wshard"), lax.all_gather(b, "wshard"), lax.all_gather(tokens, "seq")


def reduce_parts(ga, gb, dx, sm):
    if chips_of_two_by_four():
        return reduce_grads(ga, gb, dx, sm)

    def scatter(part):
        return lax.psum_scatter(part, "wshard", scatter_dimension=0, tiled=False)

    fx = lax.psum_scatter(dx, "seq", scatter_dimension=0, tiled=False)
    return (
        lax.psum(scatter(ga), "seq"), lax.all_gather(scatter(gb), "seq"), fx, jnp.zeros_like(fx),
        lax.psum(scatter(sm), "seq"),
    )


def ffn_plain(mixed, tokens, cotangent, vec, big):
    shards_n, rows9, model = big.shape
    rows = model // shards_n
    wide = (rows9 // rows - 1) // 2
    bias_output, bias_outer, gain_one, shift_one, gain_two, shift_two = vec[2:8]
    bias_inner = vec[8:8 + wide].reshape(-1)
    output_full = big[:, :rows].reshape(model, model)
    inner_full = jnp.concatenate(
        [big[:, (1 + j) * rows:(2 + j) * rows].reshape(model, model) for j in range(wide)], axis=1
    )
    outer_full = big[:, (1 + wide) * rows:].reshape(-1, model)

    residual_in = tokens.astype(f32) + contract(mixed, output_full, 0, 0) + bias_output
    first_norm, first_back = jax.vjp(layer_norm, residual_in, gain_one, shift_one)
    first_low = first_norm.astype(bf)
    inner_act = jnp.dot(first_low, inner_full, preferred_element_type=f32) + bias_inner
    gelu_out, gelu_back = jax.vjp(gelu_exact, inner_act)
    gelu_low = gelu_out.astype(bf)
    second_in = first_norm + jnp.dot(gelu_low, outer_full, preferred_element_type=f32) + bias_outer
    layer_result, second_back = jax.vjp(layer_norm, second_in, gain_two, shift_two)
    d_second, grad_gain_two, grad_bias_two = second_back(cotangent.astype(f32))
    d_outer = d_second.astype(bf)
    grad_bias_outer = jnp.sum(d_outer.astype(f32), axis=0)
    grad_outer = contract(gelu_low, d_outer, 0, 0)
    (d_inner,) = gelu_back(contract(d_outer, outer_full, 1, 1))
    d_inner_low = d_inner.astype(bf)
    grad_bias_inner = jnp.sum(d_inner_low.astype(f32), axis=0)
    grad_inner = contract(first_low, d_inner_low, 0, 0)
    d_first = contract(d_inner_low, inner_full, 1, 1) + d_second
    d_resid, grad_gain_one, grad_bias_one = first_back(d_first)
    d_attn = d_resid.astype(bf)
    grad_bias_output = jnp.sum(d_attn.astype(f32), axis=0)
    grad_output = contract(mixed, d_attn, 1, 0)
    d_mixed = contract(output_full, d_attn, 1, 1).astype(bf)
    by_rows = lambda grad: grad.astype(bf).reshape(shards_n, -1, model)
    ga = jnp.concatenate(
        [by_rows(grad_output)] + [by_rows(grad_inner[:, j * model:(j + 1) * model]) for j in range(wide)]
        + [by_rows(grad_outer)], axis=1,
    )
    none = jnp.zeros((model,), f32)
    sums = jnp.concatenate([
        jnp.stack([none, none, grad_bias_output, grad_bias_outer, grad_gain_one, grad_bias_one, grad_gain_two, grad_bias_two]),
        grad_bias_inner.reshape(wide, model)], axis=0)
    return layer_result.astype(bf), d_resid, ga, d_mixed, sums


def shards(
    tokens, cotangent, starts,
    w_query, w_key, w_value, w_output, w_inner, w_outer,
    b_query, b_value, b_output, b_inner, b_outer,
    gain_first, bias_first, gain_second, bias_second,
):
    model = tokens.shape[1]
    rows = w_query.shape[0]
    shards_n = lax.axis_size("wshard")
    seq_n = lax.axis_size("seq")
    seq_i = lax.axis_index("seq")
    width = model // seq_n
    heads = width // HD
    wide = w_inner.shape[1] // model

    def own(columns):
        return lax.dynamic_slice_in_dim(columns, seq_i * width, width, columns.ndim - 1)

    smalls = (b_query, b_value, b_output, b_outer, gain_first, bias_first, gain_second, bias_second)
    small_cols = jnp.stack(smalls + tuple(b_inner.reshape(wide, rows)), axis=1)
    cols_n = small_cols.shape[1]
    a = jnp.concatenate(
        [w_output, w_inner.reshape(rows, wide, model).transpose(1, 0, 2).reshape(wide * rows, model), w_outer], axis=0
    )
    b = jnp.concatenate([own(w_query), own(w_key), own(w_value), jnp.pad(small_cols, ((0, 0), (0, HD - cols_n)))], axis=1)
    big, side, stream = gather_parts(a, b, tokens)
    stream = stream.reshape(-1, model)
    side = side.reshape(model, -1)
    w_own = side[:, :3 * width]
    vectors = side[:, 3 * width:3 * width + cols_n].astype(f32).T
    bias_query, bias_value = vectors[:2]
    bias_inner = vectors[8:].reshape(wide, shards_n, rows).transpose(1, 0, 2).reshape(-1)
    scale = HD ** -0.5
    qT = ((contract(w_own[:, :width], stream, 0, 1) + own(bias_query)[:, None]).astype(bf) * bf(scale))
    kT = contract(w_own[:, width:2 * width], stream, 0, 1).astype(bf)
    vT = (contract(w_own[:, 2 * width:], stream, 0, 1) + own(bias_value)[:, None]).astype(bf)

    def by_token(arr):
        return arr.reshape(heads, HD, -1).transpose(0, 2, 1)

    def by_feature(arr):
        return arr.transpose(0, 2, 1).reshape(width, -1)

    q3, k3, v3 = by_token(qT), by_token(kT), by_token(vT)
    oT, mixT, lse = attn_fwd(starts, qT, k3, vT, 512, 512)
    mixed = lax.all_to_all(mixT, "seq", split_axis=1, concat_axis=0, tiled=True)

    vec = jnp.concatenate([vectors[:8], bias_inner.reshape(wide, model), jnp.zeros((4, model), f32)], axis=0)
    feed = ffn_block if chips_of_two_by_four() else ffn_plain
    layer_result, d_resid, ga, d_mixed, sums = feed(mixed, tokens, cotangent, vec, big)
    doT = lax.all_to_all(d_mixed, "seq", split_axis=0, concat_axis=1, tiled=True)

    dqT, dk3, dv3 = attn_bwd(starts, qT, q3, k3, kT, v3, doT, by_token(doT), oT, lse, 256, 512)
    dT = jnp.concatenate([dqT, by_feature(dk3), by_feature(dv3)], axis=0)
    gb = contract(stream, dT, 0, 1).astype(bf).reshape(shards_n, rows, -1)
    dx = contract(dT, w_own, 0, 1).astype(bf).reshape(seq_n, -1, model)
    def spread(own_sum):
        return lax.dynamic_update_slice(jnp.zeros((model,), f32), own_sum, (seq_i * width,))

    small_rows = (
        spread(jnp.sum(dqT.astype(f32), axis=1)),
        spread(jnp.sum(dv3.astype(f32), axis=1).reshape(-1)),
        *sums[2:8],
    )
    sm = jnp.concatenate(
        [jnp.stack([row.reshape(shards_n, rows) for row in small_rows], axis=1),
         sums[8:8 + wide].reshape(shards_n, wide, rows)], axis=1,
    )
    sm = jnp.pad(sm, ((0, 0), (0, -cols_n % 8), (0, -rows % 128)))
    fa, fb, fx, fr, fs = reduce_parts(ga, gb, dx, sm)
    d_tokens = fx.astype(f32) + fr.astype(f32) + d_resid
    fb = fb.astype(f32)
    grads = [
        jnp.concatenate([fb[s, :, i * width:(i + 1) * width] for s in range(seq_n)], axis=1) for i in range(3)
    ]
    fa = fa.astype(f32)
    g_inner = jnp.concatenate([fa[(1 + j) * rows:(2 + j) * rows] for j in range(wide)], axis=1)
    tail = [fs[i, :rows] for i in range(8)]
    g_b_inner = fs[8:8 + wide, :rows].reshape(-1)
    return (
        layer_result, d_tokens, *grads,
        fa[:rows], g_inner, fa[(1 + wide) * rows:],
        tail[0], tail[1], tail[2], g_b_inner, *tail[3:],
    )


def solution(mesh):
    placed = (
        P(("wshard", "seq"), None),
        P(("wshard", "seq"), None),
        P("wshard", None),
        P("wshard", None),
        P("wshard", None),
        P("wshard", None),
        P("wshard", None),
        P("wshard", None),
        P("wshard", None),
        P("wshard"),
        P("wshard"),
        P("wshard"),
        P("wshard"),
        P("wshard"),
        P("wshard"),
        P("wshard"),
        P("wshard"),
        P("wshard"),
    )
    return jax.shard_map(
        shards,
        mesh=mesh,
        in_specs=placed,
        out_specs=(
            P(("wshard", "seq"), None),
            P(("wshard", "seq"), None),
            P("wshard", None),
            P("wshard", None),
            P("wshard", None),
            P("wshard", None),
            P("wshard", None),
            P("wshard", None),
            P("wshard"),
            P("wshard"),
            P("wshard"),
            P("wshard"),
            P("wshard"),
            P("wshard"),
            P("wshard"),
            P("wshard"),
            P("wshard"),
        ),
        check_vma=False,
    )
```

```python
import functools

import jax
import jax.numpy as jnp
from jax import lax
from jax.experimental import pallas as pl
from jax.experimental.pallas import tpu as pltpu
from jax.sharding import PartitionSpec as P

NORM_EPS = 1e-05
HD = 64
bf = jnp.bfloat16
f32 = jnp.float32


def doc_bounds(starts_ref, pos, total):
    lo = jnp.zeros_like(pos); hi = jnp.full_like(pos, total)
    for d in range(starts_ref.shape[1]):
        s = starts_ref[0, d]
        lo = jnp.where(s <= pos, jnp.maximum(lo, s), lo)
        hi = jnp.where(s > pos, jnp.minimum(hi, s), hi)
    return lo, hi

def dot(a, b):
    return lax.dot_general(a, b, (((1,), (0,)), ((), ())), preferred_element_type=f32)

def fwd_kernel(heads, bq, bk, starts, qT, k3, vT, oT, mixT, lse, acc, ml):
    total = k3.shape[1]
    i = pl.program_id(0)
    q0 = i * bq
    first, _ = doc_bounds(starts, jnp.int32(q0), total)
    _, last = doc_bounds(starts, jnp.int32(q0 + bq - 1), total)
    pos = q0 + lax.broadcasted_iota(jnp.int32, (1, bq), 1)
    lo, hi = doc_bounds(starts, pos, total)
    kb0 = first // bk
    kb1 = (last + bk - 1) // bk
    acc[...] = jnp.zeros_like(acc)
    ml[0] = jnp.full((heads, bq), -1e30, f32)
    ml[1] = jnp.zeros((heads, bq), f32)
    kio = lax.broadcasted_iota(jnp.int32, (bk, bq), 0)
    def body(j, _):
        ks = pl.multiple_of(j * bk, bk)
        mask = (kio >= lo - ks) & (kio < hi - ks)
        for h in range(heads):
            s = dot(k3[h, pl.ds(ks, bk), :], qT[HD * h:HD * (h + 1), :])
            s = jnp.where(mask, s, -1e30)
            m_old = ml[0, h:h + 1]
            m = jnp.maximum(m_old, jnp.max(s, axis=0, keepdims=True))
            p = jnp.exp(s - m)
            al = jnp.exp(m_old - m)
            ml[0, h:h + 1] = m
            ml[1, h:h + 1] = ml[1, h:h + 1] * al + jnp.sum(p, axis=0, keepdims=True)
            sl = slice(HD * h, HD * (h + 1))
            acc[sl, :] = acc[sl, :] * al + dot(vT[sl, pl.ds(ks, bk)], p.astype(bf))
        return 0
    lax.fori_loop(kb0, kb1, body, 0)
    for h in range(heads):
        sl = slice(HD * h, HD * (h + 1))
        l = ml[1, h:h + 1]
        o = acc[sl, :] / l
        oT[sl, :] = o
        mixT[sl, :] = o.astype(bf)
        lse[h:h + 1, :] = ml[0, h:h + 1] + jnp.log(l)

def attn_fwd(starts, qT, k3, vT, bq=256, bk=256):
    heads, total, _ = k3.shape
    full2 = lambda i: (0, 0)
    return pl.pallas_call(
        functools.partial(fwd_kernel, heads, bq, bk),
        grid=(total // bq,),
        in_specs=[pl.BlockSpec(memory_space=pltpu.SMEM),
                  pl.BlockSpec((heads * HD, bq), lambda i: (0, i)),
                  pl.BlockSpec(k3.shape, lambda i: (0, 0, 0)),
                  pl.BlockSpec(vT.shape, full2)],
        out_specs=[pl.BlockSpec((heads * HD, bq), lambda i: (0, i)),
                   pl.BlockSpec((heads * HD, bq), lambda i: (0, i)),
                   pl.BlockSpec((heads, bq), lambda i: (0, i))],
        out_shape=[jax.ShapeDtypeStruct((heads * HD, total), f32),
                   jax.ShapeDtypeStruct((heads * HD, total), bf),
                   jax.ShapeDtypeStruct((heads, total), f32)],
        scratch_shapes=[pltpu.VMEM((heads * HD, bq), f32), pltpu.VMEM((2, heads, bq), f32)],
        cost_estimate=pl.CostEstimate(flops=8 * heads * HD * total * total, bytes_accessed=8 * heads * HD * total, transcendentals=0),
        name="attn_fwd",
    )(starts, qT, k3, vT)

def bwd_kernel(heads, bq, bk, starts, qT, q3, k3, kT, v3, doT, do3, oT, lse, dqT, dk3, dv3, delta, dqa, dka, dva):
    total = q3.shape[1]
    i = pl.program_id(0)
    k0 = i * bk
    @pl.when(i == 0)
    def _():
        dqa[...] = jnp.zeros_like(dqa)
        for h in range(heads):
            sl = slice(HD * h, HD * (h + 1))
            delta[h:h + 1, :] = jnp.sum(doT[sl, :].astype(f32) * oT[sl, :], axis=0, keepdims=True)
    first, _ = doc_bounds(starts, jnp.int32(k0), total)
    _, last = doc_bounds(starts, jnp.int32(k0 + bk - 1), total)
    qb0 = first // bq
    qb1 = (last + bq - 1) // bq
    dka[...] = jnp.zeros_like(dka)
    dva[...] = jnp.zeros_like(dva)
    kio = k0 + lax.broadcasted_iota(jnp.int32, (bk, bq), 0)
    def body(j, _):
        qs = pl.multiple_of(j * bq, bq)
        pos = qs + lax.broadcasted_iota(jnp.int32, (1, bq), 1)
        lo, hi = doc_bounds(starts, pos, total)
        mask = (kio >= lo) & (kio < hi)
        for h in range(heads):
            sl = slice(HD * h, HD * (h + 1))
            s = dot(k3[h, :, :], qT[sl, pl.ds(qs, bq)])
            p = jnp.exp(jnp.where(mask, s - lse[h:h + 1, pl.ds(qs, bq)], -1e30))
            dp = dot(v3[h, :, :], doT[sl, pl.ds(qs, bq)])
            ds = p * (dp - delta[h:h + 1, pl.ds(qs, bq)])
            dsb = ds.astype(bf)
            dva[h] += dot(p.astype(bf), do3[h, pl.ds(qs, bq), :])
            dka[h] += dot(dsb, q3[h, pl.ds(qs, bq), :])
            dqa[sl, pl.ds(qs, bq)] += dot(kT[sl, :], dsb)
        return 0
    lax.fori_loop(qb0, qb1, body, 0)
    dk3[...] = dka[...].astype(bf)
    dv3[...] = dva[...].astype(bf)
    @pl.when(i == pl.num_programs(0) - 1)
    def _():
        dqT[...] = (dqa[...] * (HD ** -0.5)).astype(bf)

def attn_bwd(starts, qT, q3, k3, kT, v3, doT, do3, oT, lse, bq=256, bk=256):
    heads, total, _ = k3.shape
    full = lambda a: pl.BlockSpec(a.shape, lambda i: (0,) * a.ndim)
    kb3 = pl.BlockSpec((heads, bk, HD), lambda i: (0, i, 0))
    return pl.pallas_call(
        functools.partial(bwd_kernel, heads, bq, bk),
        grid=(total // bk,),
        in_specs=[pl.BlockSpec(memory_space=pltpu.SMEM), full(qT), full(q3), kb3,
                  pl.BlockSpec((heads * HD, bk), lambda i: (0, i)), kb3, full(doT), full(do3), full(oT), full(lse)],
        out_specs=[full(qT), kb3, kb3],
        out_shape=[jax.ShapeDtypeStruct(qT.shape, bf), jax.ShapeDtypeStruct(k3.shape, bf), jax.ShapeDtypeStruct(k3.shape, bf)],
        scratch_shapes=[pltpu.VMEM((heads, total), f32), pltpu.VMEM(qT.shape, f32),
                        pltpu.VMEM((heads, bk, HD), f32), pltpu.VMEM((heads, bk, HD), f32)],
        name="attn_bwd",
    )(starts, qT, q3, k3, kT, v3, doT, do3, oT, lse)


MESH = pl.DeviceIdType.MESH


class Wire:
    def __init__(self, send, recv):
        self.send, self.recv, self.used, self.open = send, recv, 0, []

    def slot(self):
        self.used += 1
        return self.used - 1

    def start(self, slot, src, dst, device):
        copy = pltpu.make_async_remote_copy(
            src_ref=src, dst_ref=dst, send_sem=self.send.at[slot], recv_sem=self.recv.at[slot],
            device_id=device, device_id_type=MESH,
        )
        copy.start()
        self.open.append(copy)

    def arrived(self, slot, dst, device):
        pltpu.make_async_remote_copy(
            src_ref=dst, dst_ref=dst, send_sem=self.send.at[slot], recv_sem=self.recv.at[slot],
            device_id=device, device_id_type=MESH,
        ).wait_recv()

    def drain(self):
        for copy in self.open:
            copy.wait_send()
        self.open = []


def grid_peers():
    shard, seq = lax.axis_index("wshard"), lax.axis_index("seq")
    z, y = shard // 2, shard % 2
    x, c = seq // 2, seq % 2
    at = lambda zz, yy, xx, cc: (zz * 2 + yy, xx * 2 + cc)
    along = [at((z + d) % 4, y, x, c) for d in range(4)]
    return z, y, x, c, along, at(z, 1 - y, x, c), at(z, y, 1 - x, c), at(z, y, x, 1 - c)


def greet(peers):
    barrier = pltpu.get_barrier_semaphore()
    for peer in peers:
        pl.semaphore_signal(barrier, inc=1, device_id=peer, device_id_type=MESH)
    pl.semaphore_wait(barrier, len(peers))


ORDER = (1, 3, 2)
SHARE = 80


def gather_kernel(b_ref, t_ref, q_ref, x_ref, send, recv, lsem):
    z, y, x, c, along, ypeer, xpeer, cpeer = grid_peers()
    own = z * 2 + y
    wire = Wire(send, recv)
    spot = lambda r, d: ((z + 4 - d) % 4) * 2 + (y if r == 0 else 1 - y)
    seq = x * 2 + c
    half = t_ref.shape[0] // 2
    parts = [pl.ds(0, half), pl.ds(half, half)]
    locals_ = [
        pltpu.make_async_copy(b_ref, q_ref.at[own], lsem.at[0]),
        pltpu.make_async_copy(t_ref, x_ref.at[seq], lsem.at[1]),
    ]
    for copy in locals_:
        copy.start()
    greet(along[1:] + [ypeer, xpeer, cpeer])
    zB = [wire.slot() for _ in range(4)]
    yB = [wire.slot() for _ in range(4)]
    tx, tc1 = [wire.slot() for _ in parts], [wire.slot() for _ in parts]
    tc0 = wire.slot()
    for slot, part in zip(tx, parts):
        wire.start(slot, t_ref.at[part], x_ref.at[seq, part], xpeer)
    for d in ORDER:
        wire.start(zB[d], b_ref, q_ref.at[own], along[d])
    wire.start(yB[0], b_ref, q_ref.at[own], ypeer)
    wire.start(tc0, t_ref, x_ref.at[seq], cpeer)
    for d in ORDER:
        w = spot(0, d)
        wire.arrived(zB[d], q_ref.at[w], along[d])
        wire.start(yB[d], q_ref.at[w], q_ref.at[w], ypeer)
    xtok = (1 - x) * 2 + c
    for i, part in enumerate(parts):
        wire.arrived(tx[i], x_ref.at[xtok, part], xpeer)
        wire.start(tc1[i], x_ref.at[xtok, part], x_ref.at[xtok, part], cpeer)
    for d in (0,) + ORDER:
        wire.arrived(yB[d], q_ref.at[spot(1, d)], ypeer)
    wire.arrived(tc0, x_ref.at[x * 2 + 1 - c], cpeer)
    for i, part in enumerate(parts):
        wire.arrived(tc1[i], x_ref.at[(1 - x) * 2 + 1 - c, part], cpeer)
    wire.drain()
    for copy in locals_:
        copy.wait()


def gather_inputs(b, tokens):
    slots = 13
    hbm = pl.BlockSpec(memory_space=pl.ANY)
    vmem = pl.BlockSpec(memory_space=pltpu.VMEM)
    return pl.pallas_call(
        gather_kernel,
        in_specs=[vmem] * 2, out_specs=[hbm] * 2,
        out_shape=[jax.ShapeDtypeStruct((8,) + b.shape, b.dtype), jax.ShapeDtypeStruct((4,) + tokens.shape, tokens.dtype)],
        scratch_shapes=[pltpu.SemaphoreType.DMA((slots,)), pltpu.SemaphoreType.DMA((slots,)), pltpu.SemaphoreType.DMA((2,))],
        compiler_params=pltpu.CompilerParams(collective_id=1, has_side_effects=True),
        name="gather_inputs",
    )(b, tokens)


def add_rows(dst, parts, rows, step=16):
    def body(i, _):
        at = pl.ds(pl.multiple_of(i * step, step), step)
        total = parts[0][at, :].astype(f32)
        for part in parts[1:]:
            total = total + part[at, :].astype(f32)
        dst[at, :] = total.astype(dst.dtype)
        return 0
    lax.fori_loop(0, rows // step, body, 0)


ALL = ORDER + (0,)


def reduce_kernel(ga, gb, dx, sm, fa, fb, fx, fr, fs, rc, rd, ry, ryd, rz, rzd, hb, ryb, rzb, hx, rxc,
                  hs, rys, rzs, s1, s2, s3, s4, fn, rn, send, recv):
    z, y, x, c, along, ypeer, xpeer, cpeer = grid_peers()
    half = ga.shape[2] // 2
    plain = half - 2 * SHARE
    base, other = pl.multiple_of(half * c, 16), pl.multiple_of(half * (1 - c), 16)
    mine, theirs = pl.multiple_of(plain + SHARE * x, 16), pl.multiple_of(plain + SHARE * (1 - x), 16)
    nrow = pl.ds(0, plain)
    wire = Wire(send, recv)
    new4 = lambda: [wire.slot() for _ in range(4)]
    kc = [new4(), new4()]
    kcx, kx, kxd = new4(), wire.slot(), new4()
    kyn, kyd, kyb, kys = new4(), new4(), wire.slot(), wire.slot()
    kzn, kzd, kzb, kzs = new4(), new4(), new4(), new4()
    fin = [wire.slot() for _ in range(13)]
    zz = lambda d: (z + d) % 4
    greet(along[1:] + [ypeer, xpeer, cpeer])
    wire.start(kys, sm.at[:, 1 - y], rys, ypeer)
    wire.start(kyb, gb.at[:, 1 - y], ryb, ypeer)
    for i, d in enumerate(ALL):
        for r in (1, 0):
            yy = y if r == 0 else 1 - y
            wire.start(kc[r][d], ga.at[zz(d), yy, pl.ds(other, half)], rc.at[zz(d), yy], cpeer)
        if i == 0:
            for t in range(2):
                wire.start(kcx[t], dx.at[t, 1 - c], rxc.at[t], cpeer)
    for d in ALL:
        for r in (1, 0):
            yy = y if r == 0 else 1 - y
            blk = rc.at[zz(d), yy]
            wire.arrived(kc[r][d], blk, cpeer)
            add_rows(blk, [ga.at[zz(d), yy, pl.ds(base, half)], blk], half)
        wire.start(kxd[d], rc.at[zz(d), :, pl.ds(theirs, SHARE)], rd.at[zz(d)], xpeer)
        wire.start(kyn[d], rc.at[zz(d), 1 - y, nrow], ry.at[zz(d)], ypeer)
    for t in range(2):
        wire.arrived(kcx[t], rxc.at[t], cpeer)
        add_rows(hx.at[t], [dx.at[t, c], rxc.at[t]], hx.shape[1])
    wire.start(kx, hx.at[1 - x], fr, xpeer)
    wire.arrived(kys, rys, ypeer)
    wire.arrived(kyb, ryb, ypeer)
    for d in ALL:
        hs[d] = sm[zz(d), y] + rys[zz(d)]
        add_rows(hb.at[d], [gb.at[zz(d), y], ryb.at[zz(d)]], hb.shape[1])
        if d:
            wire.start(kzs[d], hs.at[d], rzs.at[d], along[d])
            wire.start(kzb[d], hb.at[d], rzb.at[d], along[d])
    for d in ALL:
        wire.arrived(kxd[d], rd.at[zz(d)], xpeer)
        for yy in range(2):
            spot = rc.at[zz(d), yy, pl.ds(mine, SHARE)]
            add_rows(spot, [spot, rd.at[zz(d), yy]], SHARE)
        wire.start(kyd[d], rc.at[zz(d), 1 - y, pl.ds(mine, SHARE)], ryd.at[zz(d)], ypeer)
    for d in ALL:
        wire.arrived(kyn[d], ry.at[zz(d)], ypeer)
        spot = rc.at[zz(d), y, nrow]
        add_rows(spot, [spot, ry.at[zz(d)]], plain)
        if d:
            wire.start(kzn[d], spot, rz.at[d], along[d])
    for d in ALL:
        wire.arrived(kyd[d], ryd.at[zz(d)], ypeer)
        spot = rc.at[zz(d), y, pl.ds(mine, SHARE)]
        add_rows(spot, [spot, ryd.at[zz(d)]], SHARE)
        if d:
            wire.start(kzd[d], spot, rzd.at[d], along[d])
    for d in ORDER:
        wire.arrived(kzs[d], rzs.at[d], along[d])
        wire.arrived(kzb[d], rzb.at[d], along[d])
    s1[...] = hs[0] + rzs[1] + rzs[2] + rzs[3]
    wire.start(fin[0], s1, s2, xpeer)
    seq, xseq = 2 * x + c, 2 * (1 - x) + c
    add_rows(fb.at[seq], [hb.at[0]] + [rzb.at[d] for d in ORDER], hb.shape[1])
    wire.start(fin[1], fb.at[seq], fb.at[seq], xpeer)
    wire.start(fin[2], fb.at[seq], fb.at[seq], cpeer)
    wire.arrived(fin[0], s2, xpeer)
    s3[...] = s1[...] + s2[...]
    wire.start(fin[3], s3, s4, cpeer)
    wire.arrived(fin[1], fb.at[xseq], xpeer)
    wire.start(fin[4], fb.at[xseq], fb.at[xseq], cpeer)
    for d in ORDER:
        wire.arrived(kzn[d], rz.at[d], along[d])
    add_rows(fn, [rc.at[z, y, nrow]] + [rz.at[d] for d in ORDER], plain)
    wire.start(fin[5], fn, rn, xpeer)
    for d in ORDER:
        wire.arrived(kzd[d], rzd.at[d], along[d])
    dmine = pl.ds(pl.multiple_of(base + mine, 16), SHARE)
    dtheirs = pl.ds(pl.multiple_of(base + theirs, 16), SHARE)
    add_rows(fa.at[dmine], [rc.at[z, y, pl.ds(mine, SHARE)]] + [rzd.at[d] for d in ORDER], SHARE)
    wire.start(fin[6], fa.at[dmine], fa.at[dmine], xpeer)
    wire.start(fin[7], fa.at[dmine], fa.at[dmine], cpeer)
    wire.arrived(fin[5], rn, xpeer)
    nspan = pl.ds(base, plain)
    add_rows(fa.at[nspan], [fn, rn], plain)
    wire.start(fin[8], fa.at[nspan], fa.at[nspan], cpeer)
    wire.arrived(fin[6], fa.at[dtheirs], xpeer)
    wire.start(fin[9], fa.at[dtheirs], fa.at[dtheirs], cpeer)
    wire.arrived(kx, fr, xpeer)
    fx[...] = hx[x]
    wire.arrived(fin[3], s4, cpeer)
    fs[...] = s3[...] + s4[...]
    wire.arrived(fin[2], fb.at[2 * x + 1 - c], cpeer)
    wire.arrived(fin[4], fb.at[2 * (1 - x) + 1 - c], cpeer)
    wire.arrived(fin[8], fa.at[pl.ds(other, plain)], cpeer)
    wire.arrived(fin[7], fa.at[pl.ds(pl.multiple_of(other + mine, 16), SHARE)], cpeer)
    wire.arrived(fin[9], fa.at[pl.ds(pl.multiple_of(other + theirs, 16), SHARE)], cpeer)
    wire.drain()


def reduce_grads(ga, gb, dx, sm):
    rows, cols = ga.shape[1:]
    half = rows // 2
    plain = half - 2 * SHARE
    toks = dx.shape[1]
    vmem = pl.BlockSpec(memory_space=pltpu.VMEM)
    b0, b1 = gb.shape[1:]
    V = pltpu.VMEM
    sv = lambda *lead: V(lead + sm.shape[1:], f32)
    slots = 64
    return pl.pallas_call(
        reduce_kernel,
        in_specs=[vmem] * 4, out_specs=[vmem] * 5,
        out_shape=[jax.ShapeDtypeStruct((rows, cols), bf), jax.ShapeDtypeStruct((4, b0, b1), bf),
                   jax.ShapeDtypeStruct((toks, cols), bf), jax.ShapeDtypeStruct((toks, cols), bf),
                   jax.ShapeDtypeStruct(sm.shape[1:], f32)],
        scratch_shapes=[V((4, 2, half, cols), bf), V((4, 2, SHARE, cols), bf), V((4, plain, cols), bf), V((4, SHARE, cols), bf),
                        V((4, plain, cols), bf), V((4, SHARE, cols), bf),
                        V((4, b0, b1), bf), V((4, b0, b1), bf), V((4, b0, b1), bf),
                        V((2, toks, cols), bf), V((2, toks, cols), bf),
                        sv(4), sv(4), sv(4), sv(), sv(), sv(), sv(), V((plain, cols), bf), V((plain, cols), bf),
                        pltpu.SemaphoreType.DMA((slots,)), pltpu.SemaphoreType.DMA((slots,))],
        compiler_params=pltpu.CompilerParams(collective_id=2, has_side_effects=True, vmem_limit_bytes=67043328),
        name="reduce_grads",
    )(ga.reshape((4, 2) + ga.shape[1:]), gb.reshape((4, 2) + gb.shape[1:]), dx.reshape((2, 2) + dx.shape[1:]), sm.reshape((4, 2) + sm.shape[1:]))


def mm(a, b, left, right):
    return lax.dot_general(a, b, (((left,), (right,)), ((), ())), preferred_element_type=f32)


def chunks(total, step, body):
    def run(i, _):
        body(pl.ds(pl.multiple_of(i * step, step), step))
        return 0
    lax.fori_loop(0, total // step, run, 0)


def ffn_kernel(n, r, step, mixed, tokens, cot, vec, big, out, dres, ga, dO, small,
               w_out, w_in, w_outer, stage, fb, gp, xh1, n1b, dh2, dm, du, acc, r1, lsem, gsem, send, recv):
    toks, model = tokens.shape
    wide = w_in.shape[0]
    per = n // wide
    def outer_at(ref, j):
        if per:
            return ref.at[pl.ds(j * per, per), pl.ds((1 + wide) * r, wide * r)]
        return ref.at[:, pl.ds((1 + wide + j) * r, r)]
    z, y, x, c, along, ypeer, xpeer, cpeer = grid_peers()
    wire = Wire(send, recv)
    greet([cpeer])
    h = r // 2
    low = lambda size, side: pl.ds(pl.multiple_of(size * side, 16), size)
    def place(s, side, k):
        if k == 0:
            return w_out.at[s, low(h, side)]
        if k <= wide:
            return w_in.at[k - 1, s, low(h, side)]
        return w_outer.at[s // per, s % per, low(wide * h, side)]
    loads = [[] for _ in range(2 + wide)]
    for k in range(2 + wide):
        span = pl.ds(k * h, h if k <= wide else wide * h)
        for s in range(n):
            slot = wire.slot()
            load = pltpu.make_async_copy(big.at[s, span], place(s, c, k), lsem.at[slot])
            load.start()
            wire.start(slot, big.at[s, span], place(s, c, k), cpeer)
            loads[k].append((load, slot, place(s, 1 - c, k)))

    def ready(k):
        for load, slot, spot in loads[k]:
            load.wait()
            wire.arrived(slot, spot, cpeer)

    stores = []

    def put(value_rows, place):
        k = len(stores)
        slot = k % stage.shape[0]
        if k >= stage.shape[0]:
            stores[k - stage.shape[0]].wait()
        def body(at):
            stage[slot, at, :] = value_rows(at).astype(bf)
        chunks(model, step, body)
        shape = place.shape
        store = pltpu.make_async_copy(stage.at[slot].reshape(shape), place, gsem.at[slot])
        store.start()
        stores.append(store)

    flat = lambda ref: ref.reshape(model, model)
    row = lambda i: vec[i:i + 1, :]
    b_output, b_outer, g1, s1, g2, s2 = [row(i) for i in (2, 3, 4, 5, 6, 7)]
    small[...] = jnp.zeros_like(small)
    ready(0)
    wo = flat(w_out)

    def first(at):
        attn = mm(mixed[:, at], wo[...], 0, 0)
        z = tokens[at, :].astype(f32) + (attn + b_output)
        cen = z - jnp.mean(z, axis=-1, keepdims=True)
        inv = lax.rsqrt(jnp.mean(cen * cen, axis=-1, keepdims=True) + NORM_EPS)
        xh = cen * inv
        norm = xh * g1 + s1
        xh1[at, :] = xh
        n1b[at, :] = norm.astype(bf)
        r1[at, :] = jnp.broadcast_to(inv, (inv.shape[0], 128))
        acc[at, :] = norm + b_outer
    chunks(toks, step, first)
    for j in range(wide):
        ready(1 + j)
        wi = flat(w_in.at[j])
        bias = row(8 + j)
        def inner(at, j=j, wi=wi, bias=bias):
            u = mm(n1b[at, :], wi[...], 1, 0) + bias
            cdf = 0.5 * (1.0 + lax.erf(u * (0.5 ** 0.5)))
            pdf = jnp.exp(-0.5 * u * u) * 0.3989422804014327
            fb[j, at, :] = (u * cdf).astype(bf)
            gp[j, at, :] = cdf + u * pdf
        chunks(toks, step, inner)
    ready(1 + wide)
    for j in range(wide):
        wout = flat(w_outer.at[j])
        def outer(at, j=j, wout=wout):
            acc[at, :] += mm(fb[j, at, :], wout[...], 1, 0)
        chunks(toks, step, outer)

    def second(at):
        z = acc[at, :]
        cen = z - jnp.mean(z, axis=-1, keepdims=True)
        inv = lax.rsqrt(jnp.mean(cen * cen, axis=-1, keepdims=True) + NORM_EPS)
        xh = cen * inv
        out[at, :] = (xh * g2 + s2).astype(bf)
        g = cot[at, :].astype(f32)
        gx = g * xh
        gh = g * g2
        d = inv * (gh - jnp.mean(gh, axis=-1, keepdims=True) - xh * jnp.mean(gh * xh, axis=-1, keepdims=True))
        dh2[at, :] = d
        low = d.astype(bf)
        dm[at, :] = low
        small[6:7, :] += jnp.sum(gx, axis=0, keepdims=True)
        small[7:8, :] += jnp.sum(g, axis=0, keepdims=True)
        small[3:4, :] += jnp.sum(low.astype(f32), axis=0, keepdims=True)
    chunks(toks, step, second)
    for j in range(wide):
        wout = flat(w_outer.at[j])
        put(lambda at, j=j: mm(fb[j, :, at], dm[...], 0, 0), outer_at(ga, j))
        def dinner(at, j=j, wout=wout):
            low = (gp[j, at, :] * mm(dm[at, :], wout[...], 1, 1)).astype(bf)
            du[at, :] = low
            small[8 + j:9 + j, :] += jnp.sum(low.astype(f32), axis=0, keepdims=True)
        chunks(toks, step, dinner)
        wi = flat(w_in.at[j])
        def dfirst(at, wi=wi):
            dh2[at, :] += mm(du[at, :], wi[...], 1, 1)
        chunks(toks, step, dfirst)
        put(lambda at: mm(n1b[:, at], du[...], 0, 0), ga.at[:, pl.ds((1 + j) * r, r)])

    def last(at):
        d = dh2[at, :]
        xh = xh1[at, :]
        gh = d * g1
        inv = r1[at, 0:1]
        z = inv * (gh - jnp.mean(gh, axis=-1, keepdims=True) - xh * jnp.mean(gh * xh, axis=-1, keepdims=True))
        dres[at, :] = z
        low = z.astype(bf)
        dm[at, :] = low
        small[4:5, :] += jnp.sum(d * xh, axis=0, keepdims=True)
        small[5:6, :] += jnp.sum(d, axis=0, keepdims=True)
        small[2:3, :] += jnp.sum(low.astype(f32), axis=0, keepdims=True)
    chunks(toks, step, last)

    def back(at):
        dO[at, :] = mm(wo[at, :], dm[...], 1, 1).astype(bf)
    chunks(model, step, back)
    put(lambda at: mm(mixed[at, :], dm[...], 1, 0), ga.at[:, pl.ds(0, r)])
    for store in stores[-stage.shape[0]:]:
        store.wait()
    wire.drain()


def ffn_block(mixed, tokens, cot, vec, big, step=384):
    n, half, model = big.shape
    r = model // n
    wide = (2 * half // r - 1) // 2
    toks = tokens.shape[0]
    vmem = pl.BlockSpec(memory_space=pltpu.VMEM)
    hbm = pl.BlockSpec(memory_space=pl.ANY)
    per = n // wide
    ohold = (per, wide * r, model) if per else (n, r, model)
    V = pltpu.VMEM
    sq = lambda dt, *lead: V(lead + (toks, model), dt)
    return pl.pallas_call(
        functools.partial(ffn_kernel, n, r, step),
        in_specs=[vmem] * 4 + [hbm],
        out_specs=[vmem, vmem, hbm, vmem, vmem],
        out_shape=[jax.ShapeDtypeStruct((toks, model), bf), jax.ShapeDtypeStruct((toks, model), f32),
                   jax.ShapeDtypeStruct((n, 2 * half, model), bf), jax.ShapeDtypeStruct((model, toks), bf),
                   jax.ShapeDtypeStruct((16, model), f32)],
        scratch_shapes=[V((n, r, model), bf), V((wide, n, r, model), bf), V((wide,) + ohold, bf), V((4, model, model), bf),
                        sq(bf, wide), sq(f32, wide), sq(f32), sq(bf), sq(f32), sq(bf), sq(bf), sq(f32),
                        V((toks, 128), f32), pltpu.SemaphoreType.DMA(((2 + wide) * n,)), pltpu.SemaphoreType.DMA((4,)),
                        pltpu.SemaphoreType.DMA(((2 + wide) * n,)), pltpu.SemaphoreType.DMA(((2 + wide) * n,))],
        compiler_params=pltpu.CompilerParams(collective_id=3, has_side_effects=True, vmem_limit_bytes=67043328),
        cost_estimate=pl.CostEstimate(flops=2 * toks * model * model * (3 + 6 * wide), bytes_accessed=8 * n * half * model, transcendentals=2 * toks * model * wide),
        name="ffn_block",
    )(mixed, tokens, cot, vec, big)


def layer_norm(inputs, norm_gain, norm_bias):
    row_mean = jnp.mean(inputs, axis=-1, keepdims=True)
    centred = inputs - row_mean
    row_var = jnp.mean(centred * centred, axis=-1, keepdims=True)
    return centred * lax.rsqrt(row_var + NORM_EPS) * norm_gain + norm_bias


def gelu_exact(inputs):
    return jax.nn.gelu(inputs, approximate=False)


def contract(left_in, right_in, left_dim, right_dim):
    return lax.dot_general(
        left_in,
        right_in,
        (((left_dim,), (right_dim,)), ((), ())),
        preferred_element_type=jnp.float32,
    )


def chips_of_two_by_four():
    return lax.axis_size("wshard") == 8 and lax.axis_size("seq") == 4


def reduce_parts(ga, gb, dx, sm):
    if chips_of_two_by_four():
        return reduce_grads(ga, gb, dx, sm)

    def scatter(part):
        return lax.psum_scatter(part, "wshard", scatter_dimension=0, tiled=False)

    fx = lax.psum_scatter(dx, "seq", scatter_dimension=0, tiled=False)
    return (
        lax.psum(scatter(ga), "seq"), lax.all_gather(scatter(gb), "seq"), fx, jnp.zeros_like(fx),
        lax.psum(scatter(sm), "seq"),
    )


def ffn_plain(mixed, tokens, cotangent, vec, big):
    shards_n, rows9, model = big.shape
    rows = model // shards_n
    wide = (rows9 // rows - 1) // 2
    bias_output, bias_outer, gain_one, shift_one, gain_two, shift_two = vec[2:8]
    bias_inner = vec[8:8 + wide].reshape(-1)
    output_full = big[:, :rows].reshape(model, model)
    inner_full = jnp.concatenate(
        [big[:, (1 + j) * rows:(2 + j) * rows].reshape(model, model) for j in range(wide)], axis=1
    )
    outer_full = big[:, (1 + wide) * rows:].reshape(-1, model)

    residual_in = tokens.astype(f32) + contract(mixed, output_full, 0, 0) + bias_output
    first_norm, first_back = jax.vjp(layer_norm, residual_in, gain_one, shift_one)
    first_low = first_norm.astype(bf)
    inner_act = jnp.dot(first_low, inner_full, preferred_element_type=f32) + bias_inner
    gelu_out, gelu_back = jax.vjp(gelu_exact, inner_act)
    gelu_low = gelu_out.astype(bf)
    second_in = first_norm + jnp.dot(gelu_low, outer_full, preferred_element_type=f32) + bias_outer
    layer_result, second_back = jax.vjp(layer_norm, second_in, gain_two, shift_two)
    d_second, grad_gain_two, grad_bias_two = second_back(cotangent.astype(f32))
    d_outer = d_second.astype(bf)
    grad_bias_outer = jnp.sum(d_outer.astype(f32), axis=0)
    grad_outer = contract(gelu_low, d_outer, 0, 0)
    (d_inner,) = gelu_back(contract(d_outer, outer_full, 1, 1))
    d_inner_low = d_inner.astype(bf)
    grad_bias_inner = jnp.sum(d_inner_low.astype(f32), axis=0)
    grad_inner = contract(first_low, d_inner_low, 0, 0)
    d_first = contract(d_inner_low, inner_full, 1, 1) + d_second
    d_resid, grad_gain_one, grad_bias_one = first_back(d_first)
    d_attn = d_resid.astype(bf)
    grad_bias_output = jnp.sum(d_attn.astype(f32), axis=0)
    grad_output = contract(mixed, d_attn, 1, 0)
    d_mixed = contract(output_full, d_attn, 1, 1).astype(bf)
    by_rows = lambda grad: grad.astype(bf).reshape(shards_n, -1, model)
    ga = jnp.concatenate(
        [by_rows(grad_output)] + [by_rows(grad_inner[:, j * model:(j + 1) * model]) for j in range(wide)]
        + [by_rows(grad_outer)], axis=1,
    )
    none = jnp.zeros((model,), f32)
    sums = jnp.concatenate([
        jnp.stack([none, none, grad_bias_output, grad_bias_outer, grad_gain_one, grad_bias_one, grad_gain_two, grad_bias_two]),
        grad_bias_inner.reshape(wide, model)], axis=0)
    return layer_result.astype(bf), d_resid, ga, d_mixed, sums


def shards(
    tokens, cotangent, starts,
    w_query, w_key, w_value, w_output, w_inner, w_outer,
    b_query, b_value, b_output, b_inner, b_outer,
    gain_first, bias_first, gain_second, bias_second,
):
    model = tokens.shape[1]
    rows = w_query.shape[0]
    shards_n = lax.axis_size("wshard")
    seq_n = lax.axis_size("seq")
    seq_i = lax.axis_index("seq")
    width = model // seq_n
    heads = width // HD
    wide = w_inner.shape[1] // model

    def own(columns):
        return lax.dynamic_slice_in_dim(columns, seq_i * width, width, columns.ndim - 1)

    smalls = (b_query, b_value, b_output, b_outer, gain_first, bias_first, gain_second, bias_second)
    small_cols = jnp.stack(smalls + tuple(b_inner.reshape(wide, rows)), axis=1)
    cols_n = small_cols.shape[1]
    b = jnp.concatenate([own(w_query), own(w_key), own(w_value), jnp.pad(small_cols, ((0, 0), (0, HD - cols_n)))], axis=1)
    fast = chips_of_two_by_four()

    def packed(share, part):
        cut = lambda w: lax.dynamic_slice_in_dim(w, w.shape[0] // share * part, w.shape[0] // share, 0)
        inner = cut(w_inner).reshape(rows // share, wide, model).transpose(1, 0, 2).reshape(-1, model)
        return jnp.concatenate([cut(w_output), inner, cut(w_outer)], axis=0)

    if fast:
        big = lax.all_gather(packed(2, seq_i % 2), "wshard")
        side, stream = gather_inputs(b, tokens)
    else:
        big = lax.all_gather(packed(1, 0), "wshard")
        side, stream = lax.all_gather(b, "wshard"), lax.all_gather(tokens, "seq")
    stream = stream.reshape(-1, model)
    side = side.reshape(model, -1)
    w_own = side[:, :3 * width]
    vectors = side[:, 3 * width:3 * width + cols_n].astype(f32).T
    bias_query, bias_value = vectors[:2]
    bias_inner = vectors[8:].reshape(wide, shards_n, rows).transpose(1, 0, 2).reshape(-1)
    scale = HD ** -0.5
    qT = ((contract(w_own[:, :width], stream, 0, 1) + own(bias_query)[:, None]).astype(bf) * bf(scale))
    kT = contract(w_own[:, width:2 * width], stream, 0, 1).astype(bf)
    vT = (contract(w_own[:, 2 * width:], stream, 0, 1) + own(bias_value)[:, None]).astype(bf)

    def by_token(arr):
        return arr.reshape(heads, HD, -1).transpose(0, 2, 1)

    def by_feature(arr):
        return arr.transpose(0, 2, 1).reshape(width, -1)

    q3, k3, v3 = by_token(qT), by_token(kT), by_token(vT)
    oT, mixT, lse = attn_fwd(starts, qT, k3, vT, 512, 512)
    mixed = lax.all_to_all(mixT, "seq", split_axis=1, concat_axis=0, tiled=True)

    vec = jnp.concatenate([vectors[:8], bias_inner.reshape(wide, model), jnp.zeros((4, model), f32)], axis=0)
    if fast:
        layer_result, d_resid, ga, d_mixed, sums = ffn_block(mixed, tokens, cotangent, vec, big)
    else:
        layer_result, d_resid, ga, d_mixed, sums = ffn_plain(mixed, tokens, cotangent, vec, big)
    doT = lax.all_to_all(d_mixed, "seq", split_axis=0, concat_axis=1, tiled=True)

    dqT, dk3, dv3 = attn_bwd(starts, qT, q3, k3, kT, v3, doT, by_token(doT), oT, lse, 256, 512)
    dT = jnp.concatenate([dqT, by_feature(dk3), by_feature(dv3)], axis=0)
    gb = contract(stream, dT, 0, 1).astype(bf).reshape(shards_n, rows, -1)
    dx = contract(dT, w_own, 0, 1).astype(bf).reshape(seq_n, -1, model)
    def spread(own_sum):
        return lax.dynamic_update_slice(jnp.zeros((model,), f32), own_sum, (seq_i * width,))

    small_rows = (
        spread(jnp.sum(dqT.astype(f32), axis=1)),
        spread(jnp.sum(dv3.astype(f32), axis=1).reshape(-1)),
        *sums[2:8],
    )
    sm = jnp.concatenate(
        [jnp.stack([row.reshape(shards_n, rows) for row in small_rows], axis=1),
         sums[8:8 + wide].reshape(shards_n, wide, rows)], axis=1,
    )
    sm = jnp.pad(sm, ((0, 0), (0, -cols_n % 8), (0, -rows % 128)))
    fa, fb, fx, fr, fs = reduce_parts(ga, gb, dx, sm)
    d_tokens = fx.astype(f32) + fr.astype(f32) + d_resid
    fb = fb.astype(f32)
    grads = [
        jnp.concatenate([fb[s, :, i * width:(i + 1) * width] for s in range(seq_n)], axis=1) for i in range(3)
    ]
    fa = fa.astype(f32)
    g_inner = jnp.concatenate([fa[(1 + j) * rows:(2 + j) * rows] for j in range(wide)], axis=1)
    tail = [fs[i, :rows] for i in range(8)]
    g_b_inner = fs[8:8 + wide, :rows].reshape(-1)
    return (
        layer_result, d_tokens, *grads,
        fa[:rows], g_inner, fa[(1 + wide) * rows:],
        tail[0], tail[1], tail[2], g_b_inner, *tail[3:],
    )


def solution(mesh):
    placed = (
        P(("wshard", "seq"), None),
        P(("wshard", "seq"), None),
        P("wshard", None),
        P("wshard", None),
        P("wshard", None),
        P("wshard", None),
        P("wshard", None),
        P("wshard", None),
        P("wshard", None),
        P("wshard"),
        P("wshard"),
        P("wshard"),
        P("wshard"),
        P("wshard"),
        P("wshard"),
        P("wshard"),
        P("wshard"),
        P("wshard"),
    )
    return jax.shard_map(
        shards,
        mesh=mesh,
        in_specs=placed,
        out_specs=(
            P(("wshard", "seq"), None),
            P(("wshard", "seq"), None),
            P("wshard", None),
            P("wshard", None),
            P("wshard", None),
            P("wshard", None),
            P("wshard", None),
            P("wshard", None),
            P("wshard"),
            P("wshard"),
            P("wshard"),
            P("wshard"),
            P("wshard"),
            P("wshard"),
            P("wshard"),
            P("wshard"),
            P("wshard"),
        ),
        check_vma=False,
    )
```

```python
import functools

import jax
import jax.numpy as jnp
from jax import lax
from jax.experimental import pallas as pl
from jax.experimental.pallas import tpu as pltpu
from jax.sharding import PartitionSpec as P

NORM_EPS = 1e-05
HD = 64
bf = jnp.bfloat16
f32 = jnp.float32


def doc_bounds(starts_ref, pos, total):
    lo = jnp.zeros_like(pos); hi = jnp.full_like(pos, total)
    for d in range(starts_ref.shape[1]):
        s = starts_ref[0, d]
        lo = jnp.where(s <= pos, jnp.maximum(lo, s), lo)
        hi = jnp.where(s > pos, jnp.minimum(hi, s), hi)
    return lo, hi

def dot(a, b):
    return lax.dot_general(a, b, (((1,), (0,)), ((), ())), preferred_element_type=f32)

def fwd_kernel(heads, bq, bk, starts, qT, k3, vT, oT, mixT, lse, acc, ml):
    total = k3.shape[1]
    i = pl.program_id(0)
    q0 = i * bq
    first, _ = doc_bounds(starts, jnp.int32(q0), total)
    _, last = doc_bounds(starts, jnp.int32(q0 + bq - 1), total)
    pos = q0 + lax.broadcasted_iota(jnp.int32, (1, bq), 1)
    lo, hi = doc_bounds(starts, pos, total)
    kb0 = first // bk
    kb1 = (last + bk - 1) // bk
    acc[...] = jnp.zeros_like(acc)
    ml[0] = jnp.full((heads, bq), -1e30, f32)
    ml[1] = jnp.zeros((heads, bq), f32)
    kio = lax.broadcasted_iota(jnp.int32, (bk, bq), 0)
    def body(j, _):
        ks = pl.multiple_of(j * bk, bk)
        mask = (kio >= lo - ks) & (kio < hi - ks)
        for h in range(heads):
            s = dot(k3[h, pl.ds(ks, bk), :], qT[HD * h:HD * (h + 1), :])
            s = jnp.where(mask, s, -1e30)
            m_old = ml[0, h:h + 1]
            m = jnp.maximum(m_old, jnp.max(s, axis=0, keepdims=True))
            p = jnp.exp(s - m)
            al = jnp.exp(m_old - m)
            ml[0, h:h + 1] = m
            ml[1, h:h + 1] = ml[1, h:h + 1] * al + jnp.sum(p, axis=0, keepdims=True)
            sl = slice(HD * h, HD * (h + 1))
            acc[sl, :] = acc[sl, :] * al + dot(vT[sl, pl.ds(ks, bk)], p.astype(bf))
        return 0
    lax.fori_loop(kb0, kb1, body, 0)
    for h in range(heads):
        sl = slice(HD * h, HD * (h + 1))
        l = ml[1, h:h + 1]
        o = acc[sl, :] / l
        oT[sl, :] = o
        mixT[sl, :] = o.astype(bf)
        lse[h:h + 1, :] = ml[0, h:h + 1] + jnp.log(l)

def attn_fwd(starts, qT, k3, vT, bq=256, bk=256):
    heads, total, _ = k3.shape
    full2 = lambda i: (0, 0)
    return pl.pallas_call(
        functools.partial(fwd_kernel, heads, bq, bk),
        grid=(total // bq,),
        in_specs=[pl.BlockSpec(memory_space=pltpu.SMEM),
                  pl.BlockSpec((heads * HD, bq), lambda i: (0, i)),
                  pl.BlockSpec(k3.shape, lambda i: (0, 0, 0)),
                  pl.BlockSpec(vT.shape, full2)],
        out_specs=[pl.BlockSpec((heads * HD, bq), lambda i: (0, i)),
                   pl.BlockSpec((heads * HD, bq), lambda i: (0, i)),
                   pl.BlockSpec((heads, bq), lambda i: (0, i))],
        out_shape=[jax.ShapeDtypeStruct((heads * HD, total), f32),
                   jax.ShapeDtypeStruct((heads * HD, total), bf),
                   jax.ShapeDtypeStruct((heads, total), f32)],
        scratch_shapes=[pltpu.VMEM((heads * HD, bq), f32), pltpu.VMEM((2, heads, bq), f32)],
        cost_estimate=pl.CostEstimate(flops=8 * heads * HD * total * total, bytes_accessed=8 * heads * HD * total, transcendentals=0),
        name="attn_fwd",
    )(starts, qT, k3, vT)

def bwd_kernel(heads, bq, bk, starts, qT, q3, k3, kT, v3, doT, do3, oT, lse, dqT, dk3, dv3, delta, dqa, dka, dva):
    total = q3.shape[1]
    i = pl.program_id(0)
    k0 = i * bk
    @pl.when(i == 0)
    def _():
        dqa[...] = jnp.zeros_like(dqa)
        for h in range(heads):
            sl = slice(HD * h, HD * (h + 1))
            delta[h:h + 1, :] = jnp.sum(doT[sl, :].astype(f32) * oT[sl, :], axis=0, keepdims=True)
    first, _ = doc_bounds(starts, jnp.int32(k0), total)
    _, last = doc_bounds(starts, jnp.int32(k0 + bk - 1), total)
    qb0 = first // bq
    qb1 = (last + bq - 1) // bq
    dka[...] = jnp.zeros_like(dka)
    dva[...] = jnp.zeros_like(dva)
    kio = k0 + lax.broadcasted_iota(jnp.int32, (bk, bq), 0)
    def body(j, _):
        qs = pl.multiple_of(j * bq, bq)
        pos = qs + lax.broadcasted_iota(jnp.int32, (1, bq), 1)
        lo, hi = doc_bounds(starts, pos, total)
        mask = (kio >= lo) & (kio < hi)
        for h in range(heads):
            sl = slice(HD * h, HD * (h + 1))
            s = dot(k3[h, :, :], qT[sl, pl.ds(qs, bq)])
            p = jnp.exp(jnp.where(mask, s - lse[h:h + 1, pl.ds(qs, bq)], -1e30))
            dp = dot(v3[h, :, :], doT[sl, pl.ds(qs, bq)])
            ds = p * (dp - delta[h:h + 1, pl.ds(qs, bq)])
            dsb = ds.astype(bf)
            dva[h] += dot(p.astype(bf), do3[h, pl.ds(qs, bq), :])
            dka[h] += dot(dsb, q3[h, pl.ds(qs, bq), :])
            dqa[sl, pl.ds(qs, bq)] += dot(kT[sl, :], dsb)
        return 0
    lax.fori_loop(qb0, qb1, body, 0)
    dk3[...] = dka[...].astype(bf)
    dv3[...] = dva[...].astype(bf)
    @pl.when(i == pl.num_programs(0) - 1)
    def _():
        dqT[...] = (dqa[...] * (HD ** -0.5)).astype(bf)

def attn_bwd(starts, qT, q3, k3, kT, v3, doT, do3, oT, lse, bq=256, bk=256):
    heads, total, _ = k3.shape
    full = lambda a: pl.BlockSpec(a.shape, lambda i: (0,) * a.ndim)
    kb3 = pl.BlockSpec((heads, bk, HD), lambda i: (0, i, 0))
    return pl.pallas_call(
        functools.partial(bwd_kernel, heads, bq, bk),
        grid=(total // bk,),
        in_specs=[pl.BlockSpec(memory_space=pltpu.SMEM), full(qT), full(q3), kb3,
                  pl.BlockSpec((heads * HD, bk), lambda i: (0, i)), kb3, full(doT), full(do3), full(oT), full(lse)],
        out_specs=[full(qT), kb3, kb3],
        out_shape=[jax.ShapeDtypeStruct(qT.shape, bf), jax.ShapeDtypeStruct(k3.shape, bf), jax.ShapeDtypeStruct(k3.shape, bf)],
        scratch_shapes=[pltpu.VMEM((heads, total), f32), pltpu.VMEM(qT.shape, f32),
                        pltpu.VMEM((heads, bk, HD), f32), pltpu.VMEM((heads, bk, HD), f32)],
        name="attn_bwd",
    )(starts, qT, q3, k3, kT, v3, doT, do3, oT, lse)


MESH = pl.DeviceIdType.MESH


class Wire:
    def __init__(self, send, recv):
        self.send, self.recv, self.used, self.open = send, recv, 0, []

    def slot(self):
        self.used += 1
        return self.used - 1

    def start(self, slot, src, dst, device):
        copy = pltpu.make_async_remote_copy(
            src_ref=src, dst_ref=dst, send_sem=self.send.at[slot], recv_sem=self.recv.at[slot],
            device_id=device, device_id_type=MESH,
        )
        copy.start()
        self.open.append(copy)
        return copy

    def arrived(self, slot, dst, device):
        pltpu.make_async_remote_copy(
            src_ref=dst, dst_ref=dst, send_sem=self.send.at[slot], recv_sem=self.recv.at[slot],
            device_id=device, device_id_type=MESH,
        ).wait_recv()

    def sent(self, copy):
        copy.wait_send()
        self.open = [other for other in self.open if other is not copy]

    def drain(self):
        for copy in self.open:
            copy.wait_send()
        self.open = []


def grid_peers():
    shard, seq = lax.axis_index("wshard"), lax.axis_index("seq")
    z, y = shard // 2, shard % 2
    x, c = seq // 2, seq % 2
    at = lambda zz, yy, xx, cc: (zz * 2 + yy, xx * 2 + cc)
    along = [at((z + d) % 4, y, x, c) for d in range(4)]
    return z, y, x, c, along, at(z, 1 - y, x, c), at(z, y, 1 - x, c), at(z, y, x, 1 - c)


def greet(peers):
    barrier = pltpu.get_barrier_semaphore()
    for peer in peers:
        pl.semaphore_signal(barrier, inc=1, device_id=peer, device_id_type=MESH)
    pl.semaphore_wait(barrier, len(peers))


ORDER = (1, 3, 2)


def gather_kernel(b_ref, t_ref, q_ref, x_ref, send, recv, lsem):
    z, y, x, c, along, ypeer, xpeer, cpeer = grid_peers()
    own = z * 2 + y
    wire = Wire(send, recv)
    spot = lambda r, d: ((z + 4 - d) % 4) * 2 + (y if r == 0 else 1 - y)
    seq = x * 2 + c
    half = t_ref.shape[0] // 2
    parts = [pl.ds(0, half), pl.ds(half, half)]
    locals_ = [
        pltpu.make_async_copy(b_ref, q_ref.at[own], lsem.at[0]),
        pltpu.make_async_copy(t_ref, x_ref.at[seq], lsem.at[1]),
    ]
    for copy in locals_:
        copy.start()
    greet(along[1:] + [ypeer, xpeer, cpeer])
    zB = [wire.slot() for _ in range(4)]
    yB = [wire.slot() for _ in range(4)]
    tx, tc1 = [wire.slot() for _ in parts], [wire.slot() for _ in parts]
    tc0 = wire.slot()
    for slot, part in zip(tx, parts):
        wire.start(slot, t_ref.at[part], x_ref.at[seq, part], xpeer)
    for d in ORDER:
        wire.start(zB[d], b_ref, q_ref.at[own], along[d])
    wire.start(yB[0], b_ref, q_ref.at[own], ypeer)
    wire.start(tc0, t_ref, x_ref.at[seq], cpeer)
    for d in ORDER:
        w = spot(0, d)
        wire.arrived(zB[d], q_ref.at[w], along[d])
        wire.start(yB[d], q_ref.at[w], q_ref.at[w], ypeer)
    xtok = (1 - x) * 2 + c
    for i, part in enumerate(parts):
        wire.arrived(tx[i], x_ref.at[xtok, part], xpeer)
        wire.start(tc1[i], x_ref.at[xtok, part], x_ref.at[xtok, part], cpeer)
    for d in (0,) + ORDER:
        wire.arrived(yB[d], q_ref.at[spot(1, d)], ypeer)
    wire.arrived(tc0, x_ref.at[x * 2 + 1 - c], cpeer)
    for i, part in enumerate(parts):
        wire.arrived(tc1[i], x_ref.at[(1 - x) * 2 + 1 - c, part], cpeer)
    wire.drain()
    for copy in locals_:
        copy.wait()


def gather_inputs(b, tokens):
    slots = 13
    hbm = pl.BlockSpec(memory_space=pl.ANY)
    vmem = pl.BlockSpec(memory_space=pltpu.VMEM)
    return pl.pallas_call(
        gather_kernel,
        in_specs=[vmem] * 2, out_specs=[hbm] * 2,
        out_shape=[jax.ShapeDtypeStruct((8,) + b.shape, b.dtype), jax.ShapeDtypeStruct((4,) + tokens.shape, tokens.dtype)],
        scratch_shapes=[pltpu.SemaphoreType.DMA((slots,)), pltpu.SemaphoreType.DMA((slots,)), pltpu.SemaphoreType.DMA((2,))],
        compiler_params=pltpu.CompilerParams(collective_id=1, has_side_effects=True),
        name="gather_inputs",
    )(b, tokens)


def add_rows(dst, parts, rows, step=16):
    def body(i, _):
        at = pl.ds(pl.multiple_of(i * step, step), step)
        total = parts[0][at, :].astype(f32)
        for part in parts[1:]:
            total = total + part[at, :].astype(f32)
        dst[at, :] = total.astype(dst.dtype)
        return 0
    lax.fori_loop(0, rows // step, body, 0)


ALL = ORDER + (0,)


def reduce_kernel(ga, gb, dx, sm, fa, fb, fx, fr, fs, hb, ryb, rzb, rxc, hs, rys, rzs, s1, s2, s3, s4, rg, send, recv):
    z, y, x, c, along, ypeer, xpeer, cpeer = grid_peers()
    wire = Wire(send, recv)
    new = lambda count: [wire.slot() for _ in range(count)]
    kc, kx, kg, kyb, kys = new(4), new(2), new(2), wire.slot(), wire.slot()
    kzb, kzs, fin = new(4), new(4), new(8)
    zz = lambda d: (z + d) % 4
    half = dx.shape[2] // 2
    halves = [pl.ds(0, half), pl.ds(half, half)]
    sizes = [ga.shape[0] // 32 * 16, ga.shape[0] - ga.shape[0] // 32 * 16]
    pieces = [pl.ds(0, sizes[0]), pl.ds(sizes[0], sizes[1])]
    greet(along[1:] + [ypeer, xpeer, cpeer])
    for i, at in enumerate(halves):
        wire.start(kc[i], dx.at[1 - x, 1 - c, at], rxc.at[1 - x, at], cpeer)
    wire.start(kg[0], ga.at[pieces[0]], rg.at[pieces[0]], xpeer)
    wire.start(kys, sm.at[:, 1 - y], rys, ypeer)
    wire.start(kyb, gb.at[:, 1 - y], ryb, ypeer)
    for i, at in enumerate(halves):
        wire.start(kc[2 + i], dx.at[x, 1 - c, at], rxc.at[x, at], cpeer)
    for i, at in enumerate(halves):
        spot = rxc.at[1 - x, at]
        wire.arrived(kc[i], spot, cpeer)
        add_rows(spot, [dx.at[1 - x, c, at], spot], half)
        wire.start(kx[i], spot, fr.at[at], xpeer)
    wire.start(kg[1], ga.at[pieces[1]], rg.at[pieces[1]], xpeer)
    wire.arrived(kys, rys, ypeer)
    wire.arrived(kyb, ryb, ypeer)
    for d in ALL:
        hs[d] = sm[zz(d), y] + rys[zz(d)]
        add_rows(hb.at[d], [gb.at[zz(d), y], ryb.at[zz(d)]], hb.shape[1])
        if d:
            wire.start(kzs[d], hs.at[d], rzs.at[d], along[d])
            wire.start(kzb[d], hb.at[d], rzb.at[d], along[d])
    for i, at in enumerate(halves):
        wire.arrived(kc[2 + i], rxc.at[x, at], cpeer)
        add_rows(fx.at[at], [dx.at[x, c, at], rxc.at[x, at]], half)
    wire.arrived(kg[0], rg.at[pieces[0]], xpeer)
    add_rows(fa.at[c, pieces[0]], [ga.at[pieces[0]], rg.at[pieces[0]]], sizes[0])
    wire.start(fin[5], fa.at[c, pieces[0]], fa.at[c, pieces[0]], cpeer)
    for d in ORDER:
        wire.arrived(kzs[d], rzs.at[d], along[d])
        wire.arrived(kzb[d], rzb.at[d], along[d])
    s1[...] = hs[0] + rzs[1] + rzs[2] + rzs[3]
    wire.start(fin[0], s1, s2, xpeer)
    seq, xseq = 2 * x + c, 2 * (1 - x) + c
    add_rows(fb.at[seq], [hb.at[0]] + [rzb.at[d] for d in ORDER], hb.shape[1])
    wire.start(fin[1], fb.at[seq], fb.at[seq], xpeer)
    wire.start(fin[2], fb.at[seq], fb.at[seq], cpeer)
    for i, at in enumerate(halves):
        wire.arrived(kx[i], fr.at[at], xpeer)
    wire.arrived(kg[1], rg.at[pieces[1]], xpeer)
    add_rows(fa.at[c, pieces[1]], [ga.at[pieces[1]], rg.at[pieces[1]]], sizes[1])
    wire.start(fin[6], fa.at[c, pieces[1]], fa.at[c, pieces[1]], cpeer)
    wire.arrived(fin[0], s2, xpeer)
    s3[...] = s1[...] + s2[...]
    wire.start(fin[3], s3, s4, cpeer)
    wire.arrived(fin[1], fb.at[xseq], xpeer)
    wire.start(fin[4], fb.at[xseq], fb.at[xseq], cpeer)
    wire.arrived(fin[3], s4, cpeer)
    fs[...] = s3[...] + s4[...]
    wire.arrived(fin[2], fb.at[2 * x + 1 - c], cpeer)
    wire.arrived(fin[4], fb.at[2 * (1 - x) + 1 - c], cpeer)
    for i in range(2):
        wire.arrived(fin[5 + i], fa.at[1 - c, pieces[i]], cpeer)
    wire.drain()


def reduce_grads(ga, gb, dx, sm):
    rows, cols = ga.shape
    toks = dx.shape[1]
    vmem = pl.BlockSpec(memory_space=pltpu.VMEM)
    b0, b1 = gb.shape[1:]
    V = pltpu.VMEM
    sv = lambda *lead: V(lead + sm.shape[1:], f32)
    slots = 26
    return pl.pallas_call(
        reduce_kernel,
        in_specs=[vmem] * 4, out_specs=[vmem] * 5,
        out_shape=[jax.ShapeDtypeStruct((2, rows, cols), bf), jax.ShapeDtypeStruct((4, b0, b1), bf),
                   jax.ShapeDtypeStruct((toks, cols), bf), jax.ShapeDtypeStruct((toks, cols), bf),
                   jax.ShapeDtypeStruct(sm.shape[1:], f32)],
        scratch_shapes=[V((4, b0, b1), bf), V((4, b0, b1), bf), V((4, b0, b1), bf), V((2, toks, cols), bf),
                        sv(4), sv(4), sv(4), sv(), sv(), sv(), sv(), V((rows, cols), bf),
                        pltpu.SemaphoreType.DMA((slots,)), pltpu.SemaphoreType.DMA((slots,))],
        compiler_params=pltpu.CompilerParams(collective_id=2, has_side_effects=True, vmem_limit_bytes=40 * 2 ** 20),
        name="reduce_grads",
    )(ga, gb.reshape((4, 2) + gb.shape[1:]), dx.reshape((2, 2) + dx.shape[1:]), sm.reshape((4, 2) + sm.shape[1:]))


def mm(a, b, left, right):
    return lax.dot_general(a, b, (((left,), (right,)), ((), ())), preferred_element_type=f32)


def chunks(total, step, body):
    def run(i, _):
        body(pl.ds(pl.multiple_of(i * step, step), step))
        return 0
    lax.fori_loop(0, total // step, run, 0)


def ffn_kernel(n, r, step, mixed, tokens, cot, vec, big, out, dres, ga, dO, small,
               w_out, w_in, w_outer, stage, fb, gp, xh1, n1b, dh2, dm, du, acc, r1, got, lsem, gsem, send, recv):
    toks, model = tokens.shape
    wide = w_in.shape[0]
    per = n // wide
    z, y, x, c, along, ypeer, xpeer, cpeer = grid_peers()
    wire = Wire(send, recv)
    greet([cpeer])
    h = r // 2
    low = lambda size, side: pl.ds(pl.multiple_of(size * side, 16), size)
    def place(s, side, k):
        if k == 0:
            return w_out.at[s, low(h, side)]
        if k <= wide:
            return w_in.at[k - 1, s, low(h, side)]
        return w_outer.at[s // per, s % per, low(wide * h, side)]
    loads = [[] for _ in range(2 + wide)]
    for k in range(2 + wide):
        span = pl.ds(k * h, h if k <= wide else wide * h)
        for s in range(n):
            slot = wire.slot()
            load = pltpu.make_async_copy(big.at[s, span], place(s, c, k), lsem.at[slot])
            load.start()
            wire.start(slot, big.at[s, span], place(s, c, k), cpeer)
            loads[k].append((load, slot, place(s, 1 - c, k)))

    def ready(k):
        for load, slot, spot in loads[k]:
            load.wait()
            wire.arrived(slot, spot, cpeer)

    stores = []

    pending, swaps = [], []

    def finish():
        k, slot, groups, size, span, way = pending.pop()
        wire.arrived(way, got.at[k].reshape((groups, size, model)), cpeer)
        rows, strip = groups * size, min(size, 96)
        def body(i, _):
            at = i * strip
            mine = pl.ds(pl.multiple_of((at // size * 2 + c) * size + at % size, 16), strip)
            theirs = pl.ds(pl.multiple_of(at, 16), strip)
            stage[slot, mine, :] = (stage[slot, mine, :].astype(f32) + got[k, theirs, :].astype(f32)).astype(bf)
            return 0
        lax.fori_loop(0, rows // strip, body, 0)
        whole = stage.at[slot].reshape((groups, 2 * size, model))
        store = pltpu.make_async_copy(whole.at[:, low(size, c)], span, gsem.at[slot])
        store.start()
        stores.append(store)

    def put(value_rows, groups, span):
        k = len(swaps)
        slot = k % stage.shape[0]
        if k >= stage.shape[0]:
            wire.sent(swaps[k - stage.shape[0]])
            stores[k - stage.shape[0]].wait()
        def body(at):
            stage[slot, at, :] = value_rows(at).astype(bf)
        chunks(model, step, body)
        size = model // groups // 2
        way = wire.slot()
        whole = stage.at[slot].reshape((groups, 2 * size, model))
        swaps.append(wire.start(way, whole.at[:, low(size, 1 - c)], got.at[k].reshape((groups, size, model)), cpeer))
        if pending:
            finish()
        pending.append((k, slot, groups, size, span, way))

    flat = lambda ref: ref.reshape(model, model)
    row = lambda i: vec[i:i + 1, :]
    b_output, b_outer, g1, s1, g2, s2 = [row(i) for i in (2, 3, 4, 5, 6, 7)]
    small[...] = jnp.zeros_like(small)
    ready(0)
    wo = flat(w_out)

    def first(at):
        attn = mm(mixed[:, at], wo[...], 0, 0)
        z = tokens[at, :].astype(f32) + (attn + b_output)
        cen = z - jnp.mean(z, axis=-1, keepdims=True)
        inv = lax.rsqrt(jnp.mean(cen * cen, axis=-1, keepdims=True) + NORM_EPS)
        xh = cen * inv
        norm = xh * g1 + s1
        xh1[at, :] = xh
        n1b[at, :] = norm.astype(bf)
        r1[at, :] = jnp.broadcast_to(inv, (inv.shape[0], 128))
        acc[at, :] = norm + b_outer
    chunks(toks, step, first)
    for j in range(wide):
        ready(1 + j)
        wi = flat(w_in.at[j])
        bias = row(8 + j)
        def inner(at, j=j, wi=wi, bias=bias):
            u = mm(n1b[at, :], wi[...], 1, 0) + bias
            cdf = 0.5 * (1.0 + lax.erf(u * (0.5 ** 0.5)))
            pdf = jnp.exp(-0.5 * u * u) * 0.3989422804014327
            fb[j, at, :] = (u * cdf).astype(bf)
            gp[j, at, :] = cdf + u * pdf
        chunks(toks, step, inner)
    ready(1 + wide)
    for j in range(wide):
        wout = flat(w_outer.at[j])
        def outer(at, j=j, wout=wout):
            acc[at, :] += mm(fb[j, at, :], wout[...], 1, 0)
        chunks(toks, step, outer)

    def second(at):
        z = acc[at, :]
        cen = z - jnp.mean(z, axis=-1, keepdims=True)
        inv = lax.rsqrt(jnp.mean(cen * cen, axis=-1, keepdims=True) + NORM_EPS)
        xh = cen * inv
        out[at, :] = (xh * g2 + s2).astype(bf)
        g = cot[at, :].astype(f32)
        gx = g * xh
        gh = g * g2
        d = inv * (gh - jnp.mean(gh, axis=-1, keepdims=True) - xh * jnp.mean(gh * xh, axis=-1, keepdims=True))
        dh2[at, :] = d
        low = d.astype(bf)
        dm[at, :] = low
        small[6:7, :] += jnp.sum(gx, axis=0, keepdims=True)
        small[7:8, :] += jnp.sum(g, axis=0, keepdims=True)
        small[3:4, :] += jnp.sum(low.astype(f32), axis=0, keepdims=True)
    chunks(toks, step, second)
    for j in range(wide):
        wout = flat(w_outer.at[j])
        put(lambda at, j=j: mm(fb[j, :, at], dm[...], 0, 0), per, ga.at[pl.ds(j * per, per), pl.ds((1 + wide) * h, wide * h)])
        def dinner(at, j=j, wout=wout):
            low = (gp[j, at, :] * mm(dm[at, :], wout[...], 1, 1)).astype(bf)
            du[at, :] = low
            small[8 + j:9 + j, :] += jnp.sum(low.astype(f32), axis=0, keepdims=True)
        chunks(toks, step, dinner)
        wi = flat(w_in.at[j])
        def dfirst(at, wi=wi):
            dh2[at, :] += mm(du[at, :], wi[...], 1, 1)
        chunks(toks, step, dfirst)
        put(lambda at: mm(n1b[:, at], du[...], 0, 0), n, ga.at[:, pl.ds((1 + j) * h, h)])

    def last(at):
        d = dh2[at, :]
        xh = xh1[at, :]
        gh = d * g1
        inv = r1[at, 0:1]
        z = inv * (gh - jnp.mean(gh, axis=-1, keepdims=True) - xh * jnp.mean(gh * xh, axis=-1, keepdims=True))
        dres[at, :] = z
        low = z.astype(bf)
        dm[at, :] = low
        small[4:5, :] += jnp.sum(d * xh, axis=0, keepdims=True)
        small[5:6, :] += jnp.sum(d, axis=0, keepdims=True)
        small[2:3, :] += jnp.sum(low.astype(f32), axis=0, keepdims=True)
    chunks(toks, step, last)

    def back(at):
        dO[at, :] = mm(wo[at, :], dm[...], 1, 1).astype(bf)
    chunks(model, step, back)
    put(lambda at: mm(mixed[at, :], dm[...], 1, 0), n, ga.at[:, pl.ds(0, h)])
    finish()
    for store in stores[-stage.shape[0]:]:
        store.wait()
    wire.drain()


def ffn_block(mixed, tokens, cot, vec, big, step=384):
    n, half, model = big.shape
    r = model // n
    wide = (2 * half // r - 1) // 2
    toks = tokens.shape[0]
    vmem = pl.BlockSpec(memory_space=pltpu.VMEM)
    hbm = pl.BlockSpec(memory_space=pl.ANY)
    per = n // wide
    ohold = (per, wide * r, model) if per else (n, r, model)
    V = pltpu.VMEM
    sq = lambda dt, *lead: V(lead + (toks, model), dt)
    return pl.pallas_call(
        functools.partial(ffn_kernel, n, r, step),
        in_specs=[vmem] * 4 + [hbm],
        out_specs=[vmem, vmem, hbm, vmem, vmem],
        out_shape=[jax.ShapeDtypeStruct((toks, model), bf), jax.ShapeDtypeStruct((toks, model), f32),
                   jax.ShapeDtypeStruct((n, half, model), bf), jax.ShapeDtypeStruct((model, toks), bf),
                   jax.ShapeDtypeStruct((16, model), f32)],
        scratch_shapes=[V((n, r, model), bf), V((wide, n, r, model), bf), V((wide,) + ohold, bf), V((4, model, model), bf),
                        sq(bf, wide), sq(f32, wide), sq(f32), sq(bf), sq(f32), sq(bf), sq(bf), sq(f32),
                        V((toks, 128), f32), V((1 + 2 * wide, model // 2, model), bf), pltpu.SemaphoreType.DMA(((2 + wide) * n,)), pltpu.SemaphoreType.DMA((4,)),
                        pltpu.SemaphoreType.DMA(((2 + wide) * n + 1 + 2 * wide,)), pltpu.SemaphoreType.DMA(((2 + wide) * n + 1 + 2 * wide,))],
        compiler_params=pltpu.CompilerParams(collective_id=3, has_side_effects=True, vmem_limit_bytes=67043328),
        cost_estimate=pl.CostEstimate(flops=2 * toks * model * model * (3 + 6 * wide), bytes_accessed=8 * n * half * model, transcendentals=2 * toks * model * wide),
        name="ffn_block",
    )(mixed, tokens, cot, vec, big)


def layer_norm(inputs, norm_gain, norm_bias):
    row_mean = jnp.mean(inputs, axis=-1, keepdims=True)
    centred = inputs - row_mean
    row_var = jnp.mean(centred * centred, axis=-1, keepdims=True)
    return centred * lax.rsqrt(row_var + NORM_EPS) * norm_gain + norm_bias


def gelu_exact(inputs):
    return jax.nn.gelu(inputs, approximate=False)


def contract(left_in, right_in, left_dim, right_dim):
    return lax.dot_general(
        left_in,
        right_in,
        (((left_dim,), (right_dim,)), ((), ())),
        preferred_element_type=jnp.float32,
    )


def chips_of_two_by_four():
    return lax.axis_size("wshard") == 8 and lax.axis_size("seq") == 4


def reduce_parts(ga, gb, dx, sm):
    def scatter(part):
        return lax.psum_scatter(part, "wshard", scatter_dimension=0, tiled=False)

    if chips_of_two_by_four():
        return reduce_grads(scatter(ga), gb, dx, sm)

    fx = lax.psum_scatter(dx, "seq", scatter_dimension=0, tiled=False)
    return (
        lax.psum(scatter(ga), "seq")[None], lax.all_gather(scatter(gb), "seq"), fx, jnp.zeros_like(fx),
        lax.psum(scatter(sm), "seq"),
    )


def ffn_plain(mixed, tokens, cotangent, vec, big):
    shards_n, rows9, model = big.shape
    rows = model // shards_n
    wide = (rows9 // rows - 1) // 2
    bias_output, bias_outer, gain_one, shift_one, gain_two, shift_two = vec[2:8]
    bias_inner = vec[8:8 + wide].reshape(-1)
    output_full = big[:, :rows].reshape(model, model)
    inner_full = jnp.concatenate(
        [big[:, (1 + j) * rows:(2 + j) * rows].reshape(model, model) for j in range(wide)], axis=1
    )
    outer_full = big[:, (1 + wide) * rows:].reshape(-1, model)

    residual_in = tokens.astype(f32) + contract(mixed, output_full, 0, 0) + bias_output
    first_norm, first_back = jax.vjp(layer_norm, residual_in, gain_one, shift_one)
    first_low = first_norm.astype(bf)
    inner_act = jnp.dot(first_low, inner_full, preferred_element_type=f32) + bias_inner
    gelu_out, gelu_back = jax.vjp(gelu_exact, inner_act)
    gelu_low = gelu_out.astype(bf)
    second_in = first_norm + jnp.dot(gelu_low, outer_full, preferred_element_type=f32) + bias_outer
    layer_result, second_back = jax.vjp(layer_norm, second_in, gain_two, shift_two)
    d_second, grad_gain_two, grad_bias_two = second_back(cotangent.astype(f32))
    d_outer = d_second.astype(bf)
    grad_bias_outer = jnp.sum(d_outer.astype(f32), axis=0)
    grad_outer = contract(gelu_low, d_outer, 0, 0)
    (d_inner,) = gelu_back(contract(d_outer, outer_full, 1, 1))
    d_inner_low = d_inner.astype(bf)
    grad_bias_inner = jnp.sum(d_inner_low.astype(f32), axis=0)
    grad_inner = contract(first_low, d_inner_low, 0, 0)
    d_first = contract(d_inner_low, inner_full, 1, 1) + d_second
    d_resid, grad_gain_one, grad_bias_one = first_back(d_first)
    d_attn = d_resid.astype(bf)
    grad_bias_output = jnp.sum(d_attn.astype(f32), axis=0)
    grad_output = contract(mixed, d_attn, 1, 0)
    d_mixed = contract(output_full, d_attn, 1, 1).astype(bf)
    by_rows = lambda grad: grad.astype(bf).reshape(shards_n, -1, model)
    ga = jnp.concatenate(
        [by_rows(grad_output)] + [by_rows(grad_inner[:, j * model:(j + 1) * model]) for j in range(wide)]
        + [by_rows(grad_outer)], axis=1,
    )
    none = jnp.zeros((model,), f32)
    sums = jnp.concatenate([
        jnp.stack([none, none, grad_bias_output, grad_bias_outer, grad_gain_one, grad_bias_one, grad_gain_two, grad_bias_two]),
        grad_bias_inner.reshape(wide, model)], axis=0)
    return layer_result.astype(bf), d_resid, ga, d_mixed, sums


def shards(
    tokens, cotangent, starts,
    w_query, w_key, w_value, w_output, w_inner, w_outer,
    b_query, b_value, b_output, b_inner, b_outer,
    gain_first, bias_first, gain_second, bias_second,
):
    model = tokens.shape[1]
    rows = w_query.shape[0]
    shards_n = lax.axis_size("wshard")
    seq_n = lax.axis_size("seq")
    seq_i = lax.axis_index("seq")
    width = model // seq_n
    heads = width // HD
    wide = w_inner.shape[1] // model

    def own(columns):
        return lax.dynamic_slice_in_dim(columns, seq_i * width, width, columns.ndim - 1)

    smalls = (b_query, b_value, b_output, b_outer, gain_first, bias_first, gain_second, bias_second)
    small_cols = jnp.stack(smalls + tuple(b_inner.reshape(wide, rows)), axis=1)
    cols_n = small_cols.shape[1]
    b = jnp.concatenate([own(w_query), own(w_key), own(w_value), jnp.pad(small_cols, ((0, 0), (0, HD - cols_n)))], axis=1)
    fast = chips_of_two_by_four()

    def packed(share, part):
        cut = lambda w: lax.dynamic_slice_in_dim(w, w.shape[0] // share * part, w.shape[0] // share, 0)
        inner = cut(w_inner).reshape(rows // share, wide, model).transpose(1, 0, 2).reshape(-1, model)
        return jnp.concatenate([cut(w_output), inner, cut(w_outer)], axis=0)

    if fast:
        big = lax.all_gather(packed(2, seq_i % 2), "wshard")
        side, stream = gather_inputs(b, tokens)
    else:
        big = lax.all_gather(packed(1, 0), "wshard")
        side, stream = lax.all_gather(b, "wshard"), lax.all_gather(tokens, "seq")
    stream = stream.reshape(-1, model)
    side = side.reshape(model, -1)
    w_own = side[:, :3 * width]
    vectors = side[:, 3 * width:3 * width + cols_n].astype(f32).T
    bias_query, bias_value = vectors[:2]
    bias_inner = vectors[8:].reshape(wide, shards_n, rows).transpose(1, 0, 2).reshape(-1)
    scale = HD ** -0.5
    qT = ((contract(w_own[:, :width], stream, 0, 1) + own(bias_query)[:, None]).astype(bf) * bf(scale))
    kT = contract(w_own[:, width:2 * width], stream, 0, 1).astype(bf)
    vT = (contract(w_own[:, 2 * width:], stream, 0, 1) + own(bias_value)[:, None]).astype(bf)

    def by_token(arr):
        return arr.reshape(heads, HD, -1).transpose(0, 2, 1)

    def by_feature(arr):
        return arr.transpose(0, 2, 1).reshape(width, -1)

    q3, k3, v3 = by_token(qT), by_token(kT), by_token(vT)
    oT, mixT, lse = attn_fwd(starts, qT, k3, vT, 512, 512)
    mixed = lax.all_to_all(mixT, "seq", split_axis=1, concat_axis=0, tiled=True)

    vec = jnp.concatenate([vectors[:8], bias_inner.reshape(wide, model), jnp.zeros((4, model), f32)], axis=0)
    if fast:
        layer_result, d_resid, ga, d_mixed, sums = ffn_block(mixed, tokens, cotangent, vec, big)
    else:
        layer_result, d_resid, ga, d_mixed, sums = ffn_plain(mixed, tokens, cotangent, vec, big)
    doT = lax.all_to_all(d_mixed, "seq", split_axis=0, concat_axis=1, tiled=True)

    dqT, dk3, dv3 = attn_bwd(starts, qT, q3, k3, kT, v3, doT, by_token(doT), oT, lse, 256, 512)
    dT = jnp.concatenate([dqT, by_feature(dk3), by_feature(dv3)], axis=0)
    gb = contract(stream, dT, 0, 1).astype(bf).reshape(shards_n, rows, -1)
    dx = contract(dT, w_own, 0, 1).astype(bf).reshape(seq_n, -1, model)
    def spread(own_sum):
        return lax.dynamic_update_slice(jnp.zeros((model,), f32), own_sum, (seq_i * width,))

    small_rows = (
        spread(jnp.sum(dqT.astype(f32), axis=1)),
        spread(jnp.sum(dv3.astype(f32), axis=1).reshape(-1)),
        *sums[2:8],
    )
    sm = jnp.concatenate(
        [jnp.stack([row.reshape(shards_n, rows) for row in small_rows], axis=1),
         sums[8:8 + wide].reshape(shards_n, wide, rows)], axis=1,
    )
    sm = jnp.pad(sm, ((0, 0), (0, -cols_n % 8), (0, -rows % 128)))
    fa, fb, fx, fr, fs = reduce_parts(ga, gb, dx, sm)
    d_tokens = fx.astype(f32) + fr.astype(f32) + d_resid
    fb = fb.astype(f32)
    grads = [
        jnp.concatenate([fb[s, :, i * width:(i + 1) * width] for s in range(seq_n)], axis=1) for i in range(3)
    ]
    fa = fa.astype(f32)
    part = rows // fa.shape[0]
    span = lambda first, count: fa[:, first * part:(first + count) * part].reshape(-1, model)
    g_inner = jnp.concatenate([span(1 + j, 1) for j in range(wide)], axis=1)
    tail = [fs[i, :rows] for i in range(8)]
    g_b_inner = fs[8:8 + wide, :rows].reshape(-1)
    return (
        layer_result, d_tokens, *grads,
        span(0, 1), g_inner, span(1 + wide, wide),
        tail[0], tail[1], tail[2], g_b_inner, *tail[3:],
    )


def solution(mesh):
    placed = (
        P(("wshard", "seq"), None),
        P(("wshard", "seq"), None),
        P("wshard", None),
        P("wshard", None),
        P("wshard", None),
        P("wshard", None),
        P("wshard", None),
        P("wshard", None),
        P("wshard", None),
        P("wshard"),
        P("wshard"),
        P("wshard"),
        P("wshard"),
        P("wshard"),
        P("wshard"),
        P("wshard"),
        P("wshard"),
        P("wshard"),
    )
    return jax.shard_map(
        shards,
        mesh=mesh,
        in_specs=placed,
        out_specs=(
            P(("wshard", "seq"), None),
            P(("wshard", "seq"), None),
            P("wshard", None),
            P("wshard", None),
            P("wshard", None),
            P("wshard", None),
            P("wshard", None),
            P("wshard", None),
            P("wshard"),
            P("wshard"),
            P("wshard"),
            P("wshard"),
            P("wshard"),
            P("wshard"),
            P("wshard"),
            P("wshard"),
            P("wshard"),
        ),
        check_vma=False,
    )
```

```python
import functools

import jax
import jax.numpy as jnp
from jax import lax
from jax.experimental import pallas as pl
from jax.experimental.pallas import tpu as pltpu
from jax.sharding import PartitionSpec as P

NORM_EPS = 1e-05
HD = 64
bf = jnp.bfloat16
f32 = jnp.float32


def doc_bounds(starts_ref, pos, total):
    lo = jnp.zeros_like(pos); hi = jnp.full_like(pos, total)
    for d in range(starts_ref.shape[1]):
        s = starts_ref[0, d]
        lo = jnp.where(s <= pos, jnp.maximum(lo, s), lo)
        hi = jnp.where(s > pos, jnp.minimum(hi, s), hi)
    return lo, hi

def dot(a, b):
    return lax.dot_general(a, b, (((1,), (0,)), ((), ())), preferred_element_type=f32)

def dot_first(a, b):
    return lax.dot_general(a, b, (((0,), (0,)), ((), ())), preferred_element_type=f32)

def turned(a):
    return a.astype(f32).T.astype(bf)

def fwd_kernel(heads, bq, bk, starts, qT, kT, vT, oT, mix, lse, acc, ml):
    total = kT.shape[1]
    toks = mix.shape[2]
    i = pl.program_id(0)
    q0 = i * bq
    first, _ = doc_bounds(starts, jnp.int32(q0), total)
    _, last = doc_bounds(starts, jnp.int32(q0 + bq - 1), total)
    pos = q0 + lax.broadcasted_iota(jnp.int32, (1, bq), 1)
    lo, hi = doc_bounds(starts, pos, total)
    kb0 = first // bk
    kb1 = (last + bk - 1) // bk
    acc[...] = jnp.zeros_like(acc)
    ml[0] = jnp.full((heads, bq), -1e30, f32)
    ml[1] = jnp.zeros((heads, bq), f32)
    kio = lax.broadcasted_iota(jnp.int32, (bk, bq), 0)
    def body(j, _):
        ks = pl.multiple_of(j * bk, bk)
        mask = (kio >= lo - ks) & (kio < hi - ks)
        for h in range(heads):
            sl = slice(HD * h, HD * (h + 1))
            s = dot_first(kT[sl, pl.ds(ks, bk)], qT[sl, :])
            s = jnp.where(mask, s, -1e30)
            m_old = ml[0, h:h + 1]
            m = jnp.maximum(m_old, jnp.max(s, axis=0, keepdims=True))
            p = jnp.exp(s - m)
            al = jnp.exp(m_old - m)
            ml[0, h:h + 1] = m
            ml[1, h:h + 1] = ml[1, h:h + 1] * al + jnp.sum(p, axis=0, keepdims=True)
            acc[sl, :] = acc[sl, :] * al + dot(vT[sl, pl.ds(ks, bk)], p.astype(bf))
        return 0
    lax.fori_loop(kb0, kb1, body, 0)
    step = min(bq, 256)
    for h in range(heads):
        sl = slice(HD * h, HD * (h + 1))
        l = ml[1, h:h + 1]
        o = acc[sl, :] / l
        oT[sl, :] = o
        for t in range(0, bq, step):
            at = q0 + t
            mix[at // toks, sl, pl.ds(pl.multiple_of(at % toks, step), step)] = o[:, t:t + step].astype(bf)
        lse[h:h + 1, :] = ml[0, h:h + 1] + jnp.log(l)

def attn_fwd(starts, qkv, toks, bq, bk):
    width, total = qkv.shape[0] // 3, qkv.shape[1]
    heads = width // HD
    return pl.pallas_call(
        functools.partial(fwd_kernel, heads, bq, bk),
        grid=(total // bq,),
        in_specs=[pl.BlockSpec(memory_space=pltpu.SMEM),
                  pl.BlockSpec((width, bq), lambda i: (0, i)),
                  pl.BlockSpec((width, total), lambda i: (1, 0)),
                  pl.BlockSpec((width, total), lambda i: (2, 0))],
        out_specs=[pl.BlockSpec((width, bq), lambda i: (0, i)),
                   pl.BlockSpec((total // toks, width, toks), lambda i: (0, 0, 0)),
                   pl.BlockSpec((heads, bq), lambda i: (0, i))],
        out_shape=[jax.ShapeDtypeStruct((width, total), f32),
                   jax.ShapeDtypeStruct((total // toks, width, toks), bf),
                   jax.ShapeDtypeStruct((heads, total), f32)],
        scratch_shapes=[pltpu.VMEM((width, bq), f32), pltpu.VMEM((2, heads, bq), f32)],
        cost_estimate=pl.CostEstimate(flops=8 * width * total * total, bytes_accessed=8 * width * total, transcendentals=0),
        name="attn_fwd",
    )(starts, qkv, qkv, qkv)

def bwd_kernel(heads, bq, bk, starts, qT, kT, vT, doT, oT, lse, dT, q3, do3, delta, dqa, dka, dva):
    width, total = qT.shape
    toks = doT.shape[2]
    i = pl.program_id(0)
    k0 = pl.multiple_of(i * bk, bk)
    @pl.when(i == 0)
    def _():
        dqa[...] = jnp.zeros_like(dqa)
        for h in range(heads):
            sl = slice(HD * h, HD * (h + 1))
            for b in range(doT.shape[0]):
                at = slice(b * toks, (b + 1) * toks)
                delta[h:h + 1, at] = jnp.sum(doT[b, sl, :].astype(f32) * oT[sl, at], axis=0, keepdims=True)
                q3[h, at, :] = turned(qT[sl, at])
                do3[h, at, :] = turned(doT[b, sl, :])
    first, _ = doc_bounds(starts, jnp.int32(k0), total)
    _, last = doc_bounds(starts, jnp.int32(k0 + bk - 1), total)
    qb0 = first // bq
    qb1 = (last + bq - 1) // bq
    dka[...] = jnp.zeros_like(dka)
    dva[...] = jnp.zeros_like(dva)
    kio = k0 + lax.broadcasted_iota(jnp.int32, (bk, bq), 0)
    def body(j, _):
        qs = pl.multiple_of(j * bq, bq)
        pos = qs + lax.broadcasted_iota(jnp.int32, (1, bq), 1)
        lo, hi = doc_bounds(starts, pos, total)
        mask = (kio >= lo) & (kio < hi)
        for h in range(heads):
            sl = slice(HD * h, HD * (h + 1))
            s = dot_first(kT[sl, :], qT[sl, pl.ds(qs, bq)])
            p = jnp.exp(jnp.where(mask, s - lse[h:h + 1, pl.ds(qs, bq)], -1e30))
            dp = dot_first(vT[sl, :], doT[qs // toks, sl, pl.ds(pl.multiple_of(qs % toks, bq), bq)])
            ds = p * (dp - delta[h:h + 1, pl.ds(qs, bq)])
            dsb = ds.astype(bf)
            dva[h] += dot(p.astype(bf), do3[h, pl.ds(qs, bq), :])
            dka[h] += dot(dsb, q3[h, pl.ds(qs, bq), :])
            dqa[sl, pl.ds(qs, bq)] += dot(kT[sl, :], dsb)
        return 0
    lax.fori_loop(qb0, qb1, body, 0)
    for h in range(heads):
        dT[width + HD * h:width + HD * (h + 1), pl.ds(k0, bk)] = dka[h].T.astype(bf)
        dT[2 * width + HD * h:2 * width + HD * (h + 1), pl.ds(k0, bk)] = dva[h].T.astype(bf)
    @pl.when(i == pl.num_programs(0) - 1)
    def _():
        dT[0:width, :] = (dqa[...] * (HD ** -0.5)).astype(bf)

def attn_bwd(starts, qkv, doT, oT, lse, bq, bk):
    width, total = qkv.shape[0] // 3, qkv.shape[1]
    heads = width // HD
    full = lambda a: pl.BlockSpec(a.shape, lambda i: (0,) * a.ndim)
    return pl.pallas_call(
        functools.partial(bwd_kernel, heads, bq, bk),
        grid=(total // bk,),
        in_specs=[pl.BlockSpec(memory_space=pltpu.SMEM),
                  pl.BlockSpec((width, total), lambda i: (0, 0)), pl.BlockSpec((width, bk), lambda i: (1, i)),
                  pl.BlockSpec((width, bk), lambda i: (2, i)), full(doT), full(oT), full(lse)],
        out_specs=pl.BlockSpec(qkv.shape, lambda i: (0, 0)),
        out_shape=jax.ShapeDtypeStruct(qkv.shape, bf),
        scratch_shapes=[pltpu.VMEM((heads, total, HD), bf), pltpu.VMEM((heads, total, HD), bf),
                        pltpu.VMEM((heads, total), f32), pltpu.VMEM((width, total), f32),
                        pltpu.VMEM((heads, bk, HD), f32), pltpu.VMEM((heads, bk, HD), f32)],
        cost_estimate=pl.CostEstimate(flops=8 * width * total * total, bytes_accessed=8 * width * total, transcendentals=0),
        name="attn_bwd",
    )(starts, qkv, qkv, qkv, doT, oT, lse)


MESH = pl.DeviceIdType.MESH


class Wire:
    def __init__(self, send, recv):
        self.send, self.recv, self.used, self.open = send, recv, 0, []

    def slot(self):
        self.used += 1
        return self.used - 1

    def start(self, slot, src, dst, device):
        copy = pltpu.make_async_remote_copy(
            src_ref=src, dst_ref=dst, send_sem=self.send.at[slot], recv_sem=self.recv.at[slot],
            device_id=device, device_id_type=MESH,
        )
        copy.start()
        self.open.append(copy)
        return copy

    def arrived(self, slot, dst, device):
        pltpu.make_async_remote_copy(
            src_ref=dst, dst_ref=dst, send_sem=self.send.at[slot], recv_sem=self.recv.at[slot],
            device_id=device, device_id_type=MESH,
        ).wait_recv()

    def sent(self, copy):
        copy.wait_send()
        self.open = [other for other in self.open if other is not copy]

    def drain(self):
        for copy in self.open:
            copy.wait_send()
        self.open = []


def grid_peers():
    shard, seq = lax.axis_index("wshard"), lax.axis_index("seq")
    z, y = shard // 2, shard % 2
    x, c = seq // 2, seq % 2
    at = lambda zz, yy, xx, cc: (zz * 2 + yy, xx * 2 + cc)
    along = [at((z + d) % 4, y, x, c) for d in range(4)]
    return z, y, x, c, along, at(z, 1 - y, x, c), at(z, y, 1 - x, c), at(z, y, x, 1 - c)


def greet(peers):
    barrier = pltpu.get_barrier_semaphore()
    for peer in peers:
        pl.semaphore_signal(barrier, inc=1, device_id=peer, device_id_type=MESH)
    pl.semaphore_wait(barrier, len(peers))


ORDER = (1, 3, 2)


def gather_kernel(b_ref, t_ref, q_ref, x_ref, send, recv, lsem):
    z, y, x, c, along, ypeer, xpeer, cpeer = grid_peers()
    own = z * 2 + y
    wire = Wire(send, recv)
    spot = lambda r, d: ((z + 4 - d) % 4) * 2 + (y if r == 0 else 1 - y)
    seq = x * 2 + c
    half = t_ref.shape[0] // 2
    parts = [pl.ds(0, half), pl.ds(half, half)]
    locals_ = [
        pltpu.make_async_copy(b_ref, q_ref.at[own], lsem.at[0]),
        pltpu.make_async_copy(t_ref, x_ref.at[seq], lsem.at[1]),
    ]
    for copy in locals_:
        copy.start()
    greet(along[1:] + [ypeer, xpeer, cpeer])
    zB = [wire.slot() for _ in range(4)]
    yB = [wire.slot() for _ in range(4)]
    tx, tc1 = [wire.slot() for _ in parts], [wire.slot() for _ in parts]
    tc0 = wire.slot()
    for slot, part in zip(tx, parts):
        wire.start(slot, t_ref.at[part], x_ref.at[seq, part], xpeer)
    for d in ORDER:
        wire.start(zB[d], b_ref, q_ref.at[own], along[d])
    wire.start(yB[0], b_ref, q_ref.at[own], ypeer)
    wire.start(tc0, t_ref, x_ref.at[seq], cpeer)
    for d in ORDER:
        w = spot(0, d)
        wire.arrived(zB[d], q_ref.at[w], along[d])
        wire.start(yB[d], q_ref.at[w], q_ref.at[w], ypeer)
    xtok = (1 - x) * 2 + c
    for i, part in enumerate(parts):
        wire.arrived(tx[i], x_ref.at[xtok, part], xpeer)
        wire.start(tc1[i], x_ref.at[xtok, part], x_ref.at[xtok, part], cpeer)
    for d in (0,) + ORDER:
        wire.arrived(yB[d], q_ref.at[spot(1, d)], ypeer)
    wire.arrived(tc0, x_ref.at[x * 2 + 1 - c], cpeer)
    for i, part in enumerate(parts):
        wire.arrived(tc1[i], x_ref.at[(1 - x) * 2 + 1 - c, part], cpeer)
    wire.drain()
    for copy in locals_:
        copy.wait()


def gather_inputs(b, tokens):
    slots = 13
    hbm = pl.BlockSpec(memory_space=pl.ANY)
    vmem = pl.BlockSpec(memory_space=pltpu.VMEM)
    return pl.pallas_call(
        gather_kernel,
        in_specs=[vmem] * 2, out_specs=[hbm] * 2,
        out_shape=[jax.ShapeDtypeStruct((8,) + b.shape, b.dtype), jax.ShapeDtypeStruct((4,) + tokens.shape, tokens.dtype)],
        scratch_shapes=[pltpu.SemaphoreType.DMA((slots,)), pltpu.SemaphoreType.DMA((slots,)), pltpu.SemaphoreType.DMA((2,))],
        compiler_params=pltpu.CompilerParams(collective_id=1, has_side_effects=True),
        name="gather_inputs",
    )(b, tokens)


def add_rows(dst, parts, rows, step=16):
    def body(i, _):
        at = pl.ds(pl.multiple_of(i * step, step), step)
        total = parts[0][at, :].astype(f32)
        for part in parts[1:]:
            total = total + part[at, :].astype(f32)
        dst[at, :] = total.astype(dst.dtype)
        return 0
    lax.fori_loop(0, rows // step, body, 0)


ALL = ORDER + (0,)


def reduce_kernel(ga, gb, dx, sm, fa, fb, fx, fr, fs, hb, ryb, rzb, rxc, hs, rys, rzs, s1, s2, s3, s4, rg, send, recv):
    z, y, x, c, along, ypeer, xpeer, cpeer = grid_peers()
    wire = Wire(send, recv)
    new = lambda count: [wire.slot() for _ in range(count)]
    kc, kx, kg, kyb, kys = new(4), new(2), new(2), wire.slot(), wire.slot()
    kzb, kzs, fin = new(4), new(4), new(8)
    zz = lambda d: (z + d) % 4
    half = dx.shape[2] // 2
    halves = [pl.ds(0, half), pl.ds(half, half)]
    sizes = [ga.shape[0] // 32 * 16, ga.shape[0] - ga.shape[0] // 32 * 16]
    pieces = [pl.ds(0, sizes[0]), pl.ds(sizes[0], sizes[1])]
    greet(along[1:] + [ypeer, xpeer, cpeer])
    for i, at in enumerate(halves):
        wire.start(kc[i], dx.at[1 - x, 1 - c, at], rxc.at[1 - x, at], cpeer)
    wire.start(kg[0], ga.at[pieces[0]], rg.at[pieces[0]], xpeer)
    wire.start(kys, sm.at[:, 1 - y], rys, ypeer)
    wire.start(kyb, gb.at[:, 1 - y], ryb, ypeer)
    for i, at in enumerate(halves):
        wire.start(kc[2 + i], dx.at[x, 1 - c, at], rxc.at[x, at], cpeer)
    for i, at in enumerate(halves):
        spot = rxc.at[1 - x, at]
        wire.arrived(kc[i], spot, cpeer)
        add_rows(spot, [dx.at[1 - x, c, at], spot], half)
        wire.start(kx[i], spot, fr.at[at], xpeer)
    wire.start(kg[1], ga.at[pieces[1]], rg.at[pieces[1]], xpeer)
    wire.arrived(kys, rys, ypeer)
    wire.arrived(kyb, ryb, ypeer)
    for d in ALL:
        hs[d] = sm[zz(d), y] + rys[zz(d)]
        add_rows(hb.at[d], [gb.at[zz(d), y], ryb.at[zz(d)]], hb.shape[1])
        if d:
            wire.start(kzs[d], hs.at[d], rzs.at[d], along[d])
            wire.start(kzb[d], hb.at[d], rzb.at[d], along[d])
    for i, at in enumerate(halves):
        wire.arrived(kc[2 + i], rxc.at[x, at], cpeer)
        add_rows(fx.at[at], [dx.at[x, c, at], rxc.at[x, at]], half)
    wire.arrived(kg[0], rg.at[pieces[0]], xpeer)
    add_rows(fa.at[c, pieces[0]], [ga.at[pieces[0]], rg.at[pieces[0]]], sizes[0])
    wire.start(fin[5], fa.at[c, pieces[0]], fa.at[c, pieces[0]], cpeer)
    for d in ORDER:
        wire.arrived(kzs[d], rzs.at[d], along[d])
        wire.arrived(kzb[d], rzb.at[d], along[d])
    s1[...] = hs[0] + rzs[1] + rzs[2] + rzs[3]
    wire.start(fin[0], s1, s2, xpeer)
    seq, xseq = 2 * x + c, 2 * (1 - x) + c
    add_rows(fb.at[seq], [hb.at[0]] + [rzb.at[d] for d in ORDER], hb.shape[1])
    wire.start(fin[1], fb.at[seq], fb.at[seq], xpeer)
    wire.start(fin[2], fb.at[seq], fb.at[seq], cpeer)
    for i, at in enumerate(halves):
        wire.arrived(kx[i], fr.at[at], xpeer)
    wire.arrived(kg[1], rg.at[pieces[1]], xpeer)
    add_rows(fa.at[c, pieces[1]], [ga.at[pieces[1]], rg.at[pieces[1]]], sizes[1])
    wire.start(fin[6], fa.at[c, pieces[1]], fa.at[c, pieces[1]], cpeer)
    wire.arrived(fin[0], s2, xpeer)
    s3[...] = s1[...] + s2[...]
    wire.start(fin[3], s3, s4, cpeer)
    wire.arrived(fin[1], fb.at[xseq], xpeer)
    wire.start(fin[4], fb.at[xseq], fb.at[xseq], cpeer)
    wire.arrived(fin[3], s4, cpeer)
    fs[...] = s3[...] + s4[...]
    wire.arrived(fin[2], fb.at[2 * x + 1 - c], cpeer)
    wire.arrived(fin[4], fb.at[2 * (1 - x) + 1 - c], cpeer)
    for i in range(2):
        wire.arrived(fin[5 + i], fa.at[1 - c, pieces[i]], cpeer)
    wire.drain()


def reduce_grads(ga, gb, dx, sm):
    rows, cols = ga.shape
    toks = dx.shape[1]
    vmem = pl.BlockSpec(memory_space=pltpu.VMEM)
    b0, b1 = gb.shape[1:]
    V = pltpu.VMEM
    sv = lambda *lead: V(lead + sm.shape[1:], f32)
    slots = 26
    return pl.pallas_call(
        reduce_kernel,
        in_specs=[vmem] * 4, out_specs=[vmem] * 5,
        out_shape=[jax.ShapeDtypeStruct((2, rows, cols), bf), jax.ShapeDtypeStruct((4, b0, b1), bf),
                   jax.ShapeDtypeStruct((toks, cols), bf), jax.ShapeDtypeStruct((toks, cols), bf),
                   jax.ShapeDtypeStruct(sm.shape[1:], f32)],
        scratch_shapes=[V((4, b0, b1), bf), V((4, b0, b1), bf), V((4, b0, b1), bf), V((2, toks, cols), bf),
                        sv(4), sv(4), sv(4), sv(), sv(), sv(), sv(), V((rows, cols), bf),
                        pltpu.SemaphoreType.DMA((slots,)), pltpu.SemaphoreType.DMA((slots,))],
        compiler_params=pltpu.CompilerParams(collective_id=2, has_side_effects=True, vmem_limit_bytes=40 * 2 ** 20),
        name="reduce_grads",
    )(ga, gb.reshape((4, 2) + gb.shape[1:]), dx.reshape((2, 2) + dx.shape[1:]), sm.reshape((4, 2) + sm.shape[1:]))


def mm(a, b, left, right):
    return lax.dot_general(a, b, (((left,), (right,)), ((), ())), preferred_element_type=f32)


def chunks(total, step, body):
    def run(i, _):
        body(pl.ds(pl.multiple_of(i * step, step), step))
        return 0
    lax.fori_loop(0, total // step, run, 0)


def ffn_kernel(n, r, step, mixed, tokens, cot, vec, big, out, dres, ga, dO, small,
               w_out, w_in, w_outer, stage, fb, gp, xh1, n1b, dh2, dm, du, acc, r1, got, lsem, gsem, send, recv):
    toks, model = tokens.shape
    wide = w_in.shape[0]
    per = n // wide
    z, y, x, c, along, ypeer, xpeer, cpeer = grid_peers()
    wire = Wire(send, recv)
    greet([cpeer])
    h = r // 2
    low = lambda size, side: pl.ds(pl.multiple_of(size * side, 16), size)
    def place(s, side, k):
        if k == 0:
            return w_out.at[s, low(h, side)]
        if k <= wide:
            return w_in.at[k - 1, s, low(h, side)]
        return w_outer.at[s // per, s % per, low(wide * h, side)]
    loads = [[] for _ in range(2 + wide)]
    for k in range(2 + wide):
        span = pl.ds(k * h, h if k <= wide else wide * h)
        for s in range(n):
            slot = wire.slot()
            load = pltpu.make_async_copy(big.at[s, span], place(s, c, k), lsem.at[slot])
            load.start()
            wire.start(slot, big.at[s, span], place(s, c, k), cpeer)
            loads[k].append((load, slot, place(s, 1 - c, k)))

    def ready(k):
        for load, slot, spot in loads[k]:
            load.wait()
            wire.arrived(slot, spot, cpeer)

    stores = []

    pending, swaps = [], []

    def finish():
        k, slot, groups, size, span, way = pending.pop()
        wire.arrived(way, got.at[k].reshape((groups, size, model)), cpeer)
        rows, strip = groups * size, min(size, 96)
        def body(i, _):
            at = i * strip
            mine = pl.ds(pl.multiple_of((at // size * 2 + c) * size + at % size, 16), strip)
            theirs = pl.ds(pl.multiple_of(at, 16), strip)
            stage[slot, mine, :] = (stage[slot, mine, :].astype(f32) + got[k, theirs, :].astype(f32)).astype(bf)
            return 0
        lax.fori_loop(0, rows // strip, body, 0)
        whole = stage.at[slot].reshape((groups, 2 * size, model))
        store = pltpu.make_async_copy(whole.at[:, low(size, c)], span, gsem.at[slot])
        store.start()
        stores.append(store)

    def put(value_rows, groups, span):
        k = len(swaps)
        slot = k % stage.shape[0]
        if k >= stage.shape[0]:
            wire.sent(swaps[k - stage.shape[0]])
            stores[k - stage.shape[0]].wait()
        def body(at):
            stage[slot, at, :] = value_rows(at).astype(bf)
        chunks(model, step, body)
        size = model // groups // 2
        way = wire.slot()
        whole = stage.at[slot].reshape((groups, 2 * size, model))
        swaps.append(wire.start(way, whole.at[:, low(size, 1 - c)], got.at[k].reshape((groups, size, model)), cpeer))
        if pending:
            finish()
        pending.append((k, slot, groups, size, span, way))

    flat = lambda ref: ref.reshape(model, model)
    row = lambda i: vec[i:i + 1, :]
    b_output, b_outer, g1, s1, g2, s2 = [row(i) for i in (2, 3, 4, 5, 6, 7)]
    small[...] = jnp.zeros_like(small)
    ready(0)
    wo = flat(w_out)

    def first(at):
        attn = mm(mixed[:, at], wo[...], 0, 0)
        z = tokens[at, :].astype(f32) + (attn + b_output)
        cen = z - jnp.mean(z, axis=-1, keepdims=True)
        inv = lax.rsqrt(jnp.mean(cen * cen, axis=-1, keepdims=True) + NORM_EPS)
        xh = cen * inv
        norm = xh * g1 + s1
        xh1[at, :] = xh
        n1b[at, :] = norm.astype(bf)
        r1[at, :] = jnp.broadcast_to(inv, (inv.shape[0], 128))
        acc[at, :] = norm + b_outer
    chunks(toks, step, first)
    for j in range(wide):
        ready(1 + j)
        wi = flat(w_in.at[j])
        bias = row(8 + j)
        def inner(at, j=j, wi=wi, bias=bias):
            u = mm(n1b[at, :], wi[...], 1, 0) + bias
            cdf = 0.5 * (1.0 + lax.erf(u * (0.5 ** 0.5)))
            pdf = jnp.exp(-0.5 * u * u) * 0.3989422804014327
            fb[j, at, :] = (u * cdf).astype(bf)
            gp[j, at, :] = cdf + u * pdf
        chunks(toks, step, inner)
    ready(1 + wide)
    for j in range(wide):
        wout = flat(w_outer.at[j])
        def outer(at, j=j, wout=wout):
            acc[at, :] += mm(fb[j, at, :], wout[...], 1, 0)
        chunks(toks, step, outer)

    def second(at):
        z = acc[at, :]
        cen = z - jnp.mean(z, axis=-1, keepdims=True)
        inv = lax.rsqrt(jnp.mean(cen * cen, axis=-1, keepdims=True) + NORM_EPS)
        xh = cen * inv
        out[at, :] = (xh * g2 + s2).astype(bf)
        g = cot[at, :].astype(f32)
        gx = g * xh
        gh = g * g2
        d = inv * (gh - jnp.mean(gh, axis=-1, keepdims=True) - xh * jnp.mean(gh * xh, axis=-1, keepdims=True))
        dh2[at, :] = d
        low = d.astype(bf)
        dm[at, :] = low
        small[6:7, :] += jnp.sum(gx, axis=0, keepdims=True)
        small[7:8, :] += jnp.sum(g, axis=0, keepdims=True)
        small[3:4, :] += jnp.sum(low.astype(f32), axis=0, keepdims=True)
    chunks(toks, step, second)
    for j in range(wide):
        wout = flat(w_outer.at[j])
        put(lambda at, j=j: mm(fb[j, :, at], dm[...], 0, 0), per, ga.at[pl.ds(j * per, per), pl.ds((1 + wide) * h, wide * h)])
        def dinner(at, j=j, wout=wout):
            low = (gp[j, at, :] * mm(dm[at, :], wout[...], 1, 1)).astype(bf)
            du[at, :] = low
            small[8 + j:9 + j, :] += jnp.sum(low.astype(f32), axis=0, keepdims=True)
        chunks(toks, step, dinner)
        wi = flat(w_in.at[j])
        def dfirst(at, wi=wi):
            dh2[at, :] += mm(du[at, :], wi[...], 1, 1)
        chunks(toks, step, dfirst)
        put(lambda at: mm(n1b[:, at], du[...], 0, 0), n, ga.at[:, pl.ds((1 + j) * h, h)])

    def last(at):
        d = dh2[at, :]
        xh = xh1[at, :]
        gh = d * g1
        inv = r1[at, 0:1]
        z = inv * (gh - jnp.mean(gh, axis=-1, keepdims=True) - xh * jnp.mean(gh * xh, axis=-1, keepdims=True))
        dres[at, :] = z
        low = z.astype(bf)
        dm[at, :] = low
        small[4:5, :] += jnp.sum(d * xh, axis=0, keepdims=True)
        small[5:6, :] += jnp.sum(d, axis=0, keepdims=True)
        small[2:3, :] += jnp.sum(low.astype(f32), axis=0, keepdims=True)
    chunks(toks, step, last)

    def back(at):
        dO[at, :] = mm(wo[at, :], dm[...], 1, 1).astype(bf)
    chunks(model, step, back)
    put(lambda at: mm(mixed[at, :], dm[...], 1, 0), n, ga.at[:, pl.ds(0, h)])
    finish()
    for store in stores[-stage.shape[0]:]:
        store.wait()
    wire.drain()


def ffn_block(mixed, tokens, cot, vec, big, step=384):
    n, half, model = big.shape
    r = model // n
    wide = (2 * half // r - 1) // 2
    toks = tokens.shape[0]
    vmem = pl.BlockSpec(memory_space=pltpu.VMEM)
    hbm = pl.BlockSpec(memory_space=pl.ANY)
    per = n // wide
    ohold = (per, wide * r, model) if per else (n, r, model)
    V = pltpu.VMEM
    sq = lambda dt, *lead: V(lead + (toks, model), dt)
    return pl.pallas_call(
        functools.partial(ffn_kernel, n, r, step),
        in_specs=[vmem] * 4 + [hbm],
        out_specs=[vmem, vmem, hbm, vmem, vmem],
        out_shape=[jax.ShapeDtypeStruct((toks, model), bf), jax.ShapeDtypeStruct((toks, model), f32),
                   jax.ShapeDtypeStruct((n, half, model), bf), jax.ShapeDtypeStruct((model, toks), bf),
                   jax.ShapeDtypeStruct((16, model), f32)],
        scratch_shapes=[V((n, r, model), bf), V((wide, n, r, model), bf), V((wide,) + ohold, bf), V((4, model, model), bf),
                        sq(bf, wide), sq(f32, wide), sq(f32), sq(bf), sq(f32), sq(bf), sq(bf), sq(f32),
                        V((toks, 128), f32), V((1 + 2 * wide, model // 2, model), bf), pltpu.SemaphoreType.DMA(((2 + wide) * n,)), pltpu.SemaphoreType.DMA((4,)),
                        pltpu.SemaphoreType.DMA(((2 + wide) * n + 1 + 2 * wide,)), pltpu.SemaphoreType.DMA(((2 + wide) * n + 1 + 2 * wide,))],
        compiler_params=pltpu.CompilerParams(collective_id=3, has_side_effects=True, vmem_limit_bytes=67043328),
        cost_estimate=pl.CostEstimate(flops=2 * toks * model * model * (3 + 6 * wide), bytes_accessed=8 * n * half * model, transcendentals=2 * toks * model * wide),
        name="ffn_block",
    )(mixed, tokens, cot, vec, big)


def layer_norm(inputs, norm_gain, norm_bias):
    row_mean = jnp.mean(inputs, axis=-1, keepdims=True)
    centred = inputs - row_mean
    row_var = jnp.mean(centred * centred, axis=-1, keepdims=True)
    return centred * lax.rsqrt(row_var + NORM_EPS) * norm_gain + norm_bias


def gelu_exact(inputs):
    return jax.nn.gelu(inputs, approximate=False)


def contract(left_in, right_in, left_dim, right_dim):
    return lax.dot_general(
        left_in,
        right_in,
        (((left_dim,), (right_dim,)), ((), ())),
        preferred_element_type=jnp.float32,
    )


def chips_of_two_by_four():
    return lax.axis_size("wshard") == 8 and lax.axis_size("seq") == 4


def reduce_parts(ga, gb, dx, sm):
    def scatter(part):
        return lax.psum_scatter(part, "wshard", scatter_dimension=0, tiled=False)

    if chips_of_two_by_four():
        return reduce_grads(scatter(ga), gb, dx, sm)

    fx = lax.psum_scatter(dx, "seq", scatter_dimension=0, tiled=False)
    return (
        lax.psum(scatter(ga), "seq")[None], lax.all_gather(scatter(gb), "seq"), fx, jnp.zeros_like(fx),
        lax.psum(scatter(sm), "seq"),
    )


def ffn_plain(mixed, tokens, cotangent, vec, big):
    shards_n, rows9, model = big.shape
    rows = model // shards_n
    wide = (rows9 // rows - 1) // 2
    bias_output, bias_outer, gain_one, shift_one, gain_two, shift_two = vec[2:8]
    bias_inner = vec[8:8 + wide].reshape(-1)
    output_full = big[:, :rows].reshape(model, model)
    inner_full = jnp.concatenate(
        [big[:, (1 + j) * rows:(2 + j) * rows].reshape(model, model) for j in range(wide)], axis=1
    )
    outer_full = big[:, (1 + wide) * rows:].reshape(-1, model)

    residual_in = tokens.astype(f32) + contract(mixed, output_full, 0, 0) + bias_output
    first_norm, first_back = jax.vjp(layer_norm, residual_in, gain_one, shift_one)
    first_low = first_norm.astype(bf)
    inner_act = jnp.dot(first_low, inner_full, preferred_element_type=f32) + bias_inner
    gelu_out, gelu_back = jax.vjp(gelu_exact, inner_act)
    gelu_low = gelu_out.astype(bf)
    second_in = first_norm + jnp.dot(gelu_low, outer_full, preferred_element_type=f32) + bias_outer
    layer_result, second_back = jax.vjp(layer_norm, second_in, gain_two, shift_two)
    d_second, grad_gain_two, grad_bias_two = second_back(cotangent.astype(f32))
    d_outer = d_second.astype(bf)
    grad_bias_outer = jnp.sum(d_outer.astype(f32), axis=0)
    grad_outer = contract(gelu_low, d_outer, 0, 0)
    (d_inner,) = gelu_back(contract(d_outer, outer_full, 1, 1))
    d_inner_low = d_inner.astype(bf)
    grad_bias_inner = jnp.sum(d_inner_low.astype(f32), axis=0)
    grad_inner = contract(first_low, d_inner_low, 0, 0)
    d_first = contract(d_inner_low, inner_full, 1, 1) + d_second
    d_resid, grad_gain_one, grad_bias_one = first_back(d_first)
    d_attn = d_resid.astype(bf)
    grad_bias_output = jnp.sum(d_attn.astype(f32), axis=0)
    grad_output = contract(mixed, d_attn, 1, 0)
    d_mixed = contract(output_full, d_attn, 1, 1).astype(bf)
    by_rows = lambda grad: grad.astype(bf).reshape(shards_n, -1, model)
    ga = jnp.concatenate(
        [by_rows(grad_output)] + [by_rows(grad_inner[:, j * model:(j + 1) * model]) for j in range(wide)]
        + [by_rows(grad_outer)], axis=1,
    )
    none = jnp.zeros((model,), f32)
    sums = jnp.concatenate([
        jnp.stack([none, none, grad_bias_output, grad_bias_outer, grad_gain_one, grad_bias_one, grad_gain_two, grad_bias_two]),
        grad_bias_inner.reshape(wide, model)], axis=0)
    return layer_result.astype(bf), d_resid, ga, d_mixed, sums


def shards(
    tokens, cotangent, starts,
    w_query, w_key, w_value, w_output, w_inner, w_outer,
    b_query, b_value, b_output, b_inner, b_outer,
    gain_first, bias_first, gain_second, bias_second,
):
    model = tokens.shape[1]
    rows = w_query.shape[0]
    shards_n = lax.axis_size("wshard")
    seq_n = lax.axis_size("seq")
    seq_i = lax.axis_index("seq")
    width = model // seq_n
    heads = width // HD
    wide = w_inner.shape[1] // model

    def own(columns):
        return lax.select_n(seq_i, *jnp.split(columns, seq_n, axis=columns.ndim - 1))

    smalls = (b_query, b_value, b_output, b_outer, gain_first, bias_first, gain_second, bias_second)
    small_cols = jnp.stack(smalls + tuple(b_inner.reshape(wide, rows)), axis=1)
    cols_n = small_cols.shape[1]
    b = jnp.concatenate([own(w_query), own(w_key), own(w_value), jnp.pad(small_cols, ((0, 0), (0, HD - cols_n)))], axis=1)
    fast = chips_of_two_by_four()

    def packed(share, part):
        cut = lambda w: lax.select_n(part == 1, *jnp.split(w, 2)) if share == 2 else w
        inner = cut(w_inner).reshape(rows // share, wide, model).transpose(1, 0, 2).reshape(-1, model)
        return jnp.concatenate([cut(w_output), inner, cut(w_outer)], axis=0)

    if fast:
        big = lax.all_gather(packed(2, seq_i % 2), "wshard")
        side, stream = gather_inputs(b, tokens)
    else:
        big = lax.all_gather(packed(1, 0), "wshard")
        side, stream = lax.all_gather(b, "wshard"), lax.all_gather(tokens, "seq")
    stream = stream.reshape(-1, model)
    side = side.reshape(model, -1)
    w_own = side[:, :3 * width]
    vectors = side[:, 3 * width:3 * width + cols_n].astype(f32).T
    bias_query, bias_value = vectors[:2]
    bias_inner = vectors[8:].reshape(wide, shards_n, rows).transpose(1, 0, 2).reshape(-1)
    scale = HD ** -0.5
    none = jnp.zeros((width,), f32)
    bias = jnp.concatenate([own(bias_query), none, own(bias_value)])
    factor = jnp.where(jnp.arange(3 * width) < width, scale, 1.0)
    qkv = ((contract(w_own, stream, 0, 1) + bias[:, None]) * factor[:, None]).astype(bf)
    oT, mix, lse = attn_fwd(starts, qkv, tokens.shape[0], 512, 512)
    mixed = lax.all_to_all(mix, "seq", split_axis=0, concat_axis=0).reshape(model, -1)

    vec = jnp.concatenate([vectors[:8], bias_inner.reshape(wide, model), jnp.zeros((4, model), f32)], axis=0)
    if fast:
        layer_result, d_resid, ga, d_mixed, sums = ffn_block(mixed, tokens, cotangent, vec, big)
    else:
        layer_result, d_resid, ga, d_mixed, sums = ffn_plain(mixed, tokens, cotangent, vec, big)
    doT = lax.all_to_all(d_mixed.reshape(seq_n, width, -1), "seq", split_axis=0, concat_axis=0)

    dT = attn_bwd(starts, qkv, doT, oT, lse, 256, 512)
    gb = contract(stream, dT, 0, 1).astype(bf).reshape(shards_n, rows, -1)
    dx = contract(dT, w_own, 0, 1).astype(bf).reshape(seq_n, -1, model)
    def spread(own_sum):
        return lax.dynamic_update_slice(jnp.zeros((model,), f32), own_sum, (seq_i * width,))

    d_bias = jnp.sum(dT.astype(f32), axis=1)
    small_rows = (
        spread(d_bias[:width]),
        spread(d_bias[2 * width:]),
        *sums[2:8],
    )
    sm = jnp.concatenate(
        [jnp.stack([row.reshape(shards_n, rows) for row in small_rows], axis=1),
         sums[8:8 + wide].reshape(shards_n, wide, rows)], axis=1,
    )
    sm = jnp.pad(sm, ((0, 0), (0, -cols_n % 8), (0, -rows % 128)))
    fa, fb, fx, fr, fs = reduce_parts(ga, gb, dx, sm)
    d_tokens = fx.astype(f32) + fr.astype(f32) + d_resid
    fb = fb.astype(f32)
    grads = [
        jnp.concatenate([fb[s, :, i * width:(i + 1) * width] for s in range(seq_n)], axis=1) for i in range(3)
    ]
    fa = fa.astype(f32)
    part = rows // fa.shape[0]
    span = lambda first, count: fa[:, first * part:(first + count) * part].reshape(-1, model)
    g_inner = jnp.concatenate([span(1 + j, 1) for j in range(wide)], axis=1)
    tail = [fs[i, :rows] for i in range(8)]
    g_b_inner = fs[8:8 + wide, :rows].reshape(-1)
    return (
        layer_result, d_tokens, *grads,
        span(0, 1), g_inner, span(1 + wide, wide),
        tail[0], tail[1], tail[2], g_b_inner, *tail[3:],
    )


def solution(mesh):
    placed = (
        P(("wshard", "seq"), None),
        P(("wshard", "seq"), None),
        P("wshard", None),
        P("wshard", None),
        P("wshard", None),
        P("wshard", None),
        P("wshard", None),
        P("wshard", None),
        P("wshard", None),
        P("wshard"),
        P("wshard"),
        P("wshard"),
        P("wshard"),
        P("wshard"),
        P("wshard"),
        P("wshard"),
        P("wshard"),
        P("wshard"),
    )
    return jax.shard_map(
        shards,
        mesh=mesh,
        in_specs=placed,
        out_specs=(
            P(("wshard", "seq"), None),
            P(("wshard", "seq"), None),
            P("wshard", None),
            P("wshard", None),
            P("wshard", None),
            P("wshard", None),
            P("wshard", None),
            P("wshard", None),
            P("wshard"),
            P("wshard"),
            P("wshard"),
            P("wshard"),
            P("wshard"),
            P("wshard"),
            P("wshard"),
            P("wshard"),
            P("wshard"),
        ),
        check_vma=False,
    )
```

```python
import functools

import jax
import jax.numpy as jnp
from jax import lax
from jax.experimental import pallas as pl
from jax.experimental.pallas import tpu as pltpu
from jax.sharding import PartitionSpec as P

NORM_EPS = 1e-05
HD = 64
bf = jnp.bfloat16
f32 = jnp.float32


def doc_bounds(starts_ref, pos, total):
    lo = jnp.zeros_like(pos); hi = jnp.full_like(pos, total)
    for d in range(starts_ref.shape[1]):
        s = starts_ref[0, d]
        lo = jnp.where(s <= pos, jnp.maximum(lo, s), lo)
        hi = jnp.where(s > pos, jnp.minimum(hi, s), hi)
    return lo, hi

def dot(a, b):
    return lax.dot_general(a, b, (((1,), (0,)), ((), ())), preferred_element_type=f32)

def dot_first(a, b):
    return lax.dot_general(a, b, (((0,), (0,)), ((), ())), preferred_element_type=f32)

def turned(a):
    return a.astype(f32).T.astype(bf)

def fwd_kernel(heads, bq, bk, starts, qT, kT, vT, oT, mix, lse, acc, ml):
    total = kT.shape[1]
    toks = mix.shape[2]
    i = pl.program_id(0)
    q0 = i * bq
    first, _ = doc_bounds(starts, jnp.int32(q0), total)
    _, last = doc_bounds(starts, jnp.int32(q0 + bq - 1), total)
    pos = q0 + lax.broadcasted_iota(jnp.int32, (1, bq), 1)
    lo, hi = doc_bounds(starts, pos, total)
    kb0 = first // bk
    kb1 = (last + bk - 1) // bk
    acc[...] = jnp.zeros_like(acc)
    ml[0] = jnp.full((heads, bq), -1e30, f32)
    ml[1] = jnp.zeros((heads, bq), f32)
    kio = lax.broadcasted_iota(jnp.int32, (bk, bq), 0)
    def body(j, _):
        ks = pl.multiple_of(j * bk, bk)
        mask = (kio >= lo - ks) & (kio < hi - ks)
        for h in range(heads):
            sl = slice(HD * h, HD * (h + 1))
            s = dot_first(kT[sl, pl.ds(ks, bk)], qT[sl, :])
            s = jnp.where(mask, s, -1e30)
            m_old = ml[0, h:h + 1]
            m = jnp.maximum(m_old, jnp.max(s, axis=0, keepdims=True))
            p = jnp.exp(s - m)
            al = jnp.exp(m_old - m)
            ml[0, h:h + 1] = m
            ml[1, h:h + 1] = ml[1, h:h + 1] * al + jnp.sum(p, axis=0, keepdims=True)
            acc[sl, :] = acc[sl, :] * al + dot(vT[sl, pl.ds(ks, bk)], p.astype(bf))
        return 0
    lax.fori_loop(kb0, kb1, body, 0)
    step = min(bq, 256)
    for h in range(heads):
        sl = slice(HD * h, HD * (h + 1))
        l = ml[1, h:h + 1]
        o = acc[sl, :] / l
        oT[sl, :] = o
        for t in range(0, bq, step):
            at = q0 + t
            mix[at // toks, sl, pl.ds(pl.multiple_of(at % toks, step), step)] = o[:, t:t + step].astype(bf)
        lse[h:h + 1, :] = ml[0, h:h + 1] + jnp.log(l)

def attn_fwd(starts, qkv, toks, bq, bk):
    width, total = qkv.shape[0] // 3, qkv.shape[1]
    heads = width // HD
    return pl.pallas_call(
        functools.partial(fwd_kernel, heads, bq, bk),
        grid=(total // bq,),
        in_specs=[pl.BlockSpec(memory_space=pltpu.SMEM),
                  pl.BlockSpec((width, bq), lambda i: (0, i)),
                  pl.BlockSpec((width, total), lambda i: (1, 0)),
                  pl.BlockSpec((width, total), lambda i: (2, 0))],
        out_specs=[pl.BlockSpec((width, bq), lambda i: (0, i)),
                   pl.BlockSpec((total // toks, width, toks), lambda i: (0, 0, 0)),
                   pl.BlockSpec((heads, bq), lambda i: (0, i))],
        out_shape=[jax.ShapeDtypeStruct((width, total), f32),
                   jax.ShapeDtypeStruct((total // toks, width, toks), bf),
                   jax.ShapeDtypeStruct((heads, total), f32)],
        scratch_shapes=[pltpu.VMEM((width, bq), f32), pltpu.VMEM((2, heads, bq), f32)],
        cost_estimate=pl.CostEstimate(flops=8 * width * total * total, bytes_accessed=8 * width * total, transcendentals=0),
        name="attn_fwd",
    )(starts, qkv, qkv, qkv)

def bwd_kernel(heads, bq, bk, starts, qT, kT, vT, doT, oT, lse, dT, q3, do3, delta, dqa, dka, dva):
    width, total = qT.shape
    toks = doT.shape[2]
    i = pl.program_id(0)
    k0 = pl.multiple_of(i * bk, bk)
    @pl.when(i == 0)
    def _():
        dqa[...] = jnp.zeros_like(dqa)
        for h in range(heads):
            sl = slice(HD * h, HD * (h + 1))
            for b in range(doT.shape[0]):
                at = slice(b * toks, (b + 1) * toks)
                delta[h:h + 1, at] = jnp.sum(doT[b, sl, :].astype(f32) * oT[sl, at], axis=0, keepdims=True)
                q3[h, at, :] = turned(qT[sl, at])
                do3[h, at, :] = turned(doT[b, sl, :])
    first, _ = doc_bounds(starts, jnp.int32(k0), total)
    _, last = doc_bounds(starts, jnp.int32(k0 + bk - 1), total)
    qb0 = first // bq
    qb1 = (last + bq - 1) // bq
    dka[...] = jnp.zeros_like(dka)
    dva[...] = jnp.zeros_like(dva)
    kio = k0 + lax.broadcasted_iota(jnp.int32, (bk, bq), 0)
    def body(j, _):
        qs = pl.multiple_of(j * bq, bq)
        pos = qs + lax.broadcasted_iota(jnp.int32, (1, bq), 1)
        lo, hi = doc_bounds(starts, pos, total)
        mask = (kio >= lo) & (kio < hi)
        for h in range(heads):
            sl = slice(HD * h, HD * (h + 1))
            s = dot_first(kT[sl, :], qT[sl, pl.ds(qs, bq)])
            p = jnp.exp(jnp.where(mask, s - lse[h:h + 1, pl.ds(qs, bq)], -1e30))
            dp = dot_first(vT[sl, :], doT[qs // toks, sl, pl.ds(pl.multiple_of(qs % toks, bq), bq)])
            ds = p * (dp - delta[h:h + 1, pl.ds(qs, bq)])
            dsb = ds.astype(bf)
            dva[h] += dot(p.astype(bf), do3[h, pl.ds(qs, bq), :])
            dka[h] += dot(dsb, q3[h, pl.ds(qs, bq), :])
            dqa[sl, pl.ds(qs, bq)] += dot(kT[sl, :], dsb)
        return 0
    lax.fori_loop(qb0, qb1, body, 0)
    for h in range(heads):
        dT[width + HD * h:width + HD * (h + 1), pl.ds(k0, bk)] = dka[h].T.astype(bf)
        dT[2 * width + HD * h:2 * width + HD * (h + 1), pl.ds(k0, bk)] = dva[h].T.astype(bf)
    @pl.when(i == pl.num_programs(0) - 1)
    def _():
        dT[0:width, :] = (dqa[...] * (HD ** -0.5)).astype(bf)

def attn_bwd(starts, qkv, doT, oT, lse, bq, bk):
    width, total = qkv.shape[0] // 3, qkv.shape[1]
    heads = width // HD
    full = lambda a: pl.BlockSpec(a.shape, lambda i: (0,) * a.ndim)
    return pl.pallas_call(
        functools.partial(bwd_kernel, heads, bq, bk),
        grid=(total // bk,),
        in_specs=[pl.BlockSpec(memory_space=pltpu.SMEM),
                  pl.BlockSpec((width, total), lambda i: (0, 0)), pl.BlockSpec((width, bk), lambda i: (1, i)),
                  pl.BlockSpec((width, bk), lambda i: (2, i)), full(doT), full(oT), full(lse)],
        out_specs=pl.BlockSpec(qkv.shape, lambda i: (0, 0)),
        out_shape=jax.ShapeDtypeStruct(qkv.shape, bf),
        scratch_shapes=[pltpu.VMEM((heads, total, HD), bf), pltpu.VMEM((heads, total, HD), bf),
                        pltpu.VMEM((heads, total), f32), pltpu.VMEM((width, total), f32),
                        pltpu.VMEM((heads, bk, HD), f32), pltpu.VMEM((heads, bk, HD), f32)],
        cost_estimate=pl.CostEstimate(flops=8 * width * total * total, bytes_accessed=8 * width * total, transcendentals=0),
        name="attn_bwd",
    )(starts, qkv, qkv, qkv, doT, oT, lse)


MESH = pl.DeviceIdType.MESH


class Wire:
    def __init__(self, send, recv):
        self.send, self.recv, self.used, self.open = send, recv, 0, []

    def slot(self):
        self.used += 1
        return self.used - 1

    def start(self, slot, src, dst, device):
        copy = pltpu.make_async_remote_copy(
            src_ref=src, dst_ref=dst, send_sem=self.send.at[slot], recv_sem=self.recv.at[slot],
            device_id=device, device_id_type=MESH,
        )
        copy.start()
        self.open.append(copy)
        return copy

    def arrived(self, slot, dst, device):
        pltpu.make_async_remote_copy(
            src_ref=dst, dst_ref=dst, send_sem=self.send.at[slot], recv_sem=self.recv.at[slot],
            device_id=device, device_id_type=MESH,
        ).wait_recv()

    def sent(self, copy):
        copy.wait_send()
        self.open = [other for other in self.open if other is not copy]

    def drain(self):
        for copy in self.open:
            copy.wait_send()
        self.open = []


def grid_peers():
    shard, seq = lax.axis_index("wshard"), lax.axis_index("seq")
    z, y = shard // 2, shard % 2
    x, c = seq // 2, seq % 2
    at = lambda zz, yy, xx, cc: (zz * 2 + yy, xx * 2 + cc)
    along = [at((z + d) % 4, y, x, c) for d in range(4)]
    return z, y, x, c, along, at(z, 1 - y, x, c), at(z, y, 1 - x, c), at(z, y, x, 1 - c)


def greet(peers):
    barrier = pltpu.get_barrier_semaphore()
    for peer in peers:
        pl.semaphore_signal(barrier, inc=1, device_id=peer, device_id_type=MESH)
    pl.semaphore_wait(barrier, len(peers))


ORDER = (1, 3, 2)


def gather_kernel(b_ref, t_ref, q_ref, x_ref, send, recv, lsem):
    z, y, x, c, along, ypeer, xpeer, cpeer = grid_peers()
    own = z * 2 + y
    wire = Wire(send, recv)
    spot = lambda r, d: ((z + 4 - d) % 4) * 2 + (y if r == 0 else 1 - y)
    seq = x * 2 + c
    half = t_ref.shape[0] // 2
    parts = [pl.ds(0, half), pl.ds(half, half)]
    locals_ = [
        pltpu.make_async_copy(b_ref, q_ref.at[own], lsem.at[0]),
        pltpu.make_async_copy(t_ref, x_ref.at[seq], lsem.at[1]),
    ]
    for copy in locals_:
        copy.start()
    greet(along[1:] + [ypeer, xpeer, cpeer])
    zB = [wire.slot() for _ in range(4)]
    yB = [wire.slot() for _ in range(4)]
    tx, tc1 = [wire.slot() for _ in parts], [wire.slot() for _ in parts]
    tc0 = wire.slot()
    for slot, part in zip(tx, parts):
        wire.start(slot, t_ref.at[part], x_ref.at[seq, part], xpeer)
    for d in ORDER:
        wire.start(zB[d], b_ref, q_ref.at[own], along[d])
    wire.start(yB[0], b_ref, q_ref.at[own], ypeer)
    wire.start(tc0, t_ref, x_ref.at[seq], cpeer)
    for d in ORDER:
        w = spot(0, d)
        wire.arrived(zB[d], q_ref.at[w], along[d])
        wire.start(yB[d], q_ref.at[w], q_ref.at[w], ypeer)
    xtok = (1 - x) * 2 + c
    for i, part in enumerate(parts):
        wire.arrived(tx[i], x_ref.at[xtok, part], xpeer)
        wire.start(tc1[i], x_ref.at[xtok, part], x_ref.at[xtok, part], cpeer)
    for d in (0,) + ORDER:
        wire.arrived(yB[d], q_ref.at[spot(1, d)], ypeer)
    wire.arrived(tc0, x_ref.at[x * 2 + 1 - c], cpeer)
    for i, part in enumerate(parts):
        wire.arrived(tc1[i], x_ref.at[(1 - x) * 2 + 1 - c, part], cpeer)
    wire.drain()
    for copy in locals_:
        copy.wait()


def gather_inputs(b, tokens):
    slots = 13
    hbm = pl.BlockSpec(memory_space=pl.ANY)
    vmem = pl.BlockSpec(memory_space=pltpu.VMEM)
    return pl.pallas_call(
        gather_kernel,
        in_specs=[vmem] * 2, out_specs=[hbm] * 2,
        out_shape=[jax.ShapeDtypeStruct((8,) + b.shape, b.dtype), jax.ShapeDtypeStruct((4,) + tokens.shape, tokens.dtype)],
        scratch_shapes=[pltpu.SemaphoreType.DMA((slots,)), pltpu.SemaphoreType.DMA((slots,)), pltpu.SemaphoreType.DMA((2,))],
        compiler_params=pltpu.CompilerParams(collective_id=1, has_side_effects=True),
        name="gather_inputs",
    )(b, tokens)


def add_rows(dst, parts, rows, step=16):
    def body(i, _):
        at = pl.ds(pl.multiple_of(i * step, step), step)
        total = parts[0][at, :].astype(f32)
        for part in parts[1:]:
            total = total + part[at, :].astype(f32)
        dst[at, :] = total.astype(dst.dtype)
        return 0
    lax.fori_loop(0, rows // step, body, 0)


ALL = ORDER + (0,)


def reduce_kernel(ga, gb, dx, sm, fa, fb, fx, fr, fs, hb, ryb, rzb, rxc, hs, rys, rzs, s1, s2, s3, s4, rg, gv, send, recv, lsem):
    z, y, x, c, along, ypeer, xpeer, cpeer = grid_peers()
    wire = Wire(send, recv)
    new = lambda count: [wire.slot() for _ in range(count)]
    kc, kx, kg, kyb, kys = new(4), new(2), new(2), wire.slot(), wire.slot()
    kzb, kzs, fin, kq = new(4), new(4), new(8), new(3)
    zz = lambda d: (z + d) % 4
    half = dx.shape[2] // 2
    halves = [pl.ds(0, half), pl.ds(half, half)]
    both = rg.shape[0]
    quarter = ga.shape[0] - both
    sizes = [both // 32 * 16, both - both // 32 * 16]
    pieces = [pl.ds(0, sizes[0]), pl.ds(sizes[0], sizes[1])]
    last = pl.ds(both, quarter)
    kept = lambda side: pl.ds(pl.multiple_of(both + quarter * side, 16), quarter)
    fetch = pltpu.make_async_copy(ga.at[pl.ds(0, both)], gv, lsem.at[0])
    keep = pltpu.make_async_copy(ga.at[last], fa.at[c, kept(x)], lsem.at[1])
    fetch.start()
    keep.start()
    greet(along[1:] + [ypeer, xpeer, cpeer])
    for i, at in enumerate(halves):
        wire.start(kc[i], dx.at[1 - x, 1 - c, at], rxc.at[1 - x, at], cpeer)
    wire.start(kg[0], ga.at[pieces[0]], rg.at[pieces[0]], xpeer)
    wire.start(kq[0], ga.at[last], fa.at[c, kept(x)], xpeer)
    wire.start(kys, sm.at[:, 1 - y], rys, ypeer)
    wire.start(kyb, gb.at[:, 1 - y], ryb, ypeer)
    for i, at in enumerate(halves):
        wire.start(kc[2 + i], dx.at[x, 1 - c, at], rxc.at[x, at], cpeer)
    wire.start(kq[1], ga.at[last], fa.at[c, kept(x)], cpeer)
    for i, at in enumerate(halves):
        spot = rxc.at[1 - x, at]
        wire.arrived(kc[i], spot, cpeer)
        add_rows(spot, [dx.at[1 - x, c, at], spot], half)
        wire.start(kx[i], spot, fr.at[at], xpeer)
    wire.start(kg[1], ga.at[pieces[1]], rg.at[pieces[1]], xpeer)
    wire.arrived(kys, rys, ypeer)
    wire.arrived(kyb, ryb, ypeer)
    for d in ALL:
        hs[d] = sm[zz(d), y] + rys[zz(d)]
        add_rows(hb.at[d], [gb.at[zz(d), y], ryb.at[zz(d)]], hb.shape[1])
        if d:
            wire.start(kzs[d], hs.at[d], rzs.at[d], along[d])
            wire.start(kzb[d], hb.at[d], rzb.at[d], along[d])
    for i, at in enumerate(halves):
        wire.arrived(kc[2 + i], rxc.at[x, at], cpeer)
        add_rows(fx.at[at], [dx.at[x, c, at], rxc.at[x, at]], half)
    fetch.wait()
    wire.arrived(kg[0], rg.at[pieces[0]], xpeer)
    add_rows(fa.at[c, pieces[0]], [gv.at[pieces[0]], rg.at[pieces[0]]], sizes[0])
    wire.start(fin[5], fa.at[c, pieces[0]], fa.at[c, pieces[0]], cpeer)
    wire.arrived(kq[0], fa.at[c, kept(1 - x)], xpeer)
    wire.start(kq[2], fa.at[c, kept(1 - x)], fa.at[c, kept(1 - x)], cpeer)
    for d in ORDER:
        wire.arrived(kzs[d], rzs.at[d], along[d])
        wire.arrived(kzb[d], rzb.at[d], along[d])
    s1[...] = hs[0] + rzs[1] + rzs[2] + rzs[3]
    wire.start(fin[0], s1, s2, xpeer)
    seq, xseq = 2 * x + c, 2 * (1 - x) + c
    add_rows(fb.at[seq], [hb.at[0]] + [rzb.at[d] for d in ORDER], hb.shape[1])
    wire.start(fin[1], fb.at[seq], fb.at[seq], xpeer)
    wire.start(fin[2], fb.at[seq], fb.at[seq], cpeer)
    for i, at in enumerate(halves):
        wire.arrived(kx[i], fr.at[at], xpeer)
    wire.arrived(kg[1], rg.at[pieces[1]], xpeer)
    add_rows(fa.at[c, pieces[1]], [gv.at[pieces[1]], rg.at[pieces[1]]], sizes[1])
    wire.start(fin[6], fa.at[c, pieces[1]], fa.at[c, pieces[1]], cpeer)
    wire.arrived(fin[0], s2, xpeer)
    s3[...] = s1[...] + s2[...]
    wire.start(fin[3], s3, s4, cpeer)
    wire.arrived(fin[1], fb.at[xseq], xpeer)
    wire.start(fin[4], fb.at[xseq], fb.at[xseq], cpeer)
    wire.arrived(fin[3], s4, cpeer)
    fs[...] = s3[...] + s4[...]
    wire.arrived(fin[2], fb.at[2 * x + 1 - c], cpeer)
    wire.arrived(fin[4], fb.at[2 * (1 - x) + 1 - c], cpeer)
    for i in range(2):
        wire.arrived(fin[5 + i], fa.at[1 - c, pieces[i]], cpeer)
    wire.arrived(kq[1], fa.at[1 - c, kept(x)], cpeer)
    wire.arrived(kq[2], fa.at[1 - c, kept(1 - x)], cpeer)
    keep.wait()
    wire.drain()


def reduce_grads(ga, gb, dx, sm, quarter):
    both, cols = ga.shape[0] - quarter, ga.shape[1]
    rows = both + 2 * quarter
    toks = dx.shape[1]
    vmem = pl.BlockSpec(memory_space=pltpu.VMEM)
    b0, b1 = gb.shape[1:]
    V = pltpu.VMEM
    sv = lambda *lead: V(lead + sm.shape[1:], f32)
    slots = 29
    return pl.pallas_call(
        reduce_kernel,
        in_specs=[pl.BlockSpec(memory_space=pl.ANY)] + [vmem] * 3, out_specs=[vmem] * 5,
        out_shape=[jax.ShapeDtypeStruct((2, rows, cols), bf), jax.ShapeDtypeStruct((4, b0, b1), bf),
                   jax.ShapeDtypeStruct((toks, cols), bf), jax.ShapeDtypeStruct((toks, cols), bf),
                   jax.ShapeDtypeStruct(sm.shape[1:], f32)],
        scratch_shapes=[V((4, b0, b1), bf), V((4, b0, b1), bf), V((4, b0, b1), bf), V((2, toks, cols), bf),
                        sv(4), sv(4), sv(4), sv(), sv(), sv(), sv(), V((both, cols), bf), V((both, cols), bf),
                        pltpu.SemaphoreType.DMA((slots,)), pltpu.SemaphoreType.DMA((slots,)),
                        pltpu.SemaphoreType.DMA((2,))],
        compiler_params=pltpu.CompilerParams(collective_id=2, has_side_effects=True, vmem_limit_bytes=40 * 2 ** 20),
        name="reduce_grads",
    )(ga, gb.reshape((4, 2) + gb.shape[1:]), dx.reshape((2, 2) + dx.shape[1:]), sm.reshape((4, 2) + sm.shape[1:]))


def mm(a, b, left, right):
    return lax.dot_general(a, b, (((left,), (right,)), ((), ())), preferred_element_type=f32)


def chunks(total, step, body):
    def run(i, _):
        body(pl.ds(pl.multiple_of(i * step, step), step))
        return 0
    lax.fori_loop(0, total // step, run, 0)


def ffn_kernel(n, r, step, mixed, tokens, cot, vec, big, out, dres, ga, dO, small,
               w_out, w_in, w_outer, stage, fb, gp, xh1, n1b, dh2, dm, du, acc, r1, got, mid, far, lsem, gsem, send, recv):
    toks, model = tokens.shape
    wide = w_in.shape[0]
    per = n // wide
    z, y, x, c, along, ypeer, xpeer, cpeer = grid_peers()
    wire = Wire(send, recv)
    greet([cpeer, xpeer])
    h = r // 2
    low = lambda size, side: pl.ds(pl.multiple_of(size * side, 16), size)
    def place(s, side, k):
        if k == 0:
            return w_out.at[s, low(h, side)]
        if k <= wide:
            return w_in.at[k - 1, s, low(h, side)]
        return w_outer.at[s // per, s % per, low(wide * h, side)]
    loads = [[] for _ in range(2 + wide)]
    for k in range(2 + wide):
        span = pl.ds(k * h, h if k <= wide else wide * h)
        for s in range(n):
            slot = wire.slot()
            load = pltpu.make_async_copy(big.at[s, span], place(s, c, k), lsem.at[slot])
            load.start()
            wire.start(slot, big.at[s, span], place(s, c, k), cpeer)
            loads[k].append((load, slot, place(s, 1 - c, k)))

    def ready(k):
        for load, slot, spot in loads[k]:
            load.wait()
            wire.arrived(slot, spot, cpeer)

    stores = {}

    pending, swaps, crossing = [], [], []
    q = wide * h // 2
    pair = lambda ref: ref.reshape((per, 2 * q, model))

    def finish():
        k, slot, groups, size, span, way = pending.pop()
        wire.arrived(way, got.at[k].reshape((groups, size, model)), cpeer)
        strip = min(size, r)
        across = len(crossing) if groups == per else None
        def body(i, _):
            at = i * strip
            mine = pl.ds(pl.multiple_of((at // size * 2 + c) * size + at % size, 16), strip)
            theirs = pl.ds(pl.multiple_of(at, 16), strip)
            total = (stage[slot, mine, :].astype(f32) + got[k, theirs, :].astype(f32)).astype(bf)
            if across is None:
                stage[slot, mine, :] = total
            else:
                mid[across, theirs, :] = total
            return 0
        lax.fori_loop(0, groups * size // strip, body, 0)
        if across is None:
            whole = stage.at[slot].reshape((groups, 2 * size, model))
            store = pltpu.make_async_copy(whole.at[:, low(size, c)], span, gsem.at[slot])
            store.start()
            stores[k] = store
        else:
            way = wire.slot()
            wire.start(way, pair(mid.at[across]).at[:, low(q, 1 - x)], far.at[across].reshape((per, q, model)), xpeer)
            crossing.append((way, span))

    def join(j):
        way, span = crossing[j]
        wire.arrived(way, far.at[j].reshape((per, q, model)), xpeer)
        for g in range(per):
            mine = pl.ds(pl.multiple_of(g * 2 * q + x * q, 16), q)
            mid[j, mine, :] = (mid[j, mine, :].astype(f32) + far[j, g * q:(g + 1) * q, :].astype(f32)).astype(bf)
        store = pltpu.make_async_copy(pair(mid.at[j]).at[:, low(q, x)], span, gsem.at[stage.shape[0] + j])
        store.start()
        return store

    def put(value_rows, groups, span):
        k = len(swaps)
        slot = k % stage.shape[0]
        if k >= stage.shape[0]:
            wire.sent(swaps[k - stage.shape[0]])
            if k - stage.shape[0] in stores:
                stores.pop(k - stage.shape[0]).wait()
        def body(at):
            stage[slot, at, :] = value_rows(at).astype(bf)
        chunks(model, step, body)
        size = model // groups // 2
        way = wire.slot()
        whole = stage.at[slot].reshape((groups, 2 * size, model))
        swaps.append(wire.start(way, whole.at[:, low(size, 1 - c)], got.at[k].reshape((groups, size, model)), cpeer))
        if pending:
            finish()
        pending.append((k, slot, groups, size, span, way))

    flat = lambda ref: ref.reshape(model, model)
    row = lambda i: vec[i:i + 1, :]
    b_output, b_outer, g1, s1, g2, s2 = [row(i) for i in (2, 3, 4, 5, 6, 7)]
    small[...] = jnp.zeros_like(small)
    ready(0)
    wo = flat(w_out)

    def first(at):
        attn = mm(mixed[:, at], wo[...], 0, 0)
        z = tokens[at, :].astype(f32) + (attn + b_output)
        cen = z - jnp.mean(z, axis=-1, keepdims=True)
        inv = lax.rsqrt(jnp.mean(cen * cen, axis=-1, keepdims=True) + NORM_EPS)
        xh = cen * inv
        norm = xh * g1 + s1
        xh1[at, :] = xh
        n1b[at, :] = norm.astype(bf)
        r1[at, :] = jnp.broadcast_to(inv, (inv.shape[0], 128))
        acc[at, :] = norm + b_outer
    chunks(toks, step, first)
    for j in range(wide):
        ready(1 + j)
        wi = flat(w_in.at[j])
        bias = row(8 + j)
        def inner(at, j=j, wi=wi, bias=bias):
            u = mm(n1b[at, :], wi[...], 1, 0) + bias
            cdf = 0.5 * (1.0 + lax.erf(u * (0.5 ** 0.5)))
            pdf = jnp.exp(-0.5 * u * u) * 0.3989422804014327
            fb[j, at, :] = (u * cdf).astype(bf)
            gp[j, at, :] = cdf + u * pdf
        chunks(toks, step, inner)
    ready(1 + wide)
    for j in range(wide):
        wout = flat(w_outer.at[j])
        def outer(at, j=j, wout=wout):
            acc[at, :] += mm(fb[j, at, :], wout[...], 1, 0)
        chunks(toks, step, outer)

    def second(at):
        z = acc[at, :]
        cen = z - jnp.mean(z, axis=-1, keepdims=True)
        inv = lax.rsqrt(jnp.mean(cen * cen, axis=-1, keepdims=True) + NORM_EPS)
        xh = cen * inv
        out[at, :] = (xh * g2 + s2).astype(bf)
        g = cot[at, :].astype(f32)
        gx = g * xh
        gh = g * g2
        d = inv * (gh - jnp.mean(gh, axis=-1, keepdims=True) - xh * jnp.mean(gh * xh, axis=-1, keepdims=True))
        dh2[at, :] = d
        low = d.astype(bf)
        dm[at, :] = low
        small[6:7, :] += jnp.sum(gx, axis=0, keepdims=True)
        small[7:8, :] += jnp.sum(g, axis=0, keepdims=True)
        small[3:4, :] += jnp.sum(low.astype(f32), axis=0, keepdims=True)
    chunks(toks, step, second)
    for j in range(wide):
        wout = flat(w_outer.at[j])
        put(lambda at, j=j: mm(fb[j, :, at], dm[...], 0, 0), per, ga.at[pl.ds(j * per, per), pl.ds((1 + wide) * h, q)])
        def dinner(at, j=j, wout=wout):
            low = (gp[j, at, :] * mm(dm[at, :], wout[...], 1, 1)).astype(bf)
            du[at, :] = low
            small[8 + j:9 + j, :] += jnp.sum(low.astype(f32), axis=0, keepdims=True)
        chunks(toks, step, dinner)
        wi = flat(w_in.at[j])
        def dfirst(at, wi=wi):
            dh2[at, :] += mm(du[at, :], wi[...], 1, 1)
        chunks(toks, step, dfirst)
        put(lambda at: mm(n1b[:, at], du[...], 0, 0), n, ga.at[:, pl.ds((1 + j) * h, h)])

    def last(at):
        d = dh2[at, :]
        xh = xh1[at, :]
        gh = d * g1
        inv = r1[at, 0:1]
        z = inv * (gh - jnp.mean(gh, axis=-1, keepdims=True) - xh * jnp.mean(gh * xh, axis=-1, keepdims=True))
        dres[at, :] = z
        low = z.astype(bf)
        dm[at, :] = low
        small[4:5, :] += jnp.sum(d * xh, axis=0, keepdims=True)
        small[5:6, :] += jnp.sum(d, axis=0, keepdims=True)
        small[2:3, :] += jnp.sum(low.astype(f32), axis=0, keepdims=True)
    chunks(toks, step, last)

    def back(at):
        dO[at, :] = mm(wo[at, :], dm[...], 1, 1).astype(bf)
    chunks(model, step, back)
    put(lambda at: mm(mixed[at, :], dm[...], 1, 0), n, ga.at[:, pl.ds(0, h)])
    finish()
    joined = [join(j) for j in range(wide)]
    for store in [*stores.values(), *joined]:
        store.wait()
    wire.drain()


def ffn_block(mixed, tokens, cot, vec, big, step=384):
    n, half, model = big.shape
    r = model // n
    wide = (2 * half // r - 1) // 2
    toks = tokens.shape[0]
    vmem = pl.BlockSpec(memory_space=pltpu.VMEM)
    hbm = pl.BlockSpec(memory_space=pl.ANY)
    per = n // wide
    ohold = (per, wide * r, model) if per else (n, r, model)
    V = pltpu.VMEM
    sq = lambda dt, *lead: V(lead + (toks, model), dt)
    return pl.pallas_call(
        functools.partial(ffn_kernel, n, r, step),
        in_specs=[vmem] * 4 + [hbm],
        out_specs=[vmem, vmem, hbm, vmem, vmem],
        out_shape=[jax.ShapeDtypeStruct((toks, model), bf), jax.ShapeDtypeStruct((toks, model), f32),
                   jax.ShapeDtypeStruct((n, half - wide * r // 4, model), bf), jax.ShapeDtypeStruct((model, toks), bf),
                   jax.ShapeDtypeStruct((16, model), f32)],
        scratch_shapes=[V((n, r, model), bf), V((wide, n, r, model), bf), V((wide,) + ohold, bf), V((4, model, model), bf),
                        sq(bf, wide), sq(f32, wide), sq(f32), sq(bf), sq(f32), sq(bf), sq(bf), sq(f32),
                        V((toks, 128), f32), V((1 + 2 * wide, model // 2, model), bf),
                        V((wide, model // 2, model), bf), V((wide, model // 4, model), bf), pltpu.SemaphoreType.DMA(((2 + wide) * n,)), pltpu.SemaphoreType.DMA((4 + wide,)),
                        pltpu.SemaphoreType.DMA(((2 + wide) * n + 1 + 3 * wide,)), pltpu.SemaphoreType.DMA(((2 + wide) * n + 1 + 3 * wide,))],
        compiler_params=pltpu.CompilerParams(collective_id=3, has_side_effects=True, vmem_limit_bytes=67043328),
        cost_estimate=pl.CostEstimate(flops=2 * toks * model * model * (3 + 6 * wide), bytes_accessed=8 * n * half * model, transcendentals=2 * toks * model * wide),
        name="ffn_block",
    )(mixed, tokens, cot, vec, big)


def layer_norm(inputs, norm_gain, norm_bias):
    row_mean = jnp.mean(inputs, axis=-1, keepdims=True)
    centred = inputs - row_mean
    row_var = jnp.mean(centred * centred, axis=-1, keepdims=True)
    return centred * lax.rsqrt(row_var + NORM_EPS) * norm_gain + norm_bias


def gelu_exact(inputs):
    return jax.nn.gelu(inputs, approximate=False)


def contract(left_in, right_in, left_dim, right_dim):
    return lax.dot_general(
        left_in,
        right_in,
        (((left_dim,), (right_dim,)), ((), ())),
        preferred_element_type=jnp.float32,
    )


def chips_of_two_by_four():
    return lax.axis_size("wshard") == 8 and lax.axis_size("seq") == 4


def reduce_parts(ga, gb, dx, sm, quarter):
    def scatter(part):
        return lax.psum_scatter(part, "wshard", scatter_dimension=0, tiled=False)

    if chips_of_two_by_four():
        return reduce_grads(scatter(ga), gb, dx, sm, quarter)

    fx = lax.psum_scatter(dx, "seq", scatter_dimension=0, tiled=False)
    return (
        lax.psum(scatter(ga), "seq")[None], lax.all_gather(scatter(gb), "seq"), fx, jnp.zeros_like(fx),
        lax.psum(scatter(sm), "seq"),
    )


def ffn_plain(mixed, tokens, cotangent, vec, big):
    shards_n, rows9, model = big.shape
    rows = model // shards_n
    wide = (rows9 // rows - 1) // 2
    bias_output, bias_outer, gain_one, shift_one, gain_two, shift_two = vec[2:8]
    bias_inner = vec[8:8 + wide].reshape(-1)
    output_full = big[:, :rows].reshape(model, model)
    inner_full = jnp.concatenate(
        [big[:, (1 + j) * rows:(2 + j) * rows].reshape(model, model) for j in range(wide)], axis=1
    )
    outer_full = big[:, (1 + wide) * rows:].reshape(-1, model)

    residual_in = tokens.astype(f32) + contract(mixed, output_full, 0, 0) + bias_output
    first_norm, first_back = jax.vjp(layer_norm, residual_in, gain_one, shift_one)
    first_low = first_norm.astype(bf)
    inner_act = jnp.dot(first_low, inner_full, preferred_element_type=f32) + bias_inner
    gelu_out, gelu_back = jax.vjp(gelu_exact, inner_act)
    gelu_low = gelu_out.astype(bf)
    second_in = first_norm + jnp.dot(gelu_low, outer_full, preferred_element_type=f32) + bias_outer
    layer_result, second_back = jax.vjp(layer_norm, second_in, gain_two, shift_two)
    d_second, grad_gain_two, grad_bias_two = second_back(cotangent.astype(f32))
    d_outer = d_second.astype(bf)
    grad_bias_outer = jnp.sum(d_outer.astype(f32), axis=0)
    grad_outer = contract(gelu_low, d_outer, 0, 0)
    (d_inner,) = gelu_back(contract(d_outer, outer_full, 1, 1))
    d_inner_low = d_inner.astype(bf)
    grad_bias_inner = jnp.sum(d_inner_low.astype(f32), axis=0)
    grad_inner = contract(first_low, d_inner_low, 0, 0)
    d_first = contract(d_inner_low, inner_full, 1, 1) + d_second
    d_resid, grad_gain_one, grad_bias_one = first_back(d_first)
    d_attn = d_resid.astype(bf)
    grad_bias_output = jnp.sum(d_attn.astype(f32), axis=0)
    grad_output = contract(mixed, d_attn, 1, 0)
    d_mixed = contract(output_full, d_attn, 1, 1).astype(bf)
    by_rows = lambda grad: grad.astype(bf).reshape(shards_n, -1, model)
    ga = jnp.concatenate(
        [by_rows(grad_output)] + [by_rows(grad_inner[:, j * model:(j + 1) * model]) for j in range(wide)]
        + [by_rows(grad_outer)], axis=1,
    )
    none = jnp.zeros((model,), f32)
    sums = jnp.concatenate([
        jnp.stack([none, none, grad_bias_output, grad_bias_outer, grad_gain_one, grad_bias_one, grad_gain_two, grad_bias_two]),
        grad_bias_inner.reshape(wide, model), jnp.zeros((4, model), f32)], axis=0)
    return layer_result.astype(bf), d_resid, ga, d_mixed, sums


def shards(
    tokens, cotangent, starts,
    w_query, w_key, w_value, w_output, w_inner, w_outer,
    b_query, b_value, b_output, b_inner, b_outer,
    gain_first, bias_first, gain_second, bias_second,
):
    model = tokens.shape[1]
    rows = w_query.shape[0]
    shards_n = lax.axis_size("wshard")
    seq_n = lax.axis_size("seq")
    seq_i = lax.axis_index("seq")
    width = model // seq_n
    heads = width // HD
    wide = w_inner.shape[1] // model

    def own(columns):
        return lax.select_n(seq_i, *jnp.split(columns, seq_n, axis=columns.ndim - 1))

    smalls = (b_query, b_value, b_output, b_outer, gain_first, bias_first, gain_second, bias_second)
    small_cols = jnp.stack(smalls + tuple(b_inner.reshape(wide, rows)), axis=1)
    cols_n = small_cols.shape[1]
    b = jnp.concatenate([own(w_query), own(w_key), own(w_value), jnp.pad(small_cols, ((0, 0), (0, HD - cols_n)))], axis=1)
    fast = chips_of_two_by_four()

    def packed(share, part):
        cut = lambda w: lax.select_n(part == 1, *jnp.split(w, 2)) if share == 2 else w
        inner = cut(w_inner).reshape(rows // share, wide, model).transpose(1, 0, 2).reshape(-1, model)
        return jnp.concatenate([cut(w_output), inner, cut(w_outer)], axis=0)

    if fast:
        big = lax.all_gather(packed(2, seq_i % 2), "wshard")
        side, stream = gather_inputs(b, tokens)
    else:
        big = lax.all_gather(packed(1, 0), "wshard")
        side, stream = lax.all_gather(b, "wshard"), lax.all_gather(tokens, "seq")
    stream = stream.reshape(-1, model)
    side = side.reshape(model, -1)
    w_own = side[:, :3 * width]
    vectors = side[:, 3 * width:3 * width + cols_n].astype(f32).T
    bias_query, bias_value = vectors[:2]
    bias_inner = vectors[8:].reshape(wide, shards_n, rows).transpose(1, 0, 2).reshape(-1)
    scale = HD ** -0.5
    none = jnp.zeros((width,), f32)
    bias = jnp.concatenate([own(bias_query), none, own(bias_value)])
    factor = jnp.where(jnp.arange(3 * width) < width, scale, 1.0)
    qkv = ((contract(w_own, stream, 0, 1) + bias[:, None]) * factor[:, None]).astype(bf)
    oT, mix, lse = attn_fwd(starts, qkv, tokens.shape[0], 512, 512)
    mixed = lax.all_to_all(mix, "seq", split_axis=0, concat_axis=0).reshape(model, -1)

    vec = jnp.concatenate([vectors[:8], bias_inner.reshape(wide, model), jnp.zeros((4, model), f32)], axis=0)
    if fast:
        layer_result, d_resid, ga, d_mixed, sums = ffn_block(mixed, tokens, cotangent, vec, big)
    else:
        layer_result, d_resid, ga, d_mixed, sums = ffn_plain(mixed, tokens, cotangent, vec, big)
    doT = lax.all_to_all(d_mixed.reshape(seq_n, width, -1), "seq", split_axis=0, concat_axis=0)

    dT = attn_bwd(starts, qkv, doT, oT, lse, 256, 512)
    gb = contract(stream, dT, 0, 1).astype(bf).reshape(shards_n, rows, -1)
    dx = contract(dT, w_own, 0, 1).astype(bf).reshape(seq_n, -1, model)
    d_bias = contract(jnp.ones((8, dT.shape[1]), bf), dT, 1, 1)[:1]
    column = lax.broadcasted_iota(jnp.int32, (1, model), 1)
    spread = lambda own_sum: jnp.where(column // width == seq_i, jnp.tile(own_sum, (1, seq_n)), 0.0)
    row = lax.broadcasted_iota(jnp.int32, (sums.shape[0], 1), 0)
    sums = jnp.where(row == 0, spread(d_bias[:, :width]), jnp.where(row == 1, spread(d_bias[:, 2 * width:]), sums))
    sm = jnp.concatenate(
        [sums[:8].reshape(8, shards_n, rows).transpose(1, 0, 2), sums[8:8 + wide].reshape(shards_n, wide, rows)], axis=1,
    )
    sm = jnp.pad(sm, ((0, 0), (0, -cols_n % 8), (0, -rows % 128)))
    fa, fb, fx, fr, fs = reduce_parts(ga, gb, dx, sm, wide * rows // 4)
    d_tokens = fx.astype(f32) + fr.astype(f32) + d_resid
    fb = fb.astype(f32)
    grads = [
        jnp.concatenate([fb[s, :, i * width:(i + 1) * width] for s in range(seq_n)], axis=1) for i in range(3)
    ]
    fa = fa.astype(f32)
    part = rows // fa.shape[0]
    span = lambda first, count: fa[:, first * part:(first + count) * part].reshape(-1, model)
    g_inner = jnp.concatenate([span(1 + j, 1) for j in range(wide)], axis=1)
    tail = [fs[i, :rows] for i in range(8)]
    g_b_inner = fs[8:8 + wide, :rows].reshape(-1)
    return (
        layer_result, d_tokens, *grads,
        span(0, 1), g_inner, span(1 + wide, wide),
        tail[0], tail[1], tail[2], g_b_inner, *tail[3:],
    )


def solution(mesh):
    placed = (
        P(("wshard", "seq"), None),
        P(("wshard", "seq"), None),
        P("wshard", None),
        P("wshard", None),
        P("wshard", None),
        P("wshard", None),
        P("wshard", None),
        P("wshard", None),
        P("wshard", None),
        P("wshard"),
        P("wshard"),
        P("wshard"),
        P("wshard"),
        P("wshard"),
        P("wshard"),
        P("wshard"),
        P("wshard"),
        P("wshard"),
    )
    return jax.shard_map(
        shards,
        mesh=mesh,
        in_specs=placed,
        out_specs=(
            P(("wshard", "seq"), None),
            P(("wshard", "seq"), None),
            P("wshard", None),
            P("wshard", None),
            P("wshard", None),
            P("wshard", None),
            P("wshard", None),
            P("wshard", None),
            P("wshard"),
            P("wshard"),
            P("wshard"),
            P("wshard"),
            P("wshard"),
            P("wshard"),
            P("wshard"),
            P("wshard"),
            P("wshard"),
        ),
        check_vma=False,
    )
```

```python
import functools

import jax
import jax.numpy as jnp
from jax import lax
from jax.experimental import pallas as pl
from jax.experimental.pallas import tpu as pltpu
from jax.sharding import PartitionSpec as P

NORM_EPS = 1e-05
HD = 64
bf = jnp.bfloat16
f32 = jnp.float32


def doc_bounds(starts_ref, pos, total):
    lo = jnp.zeros_like(pos); hi = jnp.full_like(pos, total)
    for d in range(starts_ref.shape[1]):
        s = starts_ref[0, d]
        lo = jnp.where(s <= pos, jnp.maximum(lo, s), lo)
        hi = jnp.where(s > pos, jnp.minimum(hi, s), hi)
    return lo, hi

def dot(a, b):
    return lax.dot_general(a, b, (((1,), (0,)), ((), ())), preferred_element_type=f32)

def dot_first(a, b):
    return lax.dot_general(a, b, (((0,), (0,)), ((), ())), preferred_element_type=f32)

def turned(a):
    return a.astype(f32).T.astype(bf)

def fwd_kernel(heads, bq, bk, starts, qT, kT, vT, oT, mix, lse, acc, ml):
    total = kT.shape[1]
    toks = mix.shape[2]
    i = pl.program_id(0)
    q0 = i * bq
    first, _ = doc_bounds(starts, jnp.int32(q0), total)
    _, last = doc_bounds(starts, jnp.int32(q0 + bq - 1), total)
    pos = q0 + lax.broadcasted_iota(jnp.int32, (1, bq), 1)
    lo, hi = doc_bounds(starts, pos, total)
    kb0 = first // bk
    kb1 = (last + bk - 1) // bk
    acc[...] = jnp.zeros_like(acc)
    ml[0] = jnp.full((heads, bq), -1e30, f32)
    ml[1] = jnp.zeros((heads, bq), f32)
    kio = lax.broadcasted_iota(jnp.int32, (bk, bq), 0)
    def body(j, _):
        ks = pl.multiple_of(j * bk, bk)
        mask = (kio >= lo - ks) & (kio < hi - ks)
        for h in range(heads):
            sl = slice(HD * h, HD * (h + 1))
            s = dot_first(kT[sl, pl.ds(ks, bk)], qT[sl, :])
            s = jnp.where(mask, s, -1e30)
            m_old = ml[0, h:h + 1]
            m = jnp.maximum(m_old, jnp.max(s, axis=0, keepdims=True))
            p = jnp.exp(s - m)
            al = jnp.exp(m_old - m)
            ml[0, h:h + 1] = m
            ml[1, h:h + 1] = ml[1, h:h + 1] * al + jnp.sum(p, axis=0, keepdims=True)
            acc[sl, :] = acc[sl, :] * al + dot(vT[sl, pl.ds(ks, bk)], p.astype(bf))
        return 0
    lax.fori_loop(kb0, kb1, body, 0)
    step = min(bq, 256)
    for h in range(heads):
        sl = slice(HD * h, HD * (h + 1))
        l = ml[1, h:h + 1]
        o = acc[sl, :] / l
        oT[sl, :] = o
        for t in range(0, bq, step):
            at = q0 + t
            mix[at // toks, sl, pl.ds(pl.multiple_of(at % toks, step), step)] = o[:, t:t + step].astype(bf)
        lse[h:h + 1, :] = ml[0, h:h + 1] + jnp.log(l)

def attn_fwd(starts, qkv, toks, bq, bk):
    width, total = qkv.shape[0] // 3, qkv.shape[1]
    heads = width // HD
    return pl.pallas_call(
        functools.partial(fwd_kernel, heads, bq, bk),
        grid=(total // bq,),
        in_specs=[pl.BlockSpec(memory_space=pltpu.SMEM),
                  pl.BlockSpec((width, bq), lambda i: (0, i)),
                  pl.BlockSpec((width, total), lambda i: (1, 0)),
                  pl.BlockSpec((width, total), lambda i: (2, 0))],
        out_specs=[pl.BlockSpec((width, bq), lambda i: (0, i)),
                   pl.BlockSpec((total // toks, width, toks), lambda i: (0, 0, 0)),
                   pl.BlockSpec((heads, bq), lambda i: (0, i))],
        out_shape=[jax.ShapeDtypeStruct((width, total), f32),
                   jax.ShapeDtypeStruct((total // toks, width, toks), bf),
                   jax.ShapeDtypeStruct((heads, total), f32)],
        scratch_shapes=[pltpu.VMEM((width, bq), f32), pltpu.VMEM((2, heads, bq), f32)],
        cost_estimate=pl.CostEstimate(flops=8 * width * total * total, bytes_accessed=8 * width * total, transcendentals=0),
        name="attn_fwd",
    )(starts, qkv, qkv, qkv)

def bwd_kernel(heads, bq, bk, starts, qT, kT, vT, doT, oT, lse, dT, q3, do3, delta, dqa, dka, dva):
    width, total = qT.shape
    toks = doT.shape[2]
    i = pl.program_id(0)
    k0 = pl.multiple_of(i * bk, bk)
    @pl.when(i == 0)
    def _():
        dqa[...] = jnp.zeros_like(dqa)
        for h in range(heads):
            sl = slice(HD * h, HD * (h + 1))
            for b in range(doT.shape[0]):
                at = slice(b * toks, (b + 1) * toks)
                delta[h:h + 1, at] = jnp.sum(doT[b, sl, :].astype(f32) * oT[sl, at], axis=0, keepdims=True)
                q3[h, at, :] = turned(qT[sl, at])
                do3[h, at, :] = turned(doT[b, sl, :])
    first, _ = doc_bounds(starts, jnp.int32(k0), total)
    _, last = doc_bounds(starts, jnp.int32(k0 + bk - 1), total)
    qb0 = first // bq
    qb1 = (last + bq - 1) // bq
    dka[...] = jnp.zeros_like(dka)
    dva[...] = jnp.zeros_like(dva)
    kio = k0 + lax.broadcasted_iota(jnp.int32, (bk, bq), 0)
    def body(j, _):
        qs = pl.multiple_of(j * bq, bq)
        pos = qs + lax.broadcasted_iota(jnp.int32, (1, bq), 1)
        lo, hi = doc_bounds(starts, pos, total)
        mask = (kio >= lo) & (kio < hi)
        for h in range(heads):
            sl = slice(HD * h, HD * (h + 1))
            s = dot_first(kT[sl, :], qT[sl, pl.ds(qs, bq)])
            p = jnp.exp(jnp.where(mask, s - lse[h:h + 1, pl.ds(qs, bq)], -1e30))
            dp = dot_first(vT[sl, :], doT[qs // toks, sl, pl.ds(pl.multiple_of(qs % toks, bq), bq)])
            ds = p * (dp - delta[h:h + 1, pl.ds(qs, bq)])
            dsb = ds.astype(bf)
            dva[h] += dot(p.astype(bf), do3[h, pl.ds(qs, bq), :])
            dka[h] += dot(dsb, q3[h, pl.ds(qs, bq), :])
            dqa[sl, pl.ds(qs, bq)] += dot(kT[sl, :], dsb)
        return 0
    lax.fori_loop(qb0, qb1, body, 0)
    for h in range(heads):
        dT[width + HD * h:width + HD * (h + 1), pl.ds(k0, bk)] = dka[h].T.astype(bf)
        dT[2 * width + HD * h:2 * width + HD * (h + 1), pl.ds(k0, bk)] = dva[h].T.astype(bf)
    @pl.when(i == pl.num_programs(0) - 1)
    def _():
        dT[0:width, :] = (dqa[...] * (HD ** -0.5)).astype(bf)

def attn_bwd(starts, qkv, doT, oT, lse, bq, bk):
    width, total = qkv.shape[0] // 3, qkv.shape[1]
    heads = width // HD
    full = lambda a: pl.BlockSpec(a.shape, lambda i: (0,) * a.ndim)
    return pl.pallas_call(
        functools.partial(bwd_kernel, heads, bq, bk),
        grid=(total // bk,),
        in_specs=[pl.BlockSpec(memory_space=pltpu.SMEM),
                  pl.BlockSpec((width, total), lambda i: (0, 0)), pl.BlockSpec((width, bk), lambda i: (1, i)),
                  pl.BlockSpec((width, bk), lambda i: (2, i)), full(doT), full(oT), full(lse)],
        out_specs=pl.BlockSpec(qkv.shape, lambda i: (0, 0)),
        out_shape=jax.ShapeDtypeStruct(qkv.shape, bf),
        scratch_shapes=[pltpu.VMEM((heads, total, HD), bf), pltpu.VMEM((heads, total, HD), bf),
                        pltpu.VMEM((heads, total), f32), pltpu.VMEM((width, total), f32),
                        pltpu.VMEM((heads, bk, HD), f32), pltpu.VMEM((heads, bk, HD), f32)],
        cost_estimate=pl.CostEstimate(flops=8 * width * total * total, bytes_accessed=8 * width * total, transcendentals=0),
        name="attn_bwd",
    )(starts, qkv, qkv, qkv, doT, oT, lse)


MESH = pl.DeviceIdType.MESH


class Wire:
    def __init__(self, send, recv):
        self.send, self.recv, self.used, self.open = send, recv, 0, []

    def slot(self):
        self.used += 1
        return self.used - 1

    def start(self, slot, src, dst, device):
        copy = pltpu.make_async_remote_copy(
            src_ref=src, dst_ref=dst, send_sem=self.send.at[slot], recv_sem=self.recv.at[slot],
            device_id=device, device_id_type=MESH,
        )
        copy.start()
        self.open.append(copy)
        return copy

    def arrived(self, slot, dst, device):
        pltpu.make_async_remote_copy(
            src_ref=dst, dst_ref=dst, send_sem=self.send.at[slot], recv_sem=self.recv.at[slot],
            device_id=device, device_id_type=MESH,
        ).wait_recv()

    def sent(self, copy):
        copy.wait_send()
        self.open = [other for other in self.open if other is not copy]

    def drain(self):
        for copy in self.open:
            copy.wait_send()
        self.open = []


def grid_peers():
    shard, seq = lax.axis_index("wshard"), lax.axis_index("seq")
    z, y = shard // 2, shard % 2
    x, c = seq // 2, seq % 2
    at = lambda zz, yy, xx, cc: (zz * 2 + yy, xx * 2 + cc)
    along = [at((z + d) % 4, y, x, c) for d in range(4)]
    return z, y, x, c, along, at(z, 1 - y, x, c), at(z, y, 1 - x, c), at(z, y, x, 1 - c)


def greet(peers):
    barrier = pltpu.get_barrier_semaphore()
    for peer in peers:
        pl.semaphore_signal(barrier, inc=1, device_id=peer, device_id_type=MESH)
    pl.semaphore_wait(barrier, len(peers))


ORDER = (1, 3, 2)


def gather_kernel(b_ref, t_ref, q_ref, x_ref, send, recv, lsem):
    z, y, x, c, along, ypeer, xpeer, cpeer = grid_peers()
    own = z * 2 + y
    wire = Wire(send, recv)
    spot = lambda r, d: ((z + 4 - d) % 4) * 2 + (y if r == 0 else 1 - y)
    seq = x * 2 + c
    half = t_ref.shape[0] // 2
    parts = [pl.ds(0, half), pl.ds(half, half)]
    locals_ = [
        pltpu.make_async_copy(b_ref, q_ref.at[own], lsem.at[0]),
        pltpu.make_async_copy(t_ref, x_ref.at[seq], lsem.at[1]),
    ]
    for copy in locals_:
        copy.start()
    greet(along[1:] + [ypeer, xpeer, cpeer])
    zB = [wire.slot() for _ in range(4)]
    yB = [wire.slot() for _ in range(4)]
    tx, tc1 = [wire.slot() for _ in parts], [wire.slot() for _ in parts]
    tc0 = wire.slot()
    for slot, part in zip(tx, parts):
        wire.start(slot, t_ref.at[part], x_ref.at[seq, part], xpeer)
    for d in ORDER:
        wire.start(zB[d], b_ref, q_ref.at[own], along[d])
    wire.start(yB[0], b_ref, q_ref.at[own], ypeer)
    wire.start(tc0, t_ref, x_ref.at[seq], cpeer)
    for d in ORDER:
        w = spot(0, d)
        wire.arrived(zB[d], q_ref.at[w], along[d])
        wire.start(yB[d], q_ref.at[w], q_ref.at[w], ypeer)
    xtok = (1 - x) * 2 + c
    for i, part in enumerate(parts):
        wire.arrived(tx[i], x_ref.at[xtok, part], xpeer)
        wire.start(tc1[i], x_ref.at[xtok, part], x_ref.at[xtok, part], cpeer)
    for d in (0,) + ORDER:
        wire.arrived(yB[d], q_ref.at[spot(1, d)], ypeer)
    wire.arrived(tc0, x_ref.at[x * 2 + 1 - c], cpeer)
    for i, part in enumerate(parts):
        wire.arrived(tc1[i], x_ref.at[(1 - x) * 2 + 1 - c, part], cpeer)
    wire.drain()
    for copy in locals_:
        copy.wait()


def gather_inputs(b, tokens):
    slots = 13
    hbm = pl.BlockSpec(memory_space=pl.ANY)
    vmem = pl.BlockSpec(memory_space=pltpu.VMEM)
    return pl.pallas_call(
        gather_kernel,
        in_specs=[vmem] * 2, out_specs=[hbm] * 2,
        out_shape=[jax.ShapeDtypeStruct((8,) + b.shape, b.dtype), jax.ShapeDtypeStruct((4,) + tokens.shape, tokens.dtype)],
        scratch_shapes=[pltpu.SemaphoreType.DMA((slots,)), pltpu.SemaphoreType.DMA((slots,)), pltpu.SemaphoreType.DMA((2,))],
        compiler_params=pltpu.CompilerParams(collective_id=1, has_side_effects=True),
        name="gather_inputs",
    )(b, tokens)


def add_rows(dst, parts, rows, step=16):
    def body(i, _):
        at = pl.ds(pl.multiple_of(i * step, step), step)
        total = parts[0][at, :].astype(f32)
        for part in parts[1:]:
            total = total + part[at, :].astype(f32)
        dst[at, :] = total.astype(dst.dtype)
        return 0
    lax.fori_loop(0, rows // step, body, 0)


ALL = ORDER + (0,)


def reduce_kernel(ga, gb, dx, sm, fa, fb, fx, fr, fs, hb, ryb, rzb, rxc, hs, rys, rzs, s1, s2, s3, s4, rg, gv, send, recv, lsem):
    z, y, x, c, along, ypeer, xpeer, cpeer = grid_peers()
    wire = Wire(send, recv)
    new = lambda count: [wire.slot() for _ in range(count)]
    kc, kx, kg, kyb, kys = new(4), new(2), new(2), wire.slot(), wire.slot()
    kzb, kzs, fin, kq = new(4), new(4), new(8), new(3)
    zz = lambda d: (z + d) % 4
    half = dx.shape[2] // 2
    halves = [pl.ds(0, half), pl.ds(half, half)]
    both = rg.shape[0]
    quarter = ga.shape[0] - both
    sizes = [both // 32 * 16, both - both // 32 * 16]
    pieces = [pl.ds(0, sizes[0]), pl.ds(sizes[0], sizes[1])]
    last = pl.ds(both, quarter)
    kept = lambda side: pl.ds(pl.multiple_of(both + quarter * side, 16), quarter)
    fetch = pltpu.make_async_copy(ga.at[pl.ds(0, both)], gv, lsem.at[0])
    keep = pltpu.make_async_copy(ga.at[last], fa.at[c, kept(x)], lsem.at[1])
    fetch.start()
    keep.start()
    greet(along[1:] + [ypeer, xpeer, cpeer])
    for i, at in enumerate(halves):
        wire.start(kc[i], dx.at[1 - x, 1 - c, at], rxc.at[1 - x, at], cpeer)
    wire.start(kg[0], ga.at[pieces[0]], rg.at[pieces[0]], xpeer)
    wire.start(kq[0], ga.at[last], fa.at[c, kept(x)], xpeer)
    wire.start(kys, sm.at[:, 1 - y], rys, ypeer)
    wire.start(kyb, gb.at[:, 1 - y], ryb, ypeer)
    for i, at in enumerate(halves):
        wire.start(kc[2 + i], dx.at[x, 1 - c, at], rxc.at[x, at], cpeer)
    wire.start(kq[1], ga.at[last], fa.at[c, kept(x)], cpeer)
    for i, at in enumerate(halves):
        spot = rxc.at[1 - x, at]
        wire.arrived(kc[i], spot, cpeer)
        add_rows(spot, [dx.at[1 - x, c, at], spot], half)
        wire.start(kx[i], spot, fr.at[at], xpeer)
    wire.start(kg[1], ga.at[pieces[1]], rg.at[pieces[1]], xpeer)
    wire.arrived(kys, rys, ypeer)
    wire.arrived(kyb, ryb, ypeer)
    for d in ALL:
        hs[d] = sm[zz(d), y] + rys[zz(d)]
        add_rows(hb.at[d], [gb.at[zz(d), y], ryb.at[zz(d)]], hb.shape[1])
        if d:
            wire.start(kzs[d], hs.at[d], rzs.at[d], along[d])
            wire.start(kzb[d], hb.at[d], rzb.at[d], along[d])
    for i, at in enumerate(halves):
        wire.arrived(kc[2 + i], rxc.at[x, at], cpeer)
        add_rows(fx.at[at], [dx.at[x, c, at], rxc.at[x, at]], half)
    fetch.wait()
    wire.arrived(kg[0], rg.at[pieces[0]], xpeer)
    add_rows(fa.at[c, pieces[0]], [gv.at[pieces[0]], rg.at[pieces[0]]], sizes[0])
    wire.start(fin[5], fa.at[c, pieces[0]], fa.at[c, pieces[0]], cpeer)
    wire.arrived(kq[0], fa.at[c, kept(1 - x)], xpeer)
    wire.start(kq[2], fa.at[c, kept(1 - x)], fa.at[c, kept(1 - x)], cpeer)
    for d in ORDER:
        wire.arrived(kzs[d], rzs.at[d], along[d])
        wire.arrived(kzb[d], rzb.at[d], along[d])
    s1[...] = hs[0] + rzs[1] + rzs[2] + rzs[3]
    wire.start(fin[0], s1, s2, xpeer)
    seq, xseq = 2 * x + c, 2 * (1 - x) + c
    add_rows(fb.at[seq], [hb.at[0]] + [rzb.at[d] for d in ORDER], hb.shape[1])
    wire.start(fin[1], fb.at[seq], fb.at[seq], xpeer)
    wire.start(fin[2], fb.at[seq], fb.at[seq], cpeer)
    for i, at in enumerate(halves):
        wire.arrived(kx[i], fr.at[at], xpeer)
    wire.arrived(kg[1], rg.at[pieces[1]], xpeer)
    add_rows(fa.at[c, pieces[1]], [gv.at[pieces[1]], rg.at[pieces[1]]], sizes[1])
    wire.start(fin[6], fa.at[c, pieces[1]], fa.at[c, pieces[1]], cpeer)
    wire.arrived(fin[0], s2, xpeer)
    s3[...] = s1[...] + s2[...]
    wire.start(fin[3], s3, s4, cpeer)
    wire.arrived(fin[1], fb.at[xseq], xpeer)
    wire.start(fin[4], fb.at[xseq], fb.at[xseq], cpeer)
    wire.arrived(fin[3], s4, cpeer)
    fs[...] = s3[...] + s4[...]
    wire.arrived(fin[2], fb.at[2 * x + 1 - c], cpeer)
    wire.arrived(fin[4], fb.at[2 * (1 - x) + 1 - c], cpeer)
    for i in range(2):
        wire.arrived(fin[5 + i], fa.at[1 - c, pieces[i]], cpeer)
    wire.arrived(kq[1], fa.at[1 - c, kept(x)], cpeer)
    wire.arrived(kq[2], fa.at[1 - c, kept(1 - x)], cpeer)
    keep.wait()
    wire.drain()


def reduce_grads(ga, gb, dx, sm, quarter):
    both, cols = ga.shape[0] - quarter, ga.shape[1]
    rows = both + 2 * quarter
    toks = dx.shape[1]
    vmem = pl.BlockSpec(memory_space=pltpu.VMEM)
    b0, b1 = gb.shape[1:]
    V = pltpu.VMEM
    sv = lambda *lead: V(lead + sm.shape[1:], f32)
    slots = 29
    return pl.pallas_call(
        reduce_kernel,
        in_specs=[pl.BlockSpec(memory_space=pl.ANY)] + [vmem] * 3, out_specs=[vmem] * 5,
        out_shape=[jax.ShapeDtypeStruct((2, rows, cols), bf), jax.ShapeDtypeStruct((4, b0, b1), bf),
                   jax.ShapeDtypeStruct((toks, cols), bf), jax.ShapeDtypeStruct((toks, cols), bf),
                   jax.ShapeDtypeStruct(sm.shape[1:], f32)],
        scratch_shapes=[V((4, b0, b1), bf), V((4, b0, b1), bf), V((4, b0, b1), bf), V((2, toks, cols), bf),
                        sv(4), sv(4), sv(4), sv(), sv(), sv(), sv(), V((both, cols), bf), V((both, cols), bf),
                        pltpu.SemaphoreType.DMA((slots,)), pltpu.SemaphoreType.DMA((slots,)),
                        pltpu.SemaphoreType.DMA((2,))],
        compiler_params=pltpu.CompilerParams(collective_id=2, has_side_effects=True, vmem_limit_bytes=40 * 2 ** 20),
        name="reduce_grads",
    )(ga, gb.reshape((4, 2) + gb.shape[1:]), dx.reshape((2, 2) + dx.shape[1:]), sm.reshape((4, 2) + sm.shape[1:]))


def mm(a, b, left, right):
    return lax.dot_general(a, b, (((left,), (right,)), ((), ())), preferred_element_type=f32)


def chunks(total, step, body):
    def run(i, _):
        body(pl.ds(pl.multiple_of(i * step, step), step))
        return 0
    lax.fori_loop(0, total // step, run, 0)


def ffn_kernel(n, r, step, mixed, tokens, cot, vec, big, out, dres, ga, dO, small,
               w_out, w_in, w_outer, stage, fb, gp, xh1, n1b, dh2, dm, du, acc, r1, got, mid, far, lsem, gsem, send, recv):
    toks, model = tokens.shape
    wide = w_in.shape[0]
    per = n // wide
    z, y, x, c, along, ypeer, xpeer, cpeer = grid_peers()
    wire = Wire(send, recv)
    greet([cpeer, xpeer])
    h = r // 2
    low = lambda size, side: pl.ds(pl.multiple_of(size * side, 16), size)
    def place(s, side, k):
        if k == 0:
            return w_out.at[s, low(h, side)]
        if k <= wide:
            return w_in.at[k - 1, s, low(h, side)]
        return w_outer.at[s // per, s % per, low(wide * h, side)]
    loads = [[] for _ in range(2 + wide)]
    for k in range(2 + wide):
        span = pl.ds(k * h, h if k <= wide else wide * h)
        for s in range(n):
            slot = wire.slot()
            load = pltpu.make_async_copy(big.at[s, span], place(s, c, k), lsem.at[slot])
            load.start()
            wire.start(slot, big.at[s, span], place(s, c, k), cpeer)
            loads[k].append((load, slot, place(s, 1 - c, k)))

    def ready(k):
        for load, slot, spot in loads[k]:
            load.wait()
            wire.arrived(slot, spot, cpeer)

    stores = {}

    pending, swaps, crossing = [], [], []
    q = wide * h // 2
    pair = lambda ref: ref.reshape((per, 2 * q, model))

    def finish():
        k, slot, groups, size, span, way = pending.pop()
        wire.arrived(way, got.at[k].reshape((groups, size, model)), cpeer)
        strip = min(size, r)
        across = len(crossing) if groups == per else None
        def body(i, _):
            at = i * strip
            mine = pl.ds(pl.multiple_of((at // size * 2 + c) * size + at % size, 16), strip)
            theirs = pl.ds(pl.multiple_of(at, 16), strip)
            total = (stage[slot, mine, :].astype(f32) + got[k, theirs, :].astype(f32)).astype(bf)
            if across is None:
                stage[slot, mine, :] = total
            else:
                mid[across, theirs, :] = total
            return 0
        lax.fori_loop(0, groups * size // strip, body, 0)
        if across is None:
            whole = stage.at[slot].reshape((groups, 2 * size, model))
            store = pltpu.make_async_copy(whole.at[:, low(size, c)], span, gsem.at[slot])
            store.start()
            stores[k] = store
        else:
            way = wire.slot()
            wire.start(way, pair(mid.at[across]).at[:, low(q, 1 - x)], far.at[across].reshape((per, q, model)), xpeer)
            crossing.append((way, span))

    def join(j):
        way, span = crossing[j]
        wire.arrived(way, far.at[j].reshape((per, q, model)), xpeer)
        for g in range(per):
            mine = pl.ds(pl.multiple_of(g * 2 * q + x * q, 16), q)
            mid[j, mine, :] = (mid[j, mine, :].astype(f32) + far[j, g * q:(g + 1) * q, :].astype(f32)).astype(bf)
        store = pltpu.make_async_copy(pair(mid.at[j]).at[:, low(q, x)], span, gsem.at[stage.shape[0] + j])
        store.start()
        return store

    def put(value_rows, groups, span):
        k = len(swaps)
        slot = k % stage.shape[0]
        if k >= stage.shape[0]:
            wire.sent(swaps[k - stage.shape[0]])
            if k - stage.shape[0] in stores:
                stores.pop(k - stage.shape[0]).wait()
        def body(at):
            stage[slot, at, :] = value_rows(at).astype(bf)
        chunks(model, step, body)
        size = model // groups // 2
        way = wire.slot()
        whole = stage.at[slot].reshape((groups, 2 * size, model))
        swaps.append(wire.start(way, whole.at[:, low(size, 1 - c)], got.at[k].reshape((groups, size, model)), cpeer))
        if pending:
            finish()
        pending.append((k, slot, groups, size, span, way))

    flat = lambda ref: ref.reshape(model, model)
    row = lambda i: vec[i:i + 1, :]
    b_output, b_outer, g1, s1, g2, s2 = [row(i) for i in (2, 3, 4, 5, 6, 7)]
    small[...] = jnp.zeros_like(small)
    ready(0)
    wo = flat(w_out)

    def first(at):
        attn = mm(mixed[:, at], wo[...], 0, 0)
        z = tokens[at, :].astype(f32) + (attn + b_output)
        cen = z - jnp.mean(z, axis=-1, keepdims=True)
        inv = lax.rsqrt(jnp.mean(cen * cen, axis=-1, keepdims=True) + NORM_EPS)
        xh = cen * inv
        norm = xh * g1 + s1
        xh1[at, :] = xh
        n1b[at, :] = norm.astype(bf)
        r1[at, :] = jnp.broadcast_to(inv, (inv.shape[0], 128))
        acc[at, :] = norm + b_outer
    chunks(toks, step, first)
    for j in range(wide):
        ready(1 + j)
        wi = flat(w_in.at[j])
        bias = row(8 + j)
        def inner(at, j=j, wi=wi, bias=bias):
            u = mm(n1b[at, :], wi[...], 1, 0) + bias
            cdf = 0.5 * (1.0 + lax.erf(u * (0.5 ** 0.5)))
            pdf = jnp.exp(-0.5 * u * u) * 0.3989422804014327
            fb[j, at, :] = (u * cdf).astype(bf)
            gp[j, at, :] = cdf + u * pdf
        chunks(toks, step, inner)
    ready(1 + wide)
    for j in range(wide):
        wout = flat(w_outer.at[j])
        def outer(at, j=j, wout=wout):
            acc[at, :] += mm(fb[j, at, :], wout[...], 1, 0)
        chunks(toks, step, outer)

    def second(at):
        z = acc[at, :]
        cen = z - jnp.mean(z, axis=-1, keepdims=True)
        inv = lax.rsqrt(jnp.mean(cen * cen, axis=-1, keepdims=True) + NORM_EPS)
        xh = cen * inv
        out[at, :] = (xh * g2 + s2).astype(bf)
        g = cot[at, :].astype(f32)
        gx = g * xh
        gh = g * g2
        d = inv * (gh - jnp.mean(gh, axis=-1, keepdims=True) - xh * jnp.mean(gh * xh, axis=-1, keepdims=True))
        dh2[at, :] = d
        low = d.astype(bf)
        dm[at, :] = low
        small[6:7, :] += jnp.sum(gx, axis=0, keepdims=True)
        small[7:8, :] += jnp.sum(g, axis=0, keepdims=True)
        small[3:4, :] += jnp.sum(low.astype(f32), axis=0, keepdims=True)
    chunks(toks, step, second)
    for j in range(wide):
        wout = flat(w_outer.at[j])
        put(lambda at, j=j: mm(fb[j, :, at], dm[...], 0, 0), per, ga.at[pl.ds(j * per, per), pl.ds((1 + wide) * h, q)])
        def dinner(at, j=j, wout=wout):
            low = (gp[j, at, :] * mm(dm[at, :], wout[...], 1, 1)).astype(bf)
            du[at, :] = low
            small[8 + j:9 + j, :] += jnp.sum(low.astype(f32), axis=0, keepdims=True)
        chunks(toks, step, dinner)
        wi = flat(w_in.at[j])
        def dfirst(at, wi=wi):
            dh2[at, :] += mm(du[at, :], wi[...], 1, 1)
        chunks(toks, step, dfirst)
        put(lambda at: mm(n1b[:, at], du[...], 0, 0), n, ga.at[:, pl.ds((1 + j) * h, h)])

    def last(at):
        d = dh2[at, :]
        xh = xh1[at, :]
        gh = d * g1
        inv = r1[at, 0:1]
        z = inv * (gh - jnp.mean(gh, axis=-1, keepdims=True) - xh * jnp.mean(gh * xh, axis=-1, keepdims=True))
        dres[at, :] = z
        low = z.astype(bf)
        dm[at, :] = low
        small[4:5, :] += jnp.sum(d * xh, axis=0, keepdims=True)
        small[5:6, :] += jnp.sum(d, axis=0, keepdims=True)
        small[2:3, :] += jnp.sum(low.astype(f32), axis=0, keepdims=True)
    chunks(toks, step, last)

    def back(at):
        dO[at, :] = mm(wo[at, :], dm[...], 1, 1).astype(bf)
    chunks(model, step, back)
    put(lambda at: mm(mixed[at, :], dm[...], 1, 0), n, ga.at[:, pl.ds(0, h)])
    finish()
    joined = [join(j) for j in range(wide)]
    for store in [*stores.values(), *joined]:
        store.wait()
    wire.drain()


def ffn_block(mixed, tokens, cot, vec, big, step=384):
    n, half, model = big.shape
    r = model // n
    wide = (2 * half // r - 1) // 2
    toks = tokens.shape[0]
    vmem = pl.BlockSpec(memory_space=pltpu.VMEM)
    hbm = pl.BlockSpec(memory_space=pl.ANY)
    per = n // wide
    ohold = (per, wide * r, model) if per else (n, r, model)
    V = pltpu.VMEM
    sq = lambda dt, *lead: V(lead + (toks, model), dt)
    return pl.pallas_call(
        functools.partial(ffn_kernel, n, r, step),
        in_specs=[vmem] * 4 + [hbm],
        out_specs=[vmem, vmem, hbm, vmem, vmem],
        out_shape=[jax.ShapeDtypeStruct((toks, model), bf), jax.ShapeDtypeStruct((toks, model), f32),
                   jax.ShapeDtypeStruct((n, half - wide * r // 4, model), bf), jax.ShapeDtypeStruct((model, toks), bf),
                   jax.ShapeDtypeStruct((16, model), f32)],
        scratch_shapes=[V((n, r, model), bf), V((wide, n, r, model), bf), V((wide,) + ohold, bf), V((4, model, model), bf),
                        sq(bf, wide), sq(f32, wide), sq(f32), sq(bf), sq(f32), sq(bf), sq(bf), sq(f32),
                        V((toks, 128), f32), V((1 + 2 * wide, model // 2, model), bf),
                        V((wide, model // 2, model), bf), V((wide, model // 4, model), bf), pltpu.SemaphoreType.DMA(((2 + wide) * n,)), pltpu.SemaphoreType.DMA((4 + wide,)),
                        pltpu.SemaphoreType.DMA(((2 + wide) * n + 1 + 3 * wide,)), pltpu.SemaphoreType.DMA(((2 + wide) * n + 1 + 3 * wide,))],
        compiler_params=pltpu.CompilerParams(collective_id=3, has_side_effects=True, vmem_limit_bytes=67043328),
        cost_estimate=pl.CostEstimate(flops=2 * toks * model * model * (3 + 6 * wide), bytes_accessed=8 * n * half * model, transcendentals=2 * toks * model * wide),
        name="ffn_block",
    )(mixed, tokens, cot, vec, big)


def layer_norm(inputs, norm_gain, norm_bias):
    row_mean = jnp.mean(inputs, axis=-1, keepdims=True)
    centred = inputs - row_mean
    row_var = jnp.mean(centred * centred, axis=-1, keepdims=True)
    return centred * lax.rsqrt(row_var + NORM_EPS) * norm_gain + norm_bias


def gelu_exact(inputs):
    return jax.nn.gelu(inputs, approximate=False)


def contract(left_in, right_in, left_dim, right_dim):
    return lax.dot_general(
        left_in,
        right_in,
        (((left_dim,), (right_dim,)), ((), ())),
        preferred_element_type=jnp.float32,
    )


def chips_of_two_by_four():
    return lax.axis_size("wshard") == 8 and lax.axis_size("seq") == 4


def reduce_parts(ga, gb, dx, sm, quarter):
    def scatter(part):
        return lax.psum_scatter(part, "wshard", scatter_dimension=0, tiled=False)

    if chips_of_two_by_four():
        return reduce_grads(scatter(ga), gb, dx, sm, quarter)

    fx = lax.psum_scatter(dx, "seq", scatter_dimension=0, tiled=False)
    return (
        lax.psum(scatter(ga), "seq")[None], lax.all_gather(scatter(gb), "seq"), fx, jnp.zeros_like(fx),
        lax.psum(scatter(sm), "seq"),
    )


def ffn_plain(mixed, tokens, cotangent, vec, big):
    shards_n, rows9, model = big.shape
    rows = model // shards_n
    wide = (rows9 // rows - 1) // 2
    bias_output, bias_outer, gain_one, shift_one, gain_two, shift_two = vec[2:8]
    bias_inner = vec[8:8 + wide].reshape(-1)
    output_full = big[:, :rows].reshape(model, model)
    inner_full = jnp.concatenate(
        [big[:, (1 + j) * rows:(2 + j) * rows].reshape(model, model) for j in range(wide)], axis=1
    )
    outer_full = big[:, (1 + wide) * rows:].reshape(-1, model)

    residual_in = tokens.astype(f32) + contract(mixed, output_full, 0, 0) + bias_output
    first_norm, first_back = jax.vjp(layer_norm, residual_in, gain_one, shift_one)
    first_low = first_norm.astype(bf)
    inner_act = jnp.dot(first_low, inner_full, preferred_element_type=f32) + bias_inner
    gelu_out, gelu_back = jax.vjp(gelu_exact, inner_act)
    gelu_low = gelu_out.astype(bf)
    second_in = first_norm + jnp.dot(gelu_low, outer_full, preferred_element_type=f32) + bias_outer
    layer_result, second_back = jax.vjp(layer_norm, second_in, gain_two, shift_two)
    d_second, grad_gain_two, grad_bias_two = second_back(cotangent.astype(f32))
    d_outer = d_second.astype(bf)
    grad_bias_outer = jnp.sum(d_outer.astype(f32), axis=0)
    grad_outer = contract(gelu_low, d_outer, 0, 0)
    (d_inner,) = gelu_back(contract(d_outer, outer_full, 1, 1))
    d_inner_low = d_inner.astype(bf)
    grad_bias_inner = jnp.sum(d_inner_low.astype(f32), axis=0)
    grad_inner = contract(first_low, d_inner_low, 0, 0)
    d_first = contract(d_inner_low, inner_full, 1, 1) + d_second
    d_resid, grad_gain_one, grad_bias_one = first_back(d_first)
    d_attn = d_resid.astype(bf)
    grad_bias_output = jnp.sum(d_attn.astype(f32), axis=0)
    grad_output = contract(mixed, d_attn, 1, 0)
    d_mixed = contract(output_full, d_attn, 1, 1).astype(bf)
    by_rows = lambda grad: grad.astype(bf).reshape(shards_n, -1, model)
    ga = jnp.concatenate(
        [by_rows(grad_output)] + [by_rows(grad_inner[:, j * model:(j + 1) * model]) for j in range(wide)]
        + [by_rows(grad_outer)], axis=1,
    )
    none = jnp.zeros((model,), f32)
    sums = jnp.concatenate([
        jnp.stack([none, none, grad_bias_output, grad_bias_outer, grad_gain_one, grad_bias_one, grad_gain_two, grad_bias_two]),
        grad_bias_inner.reshape(wide, model), jnp.zeros((4, model), f32)], axis=0)
    return layer_result.astype(bf), d_resid, ga, d_mixed, sums


def shards(
    tokens, cotangent, starts,
    w_query, w_key, w_value, w_output, w_inner, w_outer,
    b_query, b_value, b_output, b_inner, b_outer,
    gain_first, bias_first, gain_second, bias_second,
):
    model = tokens.shape[1]
    rows = w_query.shape[0]
    shards_n = lax.axis_size("wshard")
    seq_n = lax.axis_size("seq")
    seq_i = lax.axis_index("seq")
    width = model // seq_n
    heads = width // HD
    wide = w_inner.shape[1] // model

    def own(columns):
        return lax.select_n(seq_i, *jnp.split(columns, seq_n, axis=columns.ndim - 1))

    smalls = (b_query, b_value, b_output, b_outer, gain_first, bias_first, gain_second, bias_second)
    small_cols = jnp.stack(smalls + tuple(b_inner.reshape(wide, rows)), axis=1)
    cols_n = small_cols.shape[1]
    b = jnp.concatenate([own(w_query), own(w_key), own(w_value), jnp.pad(small_cols, ((0, 0), (0, HD - cols_n)))], axis=1)
    fast = chips_of_two_by_four()

    def packed(share, part):
        cut = lambda w: lax.select_n(part == 1, *jnp.split(w, 2)) if share == 2 else w
        inner = cut(w_inner).reshape(rows // share, wide, model).transpose(1, 0, 2).reshape(-1, model)
        return jnp.concatenate([cut(w_output), inner, cut(w_outer)], axis=0)

    if fast:
        big = lax.all_gather(packed(2, seq_i % 2), "wshard")
        side, stream = gather_inputs(b, tokens)
    else:
        big = lax.all_gather(packed(1, 0), "wshard")
        side, stream = lax.all_gather(b, "wshard"), lax.all_gather(tokens, "seq")
    stream = stream.reshape(-1, model)
    side = side.reshape(model, -1)
    w_own = side[:, :3 * width]
    vectors = side[:, 3 * width:3 * width + cols_n].astype(f32).T
    bias_query, bias_value = vectors[:2]
    bias_inner = vectors[8:].reshape(wide, shards_n, rows).transpose(1, 0, 2).reshape(-1)
    scale = HD ** -0.5
    none = jnp.zeros((width,), f32)
    bias = jnp.concatenate([own(bias_query), none, own(bias_value)])
    factor = jnp.where(jnp.arange(3 * width) < width, scale, 1.0)
    qkv = ((contract(w_own, stream, 0, 1) + bias[:, None]) * factor[:, None]).astype(bf)
    oT, mix, lse = attn_fwd(starts, qkv, tokens.shape[0], 512, 512)
    mixed = lax.all_to_all(mix, "seq", split_axis=0, concat_axis=0).reshape(model, -1)

    vec = jnp.concatenate([vectors[:8], bias_inner.reshape(wide, model), jnp.zeros((4, model), f32)], axis=0)
    if fast:
        layer_result, d_resid, ga, d_mixed, sums = ffn_block(mixed, tokens, cotangent, vec, big)
    else:
        layer_result, d_resid, ga, d_mixed, sums = ffn_plain(mixed, tokens, cotangent, vec, big)
    doT = lax.all_to_all(d_mixed.reshape(seq_n, width, -1), "seq", split_axis=0, concat_axis=0)

    dT = attn_bwd(starts, qkv, doT, oT, lse, 256, 512)
    gb = contract(stream, dT, 0, 1).astype(bf).reshape(shards_n, rows, -1)
    dx = contract(dT, w_own, 0, 1).astype(bf).reshape(seq_n, -1, model)
    d_bias = contract(jnp.ones((8, dT.shape[1]), bf), dT, 1, 1)[:1]
    sm = jnp.concatenate(
        [sums[:8].reshape(8, shards_n, rows).transpose(1, 0, 2), sums[8:8 + wide].reshape(shards_n, wide, rows)], axis=1,
    )
    lanes = -rows % 128
    sm = jnp.pad(sm, ((0, 0), (0, -cols_n % 8), (0, lanes)))
    shard, row = (lax.broadcasted_iota(jnp.int32, sm.shape, axis) for axis in (0, 1))
    per = width // rows
    for r, first in ((0, 0), (1, 2 * width)):
        for t in range(per):
            at = first + t * rows
            own_sum = jnp.pad(d_bias[:, at:at + rows], ((0, 0), (0, lanes)))
            sm = jnp.where((row == r) & (shard == seq_i * per + t), own_sum[None], sm)
    fa, fb, fx, fr, fs = reduce_parts(ga, gb, dx, sm, wide * rows // 4)
    d_tokens = fx.astype(f32) + fr.astype(f32) + d_resid
    fb = fb.astype(f32)
    grads = [
        jnp.concatenate([fb[s, :, i * width:(i + 1) * width] for s in range(seq_n)], axis=1) for i in range(3)
    ]
    fa = fa.astype(f32)
    part = rows // fa.shape[0]
    span = lambda first, count: fa[:, first * part:(first + count) * part].reshape(-1, model)
    g_inner = jnp.concatenate([span(1 + j, 1) for j in range(wide)], axis=1)
    tail = [fs[i, :rows] for i in range(8)]
    g_b_inner = fs[8:8 + wide, :rows].reshape(-1)
    return (
        layer_result, d_tokens, *grads,
        span(0, 1), g_inner, span(1 + wide, wide),
        tail[0], tail[1], tail[2], g_b_inner, *tail[3:],
    )


def solution(mesh):
    placed = (
        P(("wshard", "seq"), None),
        P(("wshard", "seq"), None),
        P("wshard", None),
        P("wshard", None),
        P("wshard", None),
        P("wshard", None),
        P("wshard", None),
        P("wshard", None),
        P("wshard", None),
        P("wshard"),
        P("wshard"),
        P("wshard"),
        P("wshard"),
        P("wshard"),
        P("wshard"),
        P("wshard"),
        P("wshard"),
        P("wshard"),
    )
    return jax.shard_map(
        shards,
        mesh=mesh,
        in_specs=placed,
        out_specs=(
            P(("wshard", "seq"), None),
            P(("wshard", "seq"), None),
            P("wshard", None),
            P("wshard", None),
            P("wshard", None),
            P("wshard", None),
            P("wshard", None),
            P("wshard", None),
            P("wshard"),
            P("wshard"),
            P("wshard"),
            P("wshard"),
            P("wshard"),
            P("wshard"),
            P("wshard"),
            P("wshard"),
            P("wshard"),
        ),
        check_vma=False,
    )
```
